256 devices in a mesh: gx: 16 (over x, z_hi, core), gy: 16 (over y, z_lo).
Axes of the slice: x: 4, y: 4, z: 8 (z_hi: 2, z_lo: 4; z = z_hi * 4 + z_lo), core: 2. Of those that a mesh axis runs over, the one named last changes fastest.
Arguments:
- east_velocity: float32 [48, 128, 4096], P(None, 'gx', 'gy'), may hold values from -3 to 3
- north_velocity: float32 [48, 128, 4096], P(None, 'gx', 'gy'), may hold values from -3 to 3
- salinity: float32 [48, 128, 4096], P(None, 'gx', 'gy'), may hold values from -6 to 6
- surface: float32 [128, 4096], P('gx', 'gy'), may hold values from -6 to 6
- column_depth: float32 [128, 4096], P('gx', 'gy'), may hold values from 0.5 to 4
- wet_column: int32 [128, 4096], P('gx', 'gy'), may hold values 0 or 1
- active_levels: int32 [128, 4096], P('gx', 'gy'), may hold values from 1 to 48
Outputs:
- east_flow: float32 [48, 128, 4096], P(None, 'gx', 'gy')
- north_flow: float32 [48, 128, 4096], P(None, 'gx', 'gy')
- salt_next: float32 [48, 128, 4096], P(None, 'gx', 'gy')
- surface_next: float32 [128, 4096], P('gx', 'gy')
The draws below stay inside these ranges and needn't reach their ends.
All inputs are finite; a program needn't handle non-finite values. No bound on the sum of `wet_column` on one device may be relied on, other than what follows from the above.
Results may differ from the reference program's by a relative error of at most 0.000024.
Values sent between devices are 32-bit elements; how exact they have to be, the bound alone decides.
No kernel may reach another device: no remote copies, remote signals or barrier semaphores. Data moves between devices by JAX's collectives and lax.ppermute only.
A program may use at most 64 MiB of HBM per device.

```python
import math
import jax
import jax.numpy as jnp

LEV = 48
ITERS = 16
NX = 128
NY = 4096


def touch_ends(values, key, least, largest):
    spot = [jax.random.randint(jax.random.fold_in(key, axis), (), 0, length) for axis, length in enumerate(values.shape)]
    main_axis = values.shape.index(max(values.shape))
    neighbour = spot[:main_axis] + [(spot[main_axis] + 1) % values.shape[main_axis]] + spot[main_axis + 1:]
    return values.at[tuple(spot)].set(least).at[tuple(neighbour)].set(largest)


def level_of(own_key, shape, shards, low, high):
    gain = 1.0
    for position, blocks in shards:
        steps = jax.random.uniform(jax.random.fold_in(jax.random.fold_in(own_key, 6), position), (blocks,), jnp.float32, low / len(shards), high / len(shards))
        gain = gain * jnp.repeat(jnp.exp(steps), shape[position] // blocks).reshape((-1,) + (1,) * (len(shape) - 1 - position))
    return gain


def normal_values(own_key, shape, scale, reach, pieces=(), held_as=jnp.bfloat16):
    entries = jax.random.normal(own_key, shape, jnp.float32) * scale
    if len(pieces) > 0:
        entries = level_of(own_key, shape, pieces, -0.22, 0.18) * entries
    return jnp.clip(entries, min=-reach, max=reach).astype(held_as)


def setup_inputs(seed: int = 0) -> dict:
    arg_keys = jax.random.split(jax.random.key(seed), 8)
    east_velocity = normal_values(arg_keys[0], (LEV, NX, NY), 0.5, 3.0, ((1, 16), (2, 16)), jnp.float32)
    north_velocity = normal_values(arg_keys[1], (LEV, NX, NY), 0.5, 3.0, ((1, 16), (2, 16)), jnp.float32)
    salinity = normal_values(arg_keys[2], (LEV, NX, NY), 1.0, 6.0, ((1, 16), (2, 16)), jnp.float32)
    surface = normal_values(arg_keys[3], (NX, NY), 1.0, 6.0, ((0, 16), (1, 16)), jnp.float32)
    column_depth = jnp.clip(jnp.exp(math.log(4.0) - 2.0794415 * jax.random.uniform(arg_keys[4], (NX, NY), jnp.float32) ** level_of(arg_keys[4], (NX, NY), ((0, 16), (1, 16)), -0.2, 0.2)), 0.5, 4.0)
    wet_column = touch_ends((jax.random.randint(arg_keys[5], (NX, NY), 0, 8) < 7).astype(jnp.int32), jax.random.fold_in(arg_keys[5], 1), 0, 1)
    active_levels = touch_ends(jax.random.randint(arg_keys[6], (NX, NY), 1, LEV + 1), jax.random.fold_in(arg_keys[6], 1), 1, LEV).astype(jnp.int32)
    return {"east_velocity": east_velocity, "north_velocity": north_velocity, "salinity": salinity, "surface": surface, "column_depth": column_depth, "wet_column": wet_column, "active_levels": active_levels}


TIME_STEP = 0.2
CORIOLIS = 0.3
PRESS_COEF = 0.05
VISCOSITY = 0.1
DIFFUSIVITY = 0.1
SIGMA_SHIFT = 0.25
CHEB_CENTER = 3.625
CHEB_HALF = 3.375
DIVERGENCE_COEF = 8.0


def cheb_table(count):
    first = CHEB_CENTER / CHEB_HALF
    ratio = 1.0 / first
    keeps = []
    gains = []
    for index in range(count):
        ratio_next = 1.0 / (2.0 * first - ratio)
        keeps.append(ratio_next * ratio)
        gains.append(2.0 * ratio_next / CHEB_HALF)
        ratio = ratio_next
    return keeps, gains


def centre(field):
    return field[:, 2:-2, 2:-2]


def along_east(field):
    return (8.0 * (field[:, 3:-1, 2:-2] - field[:, 1:-3, 2:-2]) - (field[:, 4:, 2:-2] - field[:, :-4, 2:-2])) / 12.0


def along_north(field):
    return (8.0 * (field[:, 2:-2, 3:-1] - field[:, 2:-2, 1:-3]) - (field[:, 2:-2, 4:] - field[:, 2:-2, :-4])) / 12.0


def laplace(field):
    return field[:, 3:-1, 2:-2] + field[:, 1:-3, 2:-2] + field[:, 2:-2, 3:-1] + field[:, 2:-2, 1:-3] - 4.0 * centre(field)


def tendency(padded):
    east, north, tracer = padded[0], padded[1], padded[2]
    pressure = PRESS_COEF * jnp.cumsum(tracer, axis=0)
    east_mid = centre(east)
    north_mid = centre(north)

    def advect(field):
        return -(east_mid * along_east(field) + north_mid * along_north(field))

    east_rate = advect(east) + CORIOLIS * north_mid - along_east(pressure) + VISCOSITY * laplace(east)
    north_rate = advect(north) - CORIOLIS * east_mid - along_north(pressure) + VISCOSITY * laplace(north)
    salt_rate = advect(tracer) + DIFFUSIVITY * laplace(tracer)
    return jnp.stack([east_rate, north_rate, salt_rate])


def nine_point(field, wet):
    weighted = wet * field
    edges = weighted[2:, 1:-1] + weighted[:-2, 1:-1] + weighted[1:-1, 2:] + weighted[1:-1, :-2]
    corners = weighted[2:, 2:] + weighted[2:, :-2] + weighted[:-2, 2:] + weighted[:-2, :-2]
    stencil = (20.0 * weighted[1:-1, 1:-1] - 4.0 * edges - corners) / 6.0
    wet_mid = wet[1:-1, 1:-1]
    field_mid = field[1:-1, 1:-1]
    return wet_mid * (SIGMA_SHIFT * field_mid + stencil) + (1.0 - wet_mid) * field_mid


def reference(east_velocity, north_velocity, salinity, surface, column_depth, wet_column, active_levels):
    wet = wet_column.astype(jnp.float32)
    levels = jnp.arange(LEV, dtype=jnp.int32)
    mask3 = (levels[:, None, None] < active_levels[None]).astype(jnp.float32) * wet[None]
    state0 = jnp.stack([east_velocity, north_velocity, salinity]) * mask3

    def rate(state):
        padded = jnp.pad(state, ((0, 0), (0, 0), (2, 2), (2, 2)))
        return tendency(padded) * mask3

    state1 = state0 + TIME_STEP * rate(state0)
    state2 = 0.75 * state0 + 0.25 * (state1 + TIME_STEP * rate(state1))
    state3 = state0 / 3.0 + (2.0 / 3.0) * (state2 + TIME_STEP * rate(state2))
    flow_east = column_depth * (jnp.sum(state3[0], axis=0) / LEV)
    flow_north = column_depth * (jnp.sum(state3[1], axis=0) / LEV)
    east_pad = jnp.pad(flow_east, 1)
    north_pad = jnp.pad(flow_north, 1)
    divergence = (east_pad[2:, 1:-1] - east_pad[:-2, 1:-1]) * 0.5 + (north_pad[1:-1, 2:] - north_pad[1:-1, :-2]) * 0.5
    right_side = wet * (SIGMA_SHIFT * surface - DIVERGENCE_COEF * divergence)
    wet_pad = jnp.pad(wet, 1)

    def apply(field):
        return nine_point(jnp.pad(field, 1), wet_pad)

    solution = surface
    residual = right_side - apply(solution)
    direction = residual / CHEB_CENTER
    keeps, gains = cheb_table(ITERS)
    for index in range(ITERS):
        solution = solution + direction
        residual = residual - apply(direction)
        direction = keeps[index] * direction + gains[index] * residual
    surface_pad = jnp.pad(solution, 1)
    slope_east = (surface_pad[2:, 1:-1] - surface_pad[:-2, 1:-1]) * 0.5
    slope_north = (surface_pad[1:-1, 2:] - surface_pad[1:-1, :-2]) * 0.5
    east_flow = mask3 * (state3[0] - slope_east[None])
    north_flow = mask3 * (state3[1] - slope_north[None])
    return east_flow, north_flow, state3[2], solution
```

```python
import functools

import jax
import jax.numpy as jnp
from jax import lax
from jax.experimental import pallas as pl
from jax.experimental.pallas import tpu as pltpu
from jax.sharding import PartitionSpec as P

ITERS = 16
TIME_STEP = 0.2
CORIOLIS = 0.3
PRESS_COEF = 0.05
VISCOSITY = 0.1
DIFFUSIVITY = 0.1
SIGMA_SHIFT = 0.25
CHEB_CENTER = 3.625
CHEB_HALF = 3.375
DIVERGENCE_COEF = 8.0

LEV = 48
ROWS = 8
COLS = 256
EXT = 128
WIDE = COLS + EXT
HALO = 6
CHUNKS = 1
F32 = jnp.float32


def cheb_table(count):
    first = CHEB_CENTER / CHEB_HALF
    ratio = 1.0 / first
    keeps = []
    gains = []
    for index in range(count):
        ratio_next = 1.0 / (2.0 * first - ratio)
        keeps.append(ratio_next * ratio)
        gains.append(2.0 * ratio_next / CHEB_HALF)
        ratio = ratio_next
    return (keeps, gains)


def lanes(shape):
    return lax.broadcasted_iota(jnp.int32, shape, len(shape) - 1)


def pack_kernel(sc, u, v, s, wet, act, surf, depth, st, *outs):
    core = sc[1]
    north_odd = sc[2]
    mains = outs[:CHUNKS]
    edge_a, edge_b = outs[CHUNKS:]
    levels = LEV // CHUNKS
    count = (act[...] * wet[...]).astype(F32)
    for f, ref in enumerate((u, v, s)):
        for lev in range(LEV):
            tile = jnp.where(count > lev, ref[lev], 0.0)
            for h in range(2):
                st[f, h, pl.ds(lev, ROWS, stride=LEV), :] = tile[:, h * 128 : (h + 1) * 128]
    base = 2 * core
    for f in range(3):
        for j in range(HALO):
            for c in range(CHUNKS):
                for h in range(2):
                    start = pl.multiple_of((base + j) * LEV + c * levels, 8)
                    mains[c][f, h, j * levels : (j + 1) * levels, :] = st[f, h, pl.ds(start, levels), :]
    lane = lanes((LEV, 128)) // 32
    odd = jnp.full((LEV, 128), north_odd, jnp.int32) == 1
    for f in range(3):
        for g in range(2):
            left = jnp.zeros((LEV, 128), F32)
            right = jnp.zeros((LEV, 128), F32)
            for q in range(4):
                at = (4 * g + q) * LEV
                low = st[f, 0, at : at + LEV, :]
                high = st[f, 1, at : at + LEV, :]
                low = low if q == 0 else pltpu.roll(low, 32 * q, 1)
                high = high if q == 3 else pltpu.roll(high, 32 * q + 32, 1)
                left = jnp.where(lane == q, low, left)
                right = jnp.where(lane == q, high, right)
            at = (2 * f + g) * LEV
            edge_a[at : at + LEV, :] = jnp.where(odd, left, right)
            edge_b[at : at + LEV, :] = jnp.where(odd, right, left)
    flat = (surf[...], count, depth[...])
    lane = lanes((ROWS, 128)) // 32
    left = jnp.zeros((ROWS, 128), F32)
    right = jnp.zeros((ROWS, 128), F32)
    for q, field in enumerate(flat):
        low = field[:, :128]
        high = field[:, 128:]
        low = low if q == 0 else pltpu.roll(low, 32 * q, 1)
        high = high if q == 3 else pltpu.roll(high, 32 * q + 32, 1)
        left = jnp.where(lane == q, low, left)
        right = jnp.where(lane == q, high, right)
    odd = jnp.full((ROWS, 128), north_odd, jnp.int32) == 1
    edge_a[6 * LEV :, :] = jnp.where(odd, left, right)
    edge_b[6 * LEV :, :] = jnp.where(odd, right, left)


def ext_kernel(sc, edge_a, edge_b, wet, act, surf, depth, own, corner, flat):
    core = sc[1]
    north_odd = sc[2]

    def halves(at, size):
        a = edge_a[at : at + size, :]
        b = edge_b[at : at + size, :]
        odd = jnp.full((size, 128), north_odd, jnp.int32) == 1
        return jnp.where(odd, b, a), jnp.where(odd, a, b)

    def unpack(high, low, q):
        lane = lanes(high.shape)
        high = high if q == 0 else pltpu.roll(high, 128 - 32 * q, 1)
        low = low if q == 3 else pltpu.roll(low, 96 - 32 * q, 1)
        return jnp.where(lane < 32, high, jnp.where(lane >= 96, low, 0.0))

    for f in range(3):
        for g in range(2):
            high, low = halves((2 * f + g) * LEV, LEV)
            for q in range(4):
                at = (8 * f + 4 * g + q) * LEV
                own[at : at + LEV, :] = unpack(high, low, q)
    high, low = halves(6 * LEV, ROWS)
    count = (act[...] * wet[...]).astype(F32)
    counts = (count[:, :128], count[:, 128:], unpack(high, low, 1))
    for h in range(3):
        own[24 * LEV + 8 * h : 24 * LEV + 8 * h + 8, :] = counts[h]
        corner[9 * LEV + 8 * h : 9 * LEV + 8 * h + 8, :] = counts[h]
    flat[0, :, :COLS] = surf[...]
    flat[0, :, COLS:] = unpack(high, low, 0)
    flat[1, :, :COLS] = count
    flat[1, :, COLS:] = counts[2]
    flat[2, :, :COLS] = depth[...]
    flat[2, :, COLS:] = unpack(high, low, 2)
    lane = lanes((LEV, 128))
    inner = (lane >= 32) & (lane < 96)
    for f in range(3):
        for j in range(3):
            start = pl.multiple_of((8 * f + 2 * core + 2 * j) * LEV, 8)
            first = own[pl.ds(start, LEV), :]
            second = own[pl.ds(start + LEV, LEV), :]
            at = (3 * f + j) * LEV
            corner[at : at + LEV, :] = jnp.where(inner, pltpu.roll(second, 64, 1), first)


def shifts(q):
    return (
        pltpu.roll(q, WIDE - 1, 1),
        pltpu.roll(q, 1, 1),
        pltpu.roll(q, WIDE - 2, 1),
        pltpu.roll(q, 2, 1),
    )


def slope(ahead, behind, ahead2, behind2):
    return (8.0 / 12.0) * (ahead - behind) - (1.0 / 12.0) * (ahead2 - behind2)


def running(x, sub):
    for step in (1, 2, 4):
        x = x + jnp.where(sub >= step, pltpu.roll(x, step, 0), 0.0)
    return x


def rk_kernel(chunk, sc, st, stp, own, ownp, main, corner, flat, *rest):
    levels = LEV // CHUNKS
    if chunk:
        carry_in, sums_in = rest[:2]
        rest = rest[2:]
    out, carry, sums, flows, ext, one, two, counts = rest
    core = sc[1]
    lev0 = chunk * levels
    for f in range(3):
        for r in range(ROWS):
            for h in range(2):
                ext[f, HALO + r, :, h * 128 : (h + 1) * 128] = st[f, h, r * LEV + lev0 : r * LEV + lev0 + levels, :]
            at = (8 * f + r) * LEV + lev0
            ext[f, HALO + r, :, COLS:] = own[at : at + levels, :]
        for j in range(HALO):
            row = 14 * (1 - core) + j
            start = pl.multiple_of((2 * core + j) * LEV + lev0, 8)
            for h in range(2):
                ext[f, row, :, h * 128 : (h + 1) * 128] = stp[f, h, pl.ds(start, levels), :]
            ext[f, row, :, COLS:] = ownp[pl.ds(pl.multiple_of(start + 8 * f * LEV, 8), levels), :]
            row = 14 * core + j
            for h in range(2):
                ext[f, row, :, h * 128 : (h + 1) * 128] = main[f, h, j * levels : (j + 1) * levels, :]
        lane = lanes((levels, 128))
        outer = (lane < 32) | (lane >= 96)
        for j in range(3):
            at = (3 * f + j) * LEV + lev0
            pair = corner[at : at + levels, :]
            row = 14 * core + 2 * j
            ext[f, row, :, COLS:] = jnp.where(outer, pair, 0.0)
            ext[f, row + 1, :, COLS:] = jnp.where(outer, pltpu.roll(pair, 64, 1), 0.0)
    for h in range(3):
        tile = own[24 * LEV + 8 * h : 24 * LEV + 8 * h + 8, :]
        for r in range(ROWS):
            counts[HALO + r, :, h * 128 : (h + 1) * 128] = jnp.broadcast_to(tile[r : r + 1, :], (8, 128))
        for j in range(HALO):
            line = ownp[pl.ds(24 * LEV + 8 * h + 2 * core + j, 1), :]
            counts[14 * (1 - core) + j, :, h * 128 : (h + 1) * 128] = jnp.broadcast_to(line, (8, 128))
            line = corner[pl.ds(9 * LEV + 8 * h + 2 * (1 - core) + j, 1), :]
            counts[14 * core + j, :, h * 128 : (h + 1) * 128] = jnp.broadcast_to(line, (8, 128))

    sub = lax.broadcasted_iota(jnp.int32, (8, WIDE), 0)

    def stage(source, rows, inset, write, slot):
        def row(o, _):
            count = counts[o + inset]
            if chunk:
                sum_x = carry_in[slot + 2 * o]
                sum_y = carry_in[slot + 2 * o + 1]
            else:
                sum_x = jnp.zeros((8, WIDE), F32)
                sum_y = jnp.zeros((8, WIDE), F32)
            for t in range(levels // 8):
                here = slice(8 * t, 8 * t + 8)
                mid = []
                dxs = []
                dys = []
                laps = []
                for f in range(3):
                    q = source[f, o + 2, here, :]
                    back2, back = source[f, o, here, :], source[f, o + 1, here, :]
                    fore, fore2 = source[f, o + 3, here, :], source[f, o + 4, here, :]
                    right, left, right2, left2 = shifts(q)
                    mid.append(q)
                    dxs.append(slope(fore, back, fore2, back2))
                    dys.append(slope(right, left, right2, left2))
                    laps.append((fore + back) + (right + left) - 4.0 * q)
                press_x = running(dxs[2], sub) + sum_x
                press_y = running(dys[2], sub) + sum_y
                sum_x = jnp.broadcast_to(press_x[7:8, :], (8, WIDE))
                sum_y = jnp.broadcast_to(press_y[7:8, :], (8, WIDE))
                u, v, _s = mid
                rates = [VISCOSITY * laps[f] - (u * dxs[f] + v * dys[f]) for f in range(3)]
                rates[0] = rates[0] + (CORIOLIS * v - PRESS_COEF * press_x)
                rates[1] = rates[1] - (CORIOLIS * u + PRESS_COEF * press_y)
                keep = count > (sub + (lev0 + 8 * t)).astype(F32)
                write(o, here, t, mid, [jnp.where(keep, r, 0.0) for r in rates])
            carry[slot + 2 * o] = sum_x
            carry[slot + 2 * o + 1] = sum_y
            return 0

        lax.fori_loop(0, rows, row, 0)

    def write1(o, here, t, mid, rates):
        for f in range(3):
            one[f, o, here, :] = mid[f] + TIME_STEP * rates[f]

    def write2(o, here, t, mid, rates):
        for f in range(3):
            first = ext[f, o + 4, here, :]
            two[f, o, here, :] = 0.75 * first + (0.25 * mid[f] + (0.25 * TIME_STEP) * rates[f])

    def write3(o, here, t, mid, rates):
        for f in range(3):
            first = ext[f, o + 6, here, :]
            value = (1.0 / 3.0) * first + ((2.0 / 3.0) * mid[f] + (2.0 / 3.0 * TIME_STEP) * rates[f])
            at = pl.multiple_of(o * levels + 8 * t, 8)
            for h in range(2):
                out[f, h, pl.ds(at, 8), :] = value[:, h * 128 : (h + 1) * 128]
            if f < 2:
                if t == 0:
                    sums[f, o] = value + sums_in[f, o] if chunk else value
                else:
                    sums[f, o] = sums[f, o] + value

    stage(ext, 16, 2, write1, 0)
    stage(one, 12, 4, write2, 32)
    stage(two, 8, 6, write3, 56)
    for f in range(2):
        for o in range(ROWS):
            flows[f, o : o + 1, :] = jnp.sum(sums[f, o], axis=0, keepdims=True)
        flows[f] = flat[2] * (flows[f] * (1.0 / LEV))
        flows[2 + f] = flat[f]


def solve_kernel(peers, sc, table, flat, *rest):
    states = rest[:CHUNKS]
    east, north, salt, level = rest[CHUNKS : CHUNKS + 4]
    wide = rest[CHUNKS + 4]
    levels = LEV // CHUNKS
    me = sc[0]
    for k in range(-3, 4):
        peer = me + k
        inside = (peer >= 0) & (peer < peers)
        factor = jnp.where(inside, 1.0, 0.0).astype(F32)
        block = table[jnp.clip(peer, 0, peers - 1)]
        wide[:, 8 * (k + 3) : 8 * (k + 3) + 8, :] = block * factor
    high = 56

    def up(x):
        return pltpu.roll(x, high - 1, 0)

    def down(x):
        return pltpu.roll(x, 1, 0)

    def right(x):
        return pltpu.roll(x, WIDE - 1, 1)

    def left(x):
        return pltpu.roll(x, 1, 1)

    wet = jnp.where(wide[3] > 0.0, 1.0, 0.0)
    dry = 1.0 - wet

    def apply(e):
        w = wet * e
        rows = up(w) + down(w)
        mix = 4.0 * w + rows
        sides = right(mix) + left(mix)
        stencil = (20.0 / 6.0) * w - (4.0 / 6.0) * rows - (1.0 / 6.0) * sides
        return wet * (SIGMA_SHIFT * e + stencil) + dry * e

    flow_east = wide[0]
    flow_north = wide[1]
    x = wide[2]
    div = 0.5 * (up(flow_east) - down(flow_east)) + 0.5 * (right(flow_north) - left(flow_north))
    res = wet * (SIGMA_SHIFT * x - DIVERGENCE_COEF * div) - apply(x)
    step = res * (1.0 / CHEB_CENTER)
    keeps, gains = cheb_table(ITERS)
    for index in range(ITERS):
        x = x + step
        if index < ITERS - 1:
            res = res - apply(step)
            step = keeps[index] * step + gains[index] * res
    slope_east = (0.5 * (up(x) - down(x)))[24:32, :COLS]
    slope_north = (0.5 * (right(x) - left(x)))[24:32, :COLS]
    level[...] = x[24:32, :COLS]
    count = flat[1][:, :COLS]
    for lev in range(LEV):
        c, at = divmod(lev, levels)
        keep = count > lev
        for h in range(2):
            cols = slice(h * 128, (h + 1) * 128)
            parts = [states[c][f, h, pl.ds(at, ROWS, stride=levels), :] for f in range(3)]
            east[lev, :, cols] = jnp.where(keep[:, cols], parts[0] - slope_east[:, cols], 0.0)
            north[lev, :, cols] = jnp.where(keep[:, cols], parts[1] - slope_north[:, cols], 0.0)
            salt[lev, :, cols] = parts[2]


def swap(pairs):
    return [p for a, b in pairs for p in ((a, b), (b, a))]


def call(body, outs, scratch=(), ins=0):
    vmem = pl.BlockSpec(memory_space=pltpu.VMEM)
    smem = pl.BlockSpec(memory_space=pltpu.SMEM)
    return pl.pallas_call(
        body,
        out_shape=[jax.ShapeDtypeStruct(s, F32) for s in outs],
        in_specs=[smem] + [vmem] * ins,
        out_specs=[vmem] * len(outs),
        scratch_shapes=[pltpu.VMEM(s, F32) for s in scratch],
        compiler_params=pltpu.CompilerParams(vmem_limit_bytes=48 * 1024 * 1024),
    )


def local(u, v, s, surface, depth, wet, active):
    gx = lax.axis_size("gx")
    gy = lax.axis_size("gy")
    levels = LEV // CHUNKS
    me = lax.axis_index("gx")
    scalars = jnp.stack([me, me % 2, lax.axis_index("gy") % 2]).astype(jnp.int32)
    on_chip = swap([(i, i + 1) for i in range(0, gx, 2)])
    next_chip = swap([(i, i + 1) for i in range(1, gx - 1, 2)])
    even = swap([(i, i + 1) for i in range(0, gy, 2)])
    odd = swap([(i, i + 1) for i in range(1, gy - 1, 2)])

    st, *packed = call(
        pack_kernel,
        [(3, 2, ROWS * LEV, 128)]
        + [(3, 2, HALO * levels, 128)] * CHUNKS
        + [(6 * LEV + 8, 128)] * 2,
        ins=7,
    )(scalars, u, v, s, wet, active, surface, depth)
    mains = packed[:CHUNKS]
    edge_a = lax.ppermute(packed[CHUNKS], "gy", even)
    edge_b = lax.ppermute(packed[CHUNKS + 1], "gy", odd)
    mains = [lax.ppermute(m, "gx", next_chip) for m in mains]
    stp = lax.ppermute(st, "gx", on_chip)
    own, corner, flat = call(
        ext_kernel,
        [(24 * LEV + 24, 128), (9 * LEV + 24, 128), (3, ROWS, WIDE)],
        ins=6,
    )(scalars, edge_a, edge_b, wet, active, surface, depth)
    corner = lax.ppermute(corner, "gx", next_chip)
    ownp = lax.ppermute(own, "gx", on_chip)

    states = []
    tail = []
    for c in range(CHUNKS):
        out, carry, sums, flows = call(
            functools.partial(rk_kernel, c),
            [(3, 2, ROWS * levels, 128), (72, 8, WIDE), (2, ROWS, 8, WIDE), (4, ROWS, WIDE)],
            [(3, 20, levels, WIDE), (3, 16, levels, WIDE), (3, 12, levels, WIDE), (20, 8, WIDE)],
            ins=7 + len(tail),
        )(scalars, st, stp, own, ownp, mains[c], corner, flat, *tail)
        tail = [carry, sums]
        states.append(out)
    table = lax.all_to_all(jnp.broadcast_to(flows[None], (gx,) + flows.shape), "gx", 0, 0)
    east, north, salt, level = call(
        functools.partial(solve_kernel, gx),
        [(LEV, ROWS, COLS)] * 3 + [(ROWS, COLS)],
        [(4, 56, WIDE)],
        ins=2 + CHUNKS,
    )(scalars, table, flat, *states)
    return east, north, salt, level


def solution(mesh):
    cube = P(None, "gx", "gy")
    flat = P("gx", "gy")
    return jax.shard_map(
        local,
        mesh=mesh,
        in_specs=(cube, cube, cube, flat, flat, flat, flat),
        out_specs=(cube, cube, cube, flat),
        check_vma=False,
    )
```

```python
import functools

import jax
import jax.numpy as jnp
from jax import lax
from jax.experimental import pallas as pl
from jax.experimental.pallas import tpu as pltpu
from jax.sharding import PartitionSpec as P

ITERS = 16
TIME_STEP = 0.2
CORIOLIS = 0.3
PRESS_COEF = 0.05
VISCOSITY = 0.1
DIFFUSIVITY = 0.1
SIGMA_SHIFT = 0.25
CHEB_CENTER = 3.625
CHEB_HALF = 3.375
DIVERGENCE_COEF = 8.0

LEV = 48
ROWS = 8
COLS = 256
EXT = 128
WIDE = COLS + EXT
HALO = 6
SIZES = (24, 16, 8)
CHUNKS = len(SIZES)
STARTS = tuple(sum(SIZES[:c]) for c in range(CHUNKS))
F32 = jnp.float32


def cheb_table(count):
    first = CHEB_CENTER / CHEB_HALF
    ratio = 1.0 / first
    keeps = []
    gains = []
    for index in range(count):
        ratio_next = 1.0 / (2.0 * first - ratio)
        keeps.append(ratio_next * ratio)
        gains.append(2.0 * ratio_next / CHEB_HALF)
        ratio = ratio_next
    return (keeps, gains)


def lanes(shape):
    return lax.broadcasted_iota(jnp.int32, shape, len(shape) - 1)


def pack_kernel(sc, u, v, s, wet, act, surf, depth, edge_a, edge_b, *rest):
    mains = rest[:CHUNKS]
    st, plane = rest[CHUNKS : CHUNKS + 2]
    buffers = rest[CHUNKS + 2 : CHUNKS + 9]
    sems = rest[CHUNKS + 9]
    core = sc[1]
    north_odd = sc[2]
    sources = (wet, act, surf, depth, u, v, s)
    copies = [pltpu.make_async_copy(a, b, sems.at[i]) for i, (a, b) in enumerate(zip(sources, buffers))]
    for copy in copies:
        copy.start()
    for copy in copies[:4]:
        copy.wait()
    wet, act, surf, depth, *cubes = buffers
    count = (act[...] * wet[...]).astype(F32)
    plane[0] = surf[...]
    plane[1] = count
    plane[2] = depth[...]
    for f in range(3):
        copies[4 + f].wait()
        for lev in range(LEV):
            tile = jnp.where(count > lev, cubes[f][lev], 0.0)
            for h in range(2):
                st[f, h, pl.ds(lev, ROWS, stride=LEV), :] = tile[:, h * 128 : (h + 1) * 128]
    base = 2 * core
    for f in range(3):
        for j in range(HALO):
            for c in range(CHUNKS):
                levels = SIZES[c]
                for h in range(2):
                    start = pl.multiple_of((base + j) * LEV + STARTS[c], 8)
                    mains[c][f, h, j * levels : (j + 1) * levels, :] = st[f, h, pl.ds(start, levels), :]
    lane = lanes((LEV, 128)) // 32
    odd = jnp.full((LEV, 128), north_odd, jnp.int32) == 1
    for f in range(3):
        for g in range(2):
            left = jnp.zeros((LEV, 128), F32)
            right = jnp.zeros((LEV, 128), F32)
            for q in range(4):
                at = (4 * g + q) * LEV
                low = st[f, 0, at : at + LEV, :]
                high = st[f, 1, at : at + LEV, :]
                low = low if q == 0 else pltpu.roll(low, 32 * q, 1)
                high = high if q == 3 else pltpu.roll(high, 32 * q + 32, 1)
                left = jnp.where(lane == q, low, left)
                right = jnp.where(lane == q, high, right)
            at = (2 * f + g) * LEV
            edge_a[at : at + LEV, :] = jnp.where(odd, left, right)
            edge_b[at : at + LEV, :] = jnp.where(odd, right, left)
    flat = (surf[...], count, depth[...])
    lane = lanes((ROWS, 128)) // 32
    left = jnp.zeros((ROWS, 128), F32)
    right = jnp.zeros((ROWS, 128), F32)
    for q, field in enumerate(flat):
        low = field[:, :128]
        high = field[:, 128:]
        low = low if q == 0 else pltpu.roll(low, 32 * q, 1)
        high = high if q == 3 else pltpu.roll(high, 32 * q + 32, 1)
        left = jnp.where(lane == q, low, left)
        right = jnp.where(lane == q, high, right)
    odd = jnp.full((ROWS, 128), north_odd, jnp.int32) == 1
    edge_a[6 * LEV :, :] = jnp.where(odd, left, right)
    edge_b[6 * LEV :, :] = jnp.where(odd, right, left)


def ext_kernel(sc, edge_a, edge_b, plane, own, corner, flat):
    core = sc[1]
    north_odd = sc[2]

    def halves(at, size):
        a = edge_a[at : at + size, :]
        b = edge_b[at : at + size, :]
        odd = jnp.full((size, 128), north_odd, jnp.int32) == 1
        return jnp.where(odd, b, a), jnp.where(odd, a, b)

    def unpack(high, low, q):
        lane = lanes(high.shape)
        high = high if q == 0 else pltpu.roll(high, 128 - 32 * q, 1)
        low = low if q == 3 else pltpu.roll(low, 96 - 32 * q, 1)
        return jnp.where(lane < 32, high, jnp.where(lane >= 96, low, 0.0))

    for f in range(3):
        for g in range(2):
            high, low = halves((2 * f + g) * LEV, LEV)
            for q in range(4):
                at = (8 * f + 4 * g + q) * LEV
                own[at : at + LEV, :] = unpack(high, low, q)
    high, low = halves(6 * LEV, ROWS)
    count = plane[1]
    counts = (count[:, :128], count[:, 128:], unpack(high, low, 1))
    for h in range(3):
        own[24 * LEV + 8 * h : 24 * LEV + 8 * h + 8, :] = counts[h]
        corner[9 * LEV + 8 * h : 9 * LEV + 8 * h + 8, :] = counts[h]
    flat[0, :, :COLS] = plane[0]
    flat[0, :, COLS:] = unpack(high, low, 0)
    flat[1, :, :COLS] = count
    flat[1, :, COLS:] = counts[2]
    flat[2, :, :COLS] = plane[2]
    flat[2, :, COLS:] = unpack(high, low, 2)
    lane = lanes((LEV, 128))
    inner = (lane >= 32) & (lane < 96)
    for f in range(3):
        for j in range(3):
            start = pl.multiple_of((8 * f + 2 * core + 2 * j) * LEV, 8)
            first = own[pl.ds(start, LEV), :]
            second = own[pl.ds(start + LEV, LEV), :]
            at = (3 * f + j) * LEV
            corner[at : at + LEV, :] = jnp.where(inner, pltpu.roll(second, 64, 1), first)


def shifts(q):
    return (
        pltpu.roll(q, WIDE - 1, 1),
        pltpu.roll(q, 1, 1),
        pltpu.roll(q, WIDE - 2, 1),
        pltpu.roll(q, 2, 1),
    )


def slope(ahead, behind, ahead2, behind2):
    return (8.0 / 12.0) * (ahead - behind) - (1.0 / 12.0) * (ahead2 - behind2)


def running(x, sub):
    for step in (1, 2, 4):
        x = x + jnp.where(sub >= step, pltpu.roll(x, step, 0), 0.0)
    return x


def rk_kernel(chunk, sc, st, stp, own, ownp, main, corner, flat, *rest):
    levels = SIZES[chunk]
    if chunk:
        carry_in, sums_in = rest[:2]
        rest = rest[2:]
    out, carry, sums, flows, ext, one, two, counts = rest
    core = sc[1]
    lev0 = STARTS[chunk]
    for f in range(3):
        for r in range(ROWS):
            for h in range(2):
                ext[f, HALO + r, :, h * 128 : (h + 1) * 128] = st[f, h, r * LEV + lev0 : r * LEV + lev0 + levels, :]
            at = (8 * f + r) * LEV + lev0
            ext[f, HALO + r, :, COLS:] = own[at : at + levels, :]
        for j in range(HALO):
            row = 14 * (1 - core) + j
            start = pl.multiple_of((2 * core + j) * LEV + lev0, 8)
            for h in range(2):
                ext[f, row, :, h * 128 : (h + 1) * 128] = stp[f, h, pl.ds(start, levels), :]
            ext[f, row, :, COLS:] = ownp[pl.ds(pl.multiple_of(start + 8 * f * LEV, 8), levels), :]
            row = 14 * core + j
            for h in range(2):
                ext[f, row, :, h * 128 : (h + 1) * 128] = main[f, h, j * levels : (j + 1) * levels, :]
        lane = lanes((levels, 128))
        outer = (lane < 32) | (lane >= 96)
        for j in range(3):
            at = (3 * f + j) * LEV + lev0
            pair = corner[at : at + levels, :]
            row = 14 * core + 2 * j
            ext[f, row, :, COLS:] = jnp.where(outer, pair, 0.0)
            ext[f, row + 1, :, COLS:] = jnp.where(outer, pltpu.roll(pair, 64, 1), 0.0)
    for h in range(3):
        tile = own[24 * LEV + 8 * h : 24 * LEV + 8 * h + 8, :]
        for r in range(ROWS):
            counts[HALO + r, :, h * 128 : (h + 1) * 128] = jnp.broadcast_to(tile[r : r + 1, :], (8, 128))
        for j in range(HALO):
            line = ownp[pl.ds(24 * LEV + 8 * h + 2 * core + j, 1), :]
            counts[14 * (1 - core) + j, :, h * 128 : (h + 1) * 128] = jnp.broadcast_to(line, (8, 128))
            line = corner[pl.ds(9 * LEV + 8 * h + 2 * (1 - core) + j, 1), :]
            counts[14 * core + j, :, h * 128 : (h + 1) * 128] = jnp.broadcast_to(line, (8, 128))

    sub = lax.broadcasted_iota(jnp.int32, (8, WIDE), 0)

    def stage(source, rows, inset, write, slot):
        def row(o, _):
            count = counts[o + inset]
            if chunk:
                sum_x = carry_in[slot + 2 * o]
                sum_y = carry_in[slot + 2 * o + 1]
            else:
                sum_x = jnp.zeros((8, WIDE), F32)
                sum_y = jnp.zeros((8, WIDE), F32)
            for t in range(levels // 8):
                here = slice(8 * t, 8 * t + 8)
                mid = []
                dxs = []
                dys = []
                laps = []
                for f in range(3):
                    q = source[f, o + 2, here, :]
                    back2, back = source[f, o, here, :], source[f, o + 1, here, :]
                    fore, fore2 = source[f, o + 3, here, :], source[f, o + 4, here, :]
                    right, left, right2, left2 = shifts(q)
                    mid.append(q)
                    dxs.append(slope(fore, back, fore2, back2))
                    dys.append(slope(right, left, right2, left2))
                    laps.append((fore + back) + (right + left) - 4.0 * q)
                press_x = running(dxs[2], sub) + sum_x
                press_y = running(dys[2], sub) + sum_y
                sum_x = jnp.broadcast_to(press_x[7:8, :], (8, WIDE))
                sum_y = jnp.broadcast_to(press_y[7:8, :], (8, WIDE))
                u, v, _s = mid
                rates = [VISCOSITY * laps[f] - (u * dxs[f] + v * dys[f]) for f in range(3)]
                rates[0] = rates[0] + (CORIOLIS * v - PRESS_COEF * press_x)
                rates[1] = rates[1] - (CORIOLIS * u + PRESS_COEF * press_y)
                keep = count > (sub + (lev0 + 8 * t)).astype(F32)
                write(o, here, t, mid, [jnp.where(keep, r, 0.0) for r in rates])
            carry[slot + 2 * o] = sum_x
            carry[slot + 2 * o + 1] = sum_y
            return 0

        lax.fori_loop(0, rows, row, 0)

    def write1(o, here, t, mid, rates):
        for f in range(3):
            one[f, o, here, :] = mid[f] + TIME_STEP * rates[f]

    def write2(o, here, t, mid, rates):
        for f in range(3):
            first = ext[f, o + 4, here, :]
            two[f, o, here, :] = 0.75 * first + (0.25 * mid[f] + (0.25 * TIME_STEP) * rates[f])

    def write3(o, here, t, mid, rates):
        for f in range(3):
            first = ext[f, o + 6, here, :]
            value = (1.0 / 3.0) * first + ((2.0 / 3.0) * mid[f] + (2.0 / 3.0 * TIME_STEP) * rates[f])
            at = pl.multiple_of(o * levels + 8 * t, 8)
            for h in range(2):
                out[f, h, pl.ds(at, 8), :] = value[:, h * 128 : (h + 1) * 128]
            if f < 2:
                if t == 0:
                    sums[f, o] = value + sums_in[f, o] if chunk else value
                else:
                    sums[f, o] = sums[f, o] + value

    stage(ext, 16, 2, write1, 0)
    stage(one, 12, 4, write2, 32)
    stage(two, 8, 6, write3, 56)
    for f in range(2):
        for o in range(ROWS):
            flows[f, o : o + 1, :] = jnp.sum(sums[f, o], axis=0, keepdims=True)
        flows[f] = flat[2] * (flows[f] * (1.0 / LEV))
        flows[2 + f] = flat[f]


def solve_kernel(sc, mine, pair, remote, remote_pair, far, flat, *rest):
    states = rest[:CHUNKS]
    east, north, salt, level = rest[CHUNKS : CHUNKS + 4]
    wide = rest[CHUNKS + 4]
    core = sc[1]
    wide[:, 24:32, :] = mine[...]
    for slot, block in (
        (4 - 2 * core, pair[...]),
        (2 + 2 * core, remote[0]),
        (1 + 4 * core, remote[1]),
        (5 - 4 * core, remote_pair[0]),
        (6 - 6 * core, remote_pair[1]),
        (6 * core, far[...]),
    ):
        wide[:, pl.ds(pl.multiple_of(8 * slot, 8), 8), :] = block
    high = 56

    def up(x):
        return pltpu.roll(x, high - 1, 0)

    def down(x):
        return pltpu.roll(x, 1, 0)

    def right(x):
        return pltpu.roll(x, WIDE - 1, 1)

    def left(x):
        return pltpu.roll(x, 1, 1)

    wet = jnp.where(wide[3] > 0.0, 1.0, 0.0)
    dry = 1.0 - wet

    def apply(e):
        w = wet * e
        rows = up(w) + down(w)
        mix = 4.0 * w + rows
        sides = right(mix) + left(mix)
        stencil = (20.0 / 6.0) * w - (4.0 / 6.0) * rows - (1.0 / 6.0) * sides
        return wet * (SIGMA_SHIFT * e + stencil) + dry * e

    flow_east = wide[0]
    flow_north = wide[1]
    x = wide[2]
    div = 0.5 * (up(flow_east) - down(flow_east)) + 0.5 * (right(flow_north) - left(flow_north))
    res = wet * (SIGMA_SHIFT * x - DIVERGENCE_COEF * div) - apply(x)
    step = res * (1.0 / CHEB_CENTER)
    keeps, gains = cheb_table(ITERS)
    for index in range(ITERS):
        x = x + step
        if index < ITERS - 1:
            res = res - apply(step)
            step = keeps[index] * step + gains[index] * res
    slope_east = (0.5 * (up(x) - down(x)))[24:32, :COLS]
    slope_north = (0.5 * (right(x) - left(x)))[24:32, :COLS]
    level[...] = x[24:32, :COLS]
    count = flat[1][:, :COLS]
    for lev in range(LEV):
        c = max(i for i in range(CHUNKS) if STARTS[i] <= lev)
        levels = SIZES[c]
        at = lev - STARTS[c]
        keep = count > lev
        for h in range(2):
            cols = slice(h * 128, (h + 1) * 128)
            parts = [states[c][f, h, pl.ds(at, ROWS, stride=levels), :] for f in range(3)]
            east[lev, :, cols] = jnp.where(keep[:, cols], parts[0] - slope_east[:, cols], 0.0)
            north[lev, :, cols] = jnp.where(keep[:, cols], parts[1] - slope_north[:, cols], 0.0)
            salt[lev, :, cols] = parts[2]


def swap(pairs):
    return [p for a, b in pairs for p in ((a, b), (b, a))]


def call(body, outs, scratch=(), ins=0, space=pltpu.VMEM):
    vmem = pl.BlockSpec(memory_space=pltpu.VMEM)
    smem = pl.BlockSpec(memory_space=pltpu.SMEM)
    return pl.pallas_call(
        body,
        out_shape=[jax.ShapeDtypeStruct(s, F32) for s in outs],
        in_specs=[smem] + [pl.BlockSpec(memory_space=space)] * ins,
        out_specs=[vmem] * len(outs),
        scratch_shapes=[pltpu.VMEM(s, F32) if isinstance(s, tuple) else s for s in scratch],
        compiler_params=pltpu.CompilerParams(vmem_limit_bytes=16 * 1024 * 1024),
    )


def local(u, v, s, surface, depth, wet, active):
    gx = lax.axis_size("gx")
    gy = lax.axis_size("gy")
    me = lax.axis_index("gx")
    scalars = jnp.stack([me, me % 2, lax.axis_index("gy") % 2]).astype(jnp.int32)
    on_chip = swap([(i, i + 1) for i in range(0, gx, 2)])
    next_chip = swap([(i, i + 1) for i in range(1, gx - 1, 2)])
    far_chip = swap([(i, i + 3) for i in range(1, gx - 3, 2)])
    even = swap([(i, i + 1) for i in range(0, gy, 2)])
    odd = swap([(i, i + 1) for i in range(1, gy - 1, 2)])

    edge_a, edge_b, *packed = call(
        pack_kernel,
        [(6 * LEV + 8, 128)] * 2
        + [(3, 2, HALO * levels, 128) for levels in SIZES]
        + [(3, 2, ROWS * LEV, 128), (3, ROWS, COLS)],
        [pltpu.VMEM((ROWS, COLS), jnp.int32)] * 2
        + [(ROWS, COLS)] * 2
        + [(LEV, ROWS, COLS)] * 3
        + [pltpu.SemaphoreType.DMA((7,))],
        ins=7,
        space=pltpu.HBM,
    )(scalars, *(pltpu.with_memory_space_constraint(x, pltpu.HBM) for x in (u, v, s, wet, active, surface, depth)))
    mains = packed[:CHUNKS]
    st, plane = packed[CHUNKS:]
    edge_a = lax.ppermute(edge_a, "gy", even)
    edge_b = lax.ppermute(edge_b, "gy", odd)
    main = [lax.ppermute(mains[0], "gx", next_chip)]
    stp = lax.ppermute(st, "gx", on_chip)
    own, corner, flat = call(
        ext_kernel,
        [(24 * LEV + 24, 128), (9 * LEV + 24, 128), (3, ROWS, WIDE)],
        ins=3,
    )(scalars, edge_a, edge_b, plane)
    corner, own, *mains = lax.optimization_barrier((corner, own, *mains[1:]))
    corner = lax.ppermute(corner, "gx", next_chip)
    ownp = lax.ppermute(own, "gx", on_chip)
    main += [lax.ppermute(m, "gx", next_chip) for m in mains]

    states = []
    tail = []
    for c, levels in enumerate(SIZES):
        out, carry, sums, flows = call(
            functools.partial(rk_kernel, c),
            [(3, 2, ROWS * levels, 128), (72, 8, WIDE), (2, ROWS, 8, WIDE), (4, ROWS, WIDE)],
            [(3, 20, levels, WIDE), (3, 16, levels, WIDE), (3, 12, levels, WIDE), (20, 8, WIDE)],
            ins=7 + len(tail),
        )(scalars, st, stp, own, ownp, main[c], corner, flat, *tail)
        tail = [carry, sums]
        states.append(out)
    far = lax.ppermute(flows, "gx", far_chip)
    pair = lax.ppermute(flows, "gx", on_chip)
    remote = lax.ppermute(jnp.stack([flows, pair]), "gx", next_chip)
    remote_pair = lax.ppermute(remote, "gx", on_chip)
    east, north, salt, level = call(
        solve_kernel,
        [(LEV, ROWS, COLS)] * 3 + [(ROWS, COLS)],
        [(4, 56, WIDE)],
        ins=6 + CHUNKS,
    )(scalars, flows, pair, remote, remote_pair, far, flat, *states)
    return east, north, salt, level


def solution(mesh):
    cube = P(None, "gx", "gy")
    flat = P("gx", "gy")
    return jax.shard_map(
        local,
        mesh=mesh,
        in_specs=(cube, cube, cube, flat, flat, flat, flat),
        out_specs=(cube, cube, cube, flat),
        check_vma=False,
    )
```

```python
import functools

import jax
import jax.numpy as jnp
from jax import lax
from jax.experimental import pallas as pl
from jax.experimental.pallas import tpu as pltpu
from jax.sharding import PartitionSpec as P

ITERS = 16
TIME_STEP = 0.2
CORIOLIS = 0.3
PRESS_COEF = 0.05
VISCOSITY = 0.1
DIFFUSIVITY = 0.1
SIGMA_SHIFT = 0.25
CHEB_CENTER = 3.625
CHEB_HALF = 3.375
DIVERGENCE_COEF = 8.0

LEV = 48
ROWS = 8
COLS = 256
EXT = 128
WIDE = COLS + EXT
HALO = 6
SIZES = (32, 16)
CHUNKS = len(SIZES)
STARTS = tuple(sum(SIZES[:c]) for c in range(CHUNKS))
SLOT = 25
SLOTS = 5
EDGE_TILES = -(-3 * ROWS // SLOTS)
CORNER_TILES = -(-3 * HALO // SLOTS)
F32 = jnp.float32


def cheb_table(count):
    first = CHEB_CENTER / CHEB_HALF
    ratio = 1.0 / first
    keeps = []
    gains = []
    for index in range(count):
        ratio_next = 1.0 / (2.0 * first - ratio)
        keeps.append(ratio_next * ratio)
        gains.append(2.0 * ratio_next / CHEB_HALF)
        ratio = ratio_next
    return (keeps, gains)


def lanes(shape):
    return lax.broadcasted_iota(jnp.int32, shape, len(shape) - 1)


def place(low, high, units, slot):
    left, right = units
    lane = lanes(low.shape)
    here = (lane >= SLOT * slot) & (lane < SLOT * slot + SLOT)
    low = low if slot == 0 else pltpu.roll(low, SLOT * slot, 1)
    high = pltpu.roll(high, SLOT * slot + SLOT, 1)
    return jnp.where(here, low, left), jnp.where(here, high, right)


def unpack(high, low, slot):
    lane = lanes(high.shape)
    high = high if slot == 0 else pltpu.roll(high, 128 - SLOT * slot, 1)
    low = pltpu.roll(low, 128 - SLOT - SLOT * slot, 1)
    return jnp.where(lane < SLOT, high, jnp.where(lane >= 128 - SLOT, low, 0.0))


def ordered(first, second, flag):
    odd = jnp.full(first.shape, flag, jnp.int32) == 1
    return jnp.where(odd, second, first), jnp.where(odd, first, second)


def pack_kernel(sc, u, v, s, wet, act, surf, depth, edge_a, edge_b, corner_a, corner_b, *rest):
    mains = rest[:CHUNKS]
    st, plane = rest[CHUNKS : CHUNKS + 2]
    buffers = rest[CHUNKS + 2 : CHUNKS + 9]
    sems = rest[CHUNKS + 9]
    core = sc[1]
    north_odd = sc[2]
    sources = (wet, act, surf, depth, u, v, s)
    copies = [pltpu.make_async_copy(a, b, sems.at[i]) for i, (a, b) in enumerate(zip(sources, buffers))]
    for copy in copies:
        copy.start()
    for copy in copies[:4]:
        copy.wait()
    wet, act, surf, depth, *cubes = buffers
    count = (act[...] * wet[...]).astype(F32)
    plane[0] = surf[...]
    plane[1] = count
    plane[2] = depth[...]
    for f in range(3):
        copies[4 + f].wait()
        for lev in range(LEV):
            tile = jnp.where(count > lev, cubes[f][lev], 0.0)
            for h in range(2):
                st[pl.ds((2 * f + h) * ROWS * LEV + lev, ROWS, stride=LEV), :] = tile[:, h * 128 : (h + 1) * 128]
    base = 2 * core
    for c in range(CHUNKS):
        levels = SIZES[c]
        for f in range(3):
            for j in range(HALO):
                for h in range(2):
                    start = pl.multiple_of(((2 * f + h) * ROWS + base + j) * LEV + STARTS[c], 8)
                    at = ((2 * f + h) * HALO + j) * levels
                    mains[c][at : at + levels, :] = st[pl.ds(start, levels), :]
    for h in range(2):
        at = 6 * HALO * SIZES[0] + 8 * h
        mains[0][at : at + 8, :] = count[:, 128 * h : 128 * h + 128]
        at = 6 * ROWS * LEV + 8 * h
        st[at : at + 8, :] = count[:, 128 * h : 128 * h + 128]
    blank = jnp.zeros((LEV, 128), F32)
    for tiles, rows, first, a, b in (
        (EDGE_TILES, ROWS, 0, edge_a, edge_b),
        (CORNER_TILES, HALO, base, corner_a, corner_b),
    ):
        for g in range(tiles):
            units = (blank, blank)
            for slot in range(min(SLOTS, 3 * rows - SLOTS * g)):
                f, r = divmod(SLOTS * g + slot, rows)
                low = pl.multiple_of((2 * f * ROWS + first + r) * LEV, 8)
                high = pl.multiple_of(((2 * f + 1) * ROWS + first + r) * LEV, 8)
                units = place(st[pl.ds(low, LEV), :], st[pl.ds(high, LEV), :], units, slot)
            b[g * LEV : g * LEV + LEV, :], a[g * LEV : g * LEV + LEV, :] = ordered(*units, north_odd)
    units = (blank[:ROWS], blank[:ROWS])
    for slot, field in enumerate((surf[...], count, depth[...])):
        units = place(field[:, :128], field[:, 128:], units, slot)
    left, right = ordered(*units, north_odd)
    for tiles, a, b in ((EDGE_TILES, edge_a, edge_b), (CORNER_TILES, corner_a, corner_b)):
        b[tiles * LEV :, :] = left
        a[tiles * LEV :, :] = right


def shifts(q):
    return (
        pltpu.roll(q, WIDE - 1, 1),
        pltpu.roll(q, 1, 1),
        pltpu.roll(q, WIDE - 2, 1),
        pltpu.roll(q, 2, 1),
    )


def slope(ahead, behind, ahead2, behind2):
    return (8.0 / 12.0) * (ahead - behind) - (1.0 / 12.0) * (ahead2 - behind2)


def running(x, sub):
    for step in (1, 2, 4):
        x = x + jnp.where(sub >= step, pltpu.roll(x, step, 0), 0.0)
    return x


def rk_kernel(chunk, sc, st, stp, edge_a, edge_b, edgep_a, edgep_b, main, main0, corner_a, corner_b, plane, *rest):
    levels = SIZES[chunk]
    if chunk:
        carry_in, sums_in = rest[:2]
        rest = rest[2:]
    if chunk == CHUNKS - 1:
        flows, rest = rest[0], rest[1:]
    out, carry, sums, ext, one, two, counts, flat, remote = rest
    core = sc[1]
    north_odd = sc[2]
    lev0 = STARTS[chunk]
    beside = 16 * (1 - core)
    beyond = 2 + 14 * core
    for source, first in ((st, ROWS), (stp, beside)):
        for f in range(3):
            for r in range(ROWS):
                for h in range(2):
                    at = ((2 * f + h) * ROWS + r) * LEV + lev0
                    ext[f, first + r, :, h * 128 : (h + 1) * 128] = source[at : at + levels, :]
    for f in range(3):
        for j in range(HALO):
            for h in range(2):
                at = ((2 * f + h) * HALO + j) * levels
                ext[f, beyond + j, :, h * 128 : (h + 1) * 128] = main[at : at + levels, :]
    for tiles, rows, first, a, b in (
        (EDGE_TILES, ROWS, ROWS, edge_a, edge_b),
        (EDGE_TILES, ROWS, beside, edgep_a, edgep_b),
        (CORNER_TILES, HALO, beyond, corner_a, corner_b),
    ):
        for g in range(tiles):
            here = slice(g * LEV + lev0, g * LEV + lev0 + levels)
            high, low = ordered(a[here, :], b[here, :], north_odd)
            for slot in range(min(SLOTS, 3 * rows - SLOTS * g)):
                f, r = divmod(SLOTS * g + slot, rows)
                ext[f, first + r, :, COLS:] = unpack(high, low, slot)

    def beyond_plane(tiles, a, b, slot):
        high, low = ordered(a[tiles * LEV :, :], b[tiles * LEV :, :], north_odd)
        return unpack(high, low, slot)

    for f in range(3):
        flat[f, :, :COLS] = plane[f]
        flat[f, :, COLS:] = beyond_plane(EDGE_TILES, edge_a, edge_b, f)
    remote[0, :, COLS:] = beyond_plane(EDGE_TILES, edgep_a, edgep_b, 1)
    remote[1, :, COLS:] = beyond_plane(CORNER_TILES, corner_a, corner_b, 1)
    for h in range(2):
        at = 6 * ROWS * LEV + 8 * h
        remote[0, :, h * 128 : (h + 1) * 128] = stp[at : at + 8, :]
        at = 6 * HALO * SIZES[0] + 8 * h
        remote[1, :, h * 128 : (h + 1) * 128] = main0[at : at + 8, :]
    for r in range(ROWS):
        counts[ROWS + r] = jnp.broadcast_to(flat[1, r : r + 1, :], (8, WIDE))
        counts[beside + r] = jnp.broadcast_to(remote[0, r : r + 1, :], (8, WIDE))
    for j in range(HALO):
        counts[beyond + j] = jnp.broadcast_to(remote[1, pl.ds(2 * (1 - core) + j, 1), :], (8, WIDE))

    sub = lax.broadcasted_iota(jnp.int32, (8, WIDE), 0)

    def stage(source, lead, rows, inset, write, slot):
        def row(o, _):
            count = counts[o + inset]
            if chunk:
                sum_x = jnp.broadcast_to(carry_in[pl.ds(slot + 2 * o, 1), :], (8, WIDE))
                sum_y = jnp.broadcast_to(carry_in[pl.ds(slot + 2 * o + 1, 1), :], (8, WIDE))
            else:
                sum_x = jnp.zeros((8, WIDE), F32)
                sum_y = jnp.zeros((8, WIDE), F32)
            for t in range(levels // 8):
                here = slice(8 * t, 8 * t + 8)
                mid = []
                dxs = []
                dys = []
                laps = []
                for f in range(3):
                    q = source[f, o + lead + 2, here, :]
                    back2, back = source[f, o + lead, here, :], source[f, o + lead + 1, here, :]
                    fore, fore2 = source[f, o + lead + 3, here, :], source[f, o + lead + 4, here, :]
                    right, left, right2, left2 = shifts(q)
                    mid.append(q)
                    dxs.append(slope(fore, back, fore2, back2))
                    dys.append(slope(right, left, right2, left2))
                    laps.append((fore + back) + (right + left) - 4.0 * q)
                press_x = running(dxs[2], sub) + sum_x
                press_y = running(dys[2], sub) + sum_y
                sum_x = jnp.broadcast_to(press_x[7:8, :], (8, WIDE))
                sum_y = jnp.broadcast_to(press_y[7:8, :], (8, WIDE))
                u, v, _s = mid
                rates = [VISCOSITY * laps[f] - (u * dxs[f] + v * dys[f]) for f in range(3)]
                rates[0] = rates[0] + (CORIOLIS * v - PRESS_COEF * press_x)
                rates[1] = rates[1] - (CORIOLIS * u + PRESS_COEF * press_y)
                keep = count > (sub + (lev0 + 8 * t)).astype(F32)
                write(o, here, t, mid, [jnp.where(keep, r, 0.0) for r in rates])
            carry[pl.ds(slot + 2 * o, 1), :] = sum_x[:1, :]
            carry[pl.ds(slot + 2 * o + 1, 1), :] = sum_y[:1, :]
            return 0

        lax.fori_loop(0, rows, row, 0, unroll=max(1, min(4, 32 // levels)))

    def write1(o, here, t, mid, rates):
        for f in range(3):
            one[f, o, here, :] = mid[f] + TIME_STEP * rates[f]

    def write2(o, here, t, mid, rates):
        for f in range(3):
            first = ext[f, o + 6, here, :]
            two[f, o, here, :] = 0.75 * first + (0.25 * mid[f] + (0.25 * TIME_STEP) * rates[f])

    def write3(o, here, t, mid, rates):
        for f in range(3):
            first = ext[f, o + 8, here, :]
            value = (1.0 / 3.0) * first + ((2.0 / 3.0) * mid[f] + (2.0 / 3.0 * TIME_STEP) * rates[f])
            at = pl.multiple_of(o * levels + 8 * t, 8)
            for h in range(2):
                out[f, h, pl.ds(at, 8), :] = value[:, h * 128 : (h + 1) * 128]
            if f < 2:
                if t == 0:
                    sums[f, o] = value + sums_in[f, o] if chunk else value
                else:
                    sums[f, o] = sums[f, o] + value

    stage(ext, 2, 16, 4, write1, 0)
    stage(one, 0, 12, 6, write2, 32)
    stage(two, 0, 8, 8, write3, 56)
    if chunk == CHUNKS - 1:
        for f in range(2):
            for o in range(ROWS):
                flows[f, o : o + 1, :] = jnp.sum(sums[f, o], axis=0, keepdims=True)
            flows[f] = flat[2] * (flows[f] * (1.0 / LEV))
            flows[2 + f] = flat[f]


def solve_kernel(sc, mine, pair, remote, remote_pair, far, *rest):
    states = rest[:CHUNKS]
    east, north, salt, level = rest[CHUNKS : CHUNKS + 4]
    wide = rest[CHUNKS + 4]
    core = sc[1]
    wide[:, 24:32, :] = mine[...]
    for slot, block in (
        (4 - 2 * core, pair[...]),
        (2 + 2 * core, remote[0]),
        (1 + 4 * core, remote[1]),
        (5 - 4 * core, remote_pair[0]),
        (6 - 6 * core, remote_pair[1]),
        (6 * core, far[...]),
    ):
        wide[:, pl.ds(pl.multiple_of(8 * slot, 8), 8), :] = block
    high = 56

    def up(x):
        return pltpu.roll(x, high - 1, 0)

    def down(x):
        return pltpu.roll(x, 1, 0)

    def right(x):
        return pltpu.roll(x, WIDE - 1, 1)

    def left(x):
        return pltpu.roll(x, 1, 1)

    wet = jnp.where(wide[3] > 0.0, 1.0, 0.0)
    dry = 1.0 - wet

    def apply(e):
        w = wet * e
        rows = up(w) + down(w)
        mix = 4.0 * w + rows
        sides = right(mix) + left(mix)
        stencil = (20.0 / 6.0) * w - (4.0 / 6.0) * rows - (1.0 / 6.0) * sides
        return wet * (SIGMA_SHIFT * e + stencil) + dry * e

    flow_east = wide[0]
    flow_north = wide[1]
    x = wide[2]
    div = 0.5 * (up(flow_east) - down(flow_east)) + 0.5 * (right(flow_north) - left(flow_north))
    res = wet * (SIGMA_SHIFT * x - DIVERGENCE_COEF * div) - apply(x)
    step = res * (1.0 / CHEB_CENTER)
    keeps, gains = cheb_table(ITERS)
    for index in range(ITERS):
        x = x + step
        if index < ITERS - 1:
            res = res - apply(step)
            step = keeps[index] * step + gains[index] * res
    slope_east = (0.5 * (up(x) - down(x)))[24:32, :COLS]
    slope_north = (0.5 * (right(x) - left(x)))[24:32, :COLS]
    level[...] = x[24:32, :COLS]
    count = mine[3][:, :COLS]
    for lev in range(LEV):
        c = max(i for i in range(CHUNKS) if STARTS[i] <= lev)
        levels = SIZES[c]
        at = lev - STARTS[c]
        keep = count > lev
        for h in range(2):
            cols = slice(h * 128, (h + 1) * 128)
            parts = [states[c][f, h, pl.ds(at, ROWS, stride=levels), :] for f in range(3)]
            east[lev, :, cols] = jnp.where(keep[:, cols], parts[0] - slope_east[:, cols], 0.0)
            north[lev, :, cols] = jnp.where(keep[:, cols], parts[1] - slope_north[:, cols], 0.0)
            salt[lev, :, cols] = parts[2]


def swap(pairs):
    return [p for a, b in pairs for p in ((a, b), (b, a))]


def call(body, outs, scratch=(), ins=0, space=pltpu.VMEM, cost=None):
    vmem = pl.BlockSpec(memory_space=pltpu.VMEM)
    smem = pl.BlockSpec(memory_space=pltpu.SMEM)
    return pl.pallas_call(
        body,
        out_shape=[jax.ShapeDtypeStruct(s, F32) for s in outs],
        in_specs=[smem] + [pl.BlockSpec(memory_space=space)] * ins,
        out_specs=[vmem] * len(outs),
        scratch_shapes=[pltpu.VMEM(s, F32) if isinstance(s, tuple) else s for s in scratch],
        cost_estimate=cost and pl.CostEstimate(flops=cost, transcendentals=0, bytes_accessed=0),
        compiler_params=pltpu.CompilerParams(vmem_limit_bytes=16 * 1024 * 1024),
    )


def local(u, v, s, surface, depth, wet, active):
    gx = lax.axis_size("gx")
    gy = lax.axis_size("gy")
    me = lax.axis_index("gx")
    scalars = jnp.stack([me, me % 2, lax.axis_index("gy") % 2]).astype(jnp.int32)
    on_chip = swap([(i, i + 1) for i in range(0, gx, 2)])
    next_chip = swap([(i, i + 1) for i in range(1, gx - 1, 2)])
    far_chip = swap([(i, i + 3) for i in range(1, gx - 3, 2)])
    even = swap([(i, i + 1) for i in range(0, gy, 2)])
    odd = swap([(i, i + 1) for i in range(1, gy - 1, 2)])

    def both(first, second):
        return [(i * gy + j, k * gy + l) for i, k in first for j, l in second]

    edge_a, edge_b, corner_a, corner_b, *packed = call(
        pack_kernel,
        [(EDGE_TILES * LEV + 8, 128)] * 2
        + [(CORNER_TILES * LEV + 8, 128)] * 2
        + [(6 * HALO * levels + (0 if c else 16), 128) for c, levels in enumerate(SIZES)]
        + [(6 * ROWS * LEV + 16, 128), (3, ROWS, COLS)],
        [pltpu.VMEM((ROWS, COLS), jnp.int32)] * 2
        + [(ROWS, COLS)] * 2
        + [(LEV, ROWS, COLS)] * 3
        + [pltpu.SemaphoreType.DMA((7,))],
        ins=7,
        space=pltpu.HBM,
    )(scalars, *(pltpu.with_memory_space_constraint(x, pltpu.HBM) for x in (u, v, s, wet, active, surface, depth)))
    mains = packed[:CHUNKS]
    st, plane = packed[CHUNKS:]
    stp = lax.ppermute(st, "gx", on_chip)
    main = [lax.ppermute(mains[0], "gx", next_chip)]
    stp, corner_a, corner_b = lax.optimization_barrier((stp, corner_a, corner_b))
    edge_a = lax.ppermute(edge_a, "gy", even)
    edge_b = lax.ppermute(edge_b, "gy", odd)
    corner_a = lax.ppermute(corner_a, ("gx", "gy"), both(next_chip, even))
    corner_b = lax.ppermute(corner_b, ("gx", "gy"), both(next_chip, odd))
    corner_a, corner_b, edge_a, edge_b, *later = lax.optimization_barrier((corner_a, corner_b, edge_a, edge_b, *mains[1:]))
    main += [lax.ppermute(m, "gx", next_chip) for m in later]
    edgep_a = lax.ppermute(edge_a, "gx", on_chip)
    edgep_b = lax.ppermute(edge_b, "gx", on_chip)

    states = []
    tail = []
    for c, levels in enumerate(SIZES):
        *flows, out, carry, sums = call(
            functools.partial(rk_kernel, c),
            [(4, ROWS, WIDE)] * (c == CHUNKS - 1)
            + [(3, 2, ROWS * levels, 128), (72, WIDE), (2, ROWS, 8, WIDE)],
            [(3, 24, levels, WIDE), (3, 16, levels, WIDE), (3, 12, levels, WIDE)]
            + [(24, 8, WIDE), (3, ROWS, WIDE), (2, ROWS, WIDE)],
            ins=11 + len(tail),
        )(scalars, st, stp, edge_a, edge_b, edgep_a, edgep_b, main[c], main[0], corner_a, corner_b, plane, *tail)
        tail = [carry, sums]
        states.append(out)
    flows = flows[0]
    far = lax.ppermute(flows, "gx", far_chip)
    pair = lax.ppermute(flows, "gx", on_chip)
    remote = lax.ppermute(jnp.stack([flows, pair]), "gx", next_chip)
    remote, far = lax.optimization_barrier((remote, far))
    remote_pair = lax.ppermute(remote, "gx", on_chip)
    east, north, salt, level = call(
        solve_kernel,
        [(LEV, ROWS, COLS)] * 3 + [(ROWS, COLS)],
        [(4, 56, WIDE)],
        ins=5 + CHUNKS,
    )(scalars, flows, pair, remote, remote_pair, far, *states)
    return east, north, salt, level


def solution(mesh):
    cube = P(None, "gx", "gy")
    flat = P("gx", "gy")
    return jax.shard_map(
        local,
        mesh=mesh,
        in_specs=(cube, cube, cube, flat, flat, flat, flat),
        out_specs=(cube, cube, cube, flat),
        check_vma=False,
    )
```

```python
import functools

import jax
import jax.numpy as jnp
from jax import lax
from jax.experimental import pallas as pl
from jax.experimental.pallas import tpu as pltpu
from jax.sharding import PartitionSpec as P

ITERS = 16
TIME_STEP = 0.2
CORIOLIS = 0.3
PRESS_COEF = 0.05
VISCOSITY = 0.1
DIFFUSIVITY = 0.1
SIGMA_SHIFT = 0.25
CHEB_CENTER = 3.625
CHEB_HALF = 3.375
DIVERGENCE_COEF = 8.0

LEV = 48
ROWS = 8
COLS = 256
EXT = 128
WIDE = COLS + EXT
HALO = 6
SIZES = (32, 16)
CHUNKS = len(SIZES)
STARTS = tuple(sum(SIZES[:c]) for c in range(CHUNKS))
SLOT = 25
SLOTS = 5
EDGE_TILES = -(-3 * ROWS // SLOTS)
CORNER_TILES = -(-3 * HALO // SLOTS)
F32 = jnp.float32


def cheb_table(count):
    first = CHEB_CENTER / CHEB_HALF
    ratio = 1.0 / first
    keeps = []
    gains = []
    for index in range(count):
        ratio_next = 1.0 / (2.0 * first - ratio)
        keeps.append(ratio_next * ratio)
        gains.append(2.0 * ratio_next / CHEB_HALF)
        ratio = ratio_next
    return (keeps, gains)


def lanes(shape):
    return lax.broadcasted_iota(jnp.int32, shape, len(shape) - 1)


def place(low, high, units, slot):
    left, right = units
    lane = lanes(low.shape)
    here = (lane >= SLOT * slot) & (lane < SLOT * slot + SLOT)
    low = low if slot == 0 else pltpu.roll(low, SLOT * slot, 1)
    high = pltpu.roll(high, SLOT * slot + SLOT, 1)
    return jnp.where(here, low, left), jnp.where(here, high, right)


def unpack(high, low, slot):
    lane = lanes(high.shape)
    high = high if slot == 0 else pltpu.roll(high, 128 - SLOT * slot, 1)
    low = pltpu.roll(low, 128 - SLOT - SLOT * slot, 1)
    return jnp.where(lane < SLOT, high, jnp.where(lane >= 128 - SLOT, low, 0.0))


def ordered(first, second, flag):
    odd = jnp.full(first.shape, flag, jnp.int32) == 1
    return jnp.where(odd, second, first), jnp.where(odd, first, second)


def pack_kernel(sc, u, v, s, wet, act, surf, depth, edge_a, edge_b, corner_a, corner_b, *rest):
    mains = rest[:CHUNKS]
    st, plane = rest[CHUNKS : CHUNKS + 2]
    buffers = rest[CHUNKS + 2 : CHUNKS + 9]
    sems = rest[CHUNKS + 9]
    core = sc[1]
    north_odd = sc[2]
    sources = (wet, act, surf, depth, u, v, s)
    copies = [pltpu.make_async_copy(a, b, sems.at[i]) for i, (a, b) in enumerate(zip(sources, buffers))]
    for copy in copies:
        copy.start()
    for copy in copies[:4]:
        copy.wait()
    wet, act, surf, depth, *cubes = buffers
    count = (act[...] * wet[...]).astype(F32)
    plane[0] = surf[...]
    plane[1] = count
    plane[2] = depth[...]
    for f in range(3):
        copies[4 + f].wait()
        for lev in range(LEV):
            tile = jnp.where(count > lev, cubes[f][lev], 0.0)
            for h in range(2):
                st[pl.ds((2 * f + h) * ROWS * LEV + lev, ROWS, stride=LEV), :] = tile[:, h * 128 : (h + 1) * 128]
    base = 2 * core
    for c in range(CHUNKS):
        levels = SIZES[c]
        for f in range(3):
            for j in range(HALO):
                for h in range(2):
                    start = pl.multiple_of(((2 * f + h) * ROWS + base + j) * LEV + STARTS[c], 8)
                    at = ((2 * f + h) * HALO + j) * levels
                    mains[c][at : at + levels, :] = st[pl.ds(start, levels), :]
    for h in range(2):
        at = 6 * HALO * SIZES[0] + 8 * h
        mains[0][at : at + 8, :] = count[:, 128 * h : 128 * h + 128]
        at = 6 * ROWS * LEV + 8 * h
        st[at : at + 8, :] = count[:, 128 * h : 128 * h + 128]
    blank = jnp.zeros((LEV, 128), F32)
    for tiles, rows, first, a, b in (
        (EDGE_TILES, ROWS, 0, edge_a, edge_b),
        (CORNER_TILES, HALO, base, corner_a, corner_b),
    ):
        for g in range(tiles):
            units = (blank, blank)
            for slot in range(min(SLOTS, 3 * rows - SLOTS * g)):
                f, r = divmod(SLOTS * g + slot, rows)
                low = pl.multiple_of((2 * f * ROWS + first + r) * LEV, 8)
                high = pl.multiple_of(((2 * f + 1) * ROWS + first + r) * LEV, 8)
                units = place(st[pl.ds(low, LEV), :], st[pl.ds(high, LEV), :], units, slot)
            b[g * LEV : g * LEV + LEV, :], a[g * LEV : g * LEV + LEV, :] = ordered(*units, north_odd)
    units = (blank[:ROWS], blank[:ROWS])
    for slot, field in enumerate((surf[...], count, depth[...])):
        units = place(field[:, :128], field[:, 128:], units, slot)
    left, right = ordered(*units, north_odd)
    for tiles, a, b in ((EDGE_TILES, edge_a, edge_b), (CORNER_TILES, corner_a, corner_b)):
        b[tiles * LEV :, :] = left
        a[tiles * LEV :, :] = right


def shifts(q):
    return (
        pltpu.roll(q, WIDE - 1, 1),
        pltpu.roll(q, 1, 1),
        pltpu.roll(q, WIDE - 2, 1),
        pltpu.roll(q, 2, 1),
    )


def slope(ahead, behind, ahead2, behind2):
    return (8.0 / 12.0) * (ahead - behind) - (1.0 / 12.0) * (ahead2 - behind2)


def running(x, sub):
    for step in (1, 2, 4):
        x = x + jnp.where(sub >= step, pltpu.roll(x, step, 0), 0.0)
    return x


def rk_kernel(chunk, sc, st, stp, edge_a, edge_b, edgep_a, edgep_b, main, main0, corner_a, corner_b, plane, *rest):
    levels = SIZES[chunk]
    if chunk:
        carry_in, sums_in = rest[:2]
        rest = rest[2:]
    if chunk == CHUNKS - 1:
        flows, rest = rest[0], rest[1:]
    out, carry, sums, ext, one, two, counts, flat, remote = rest
    core = sc[1]
    north_odd = sc[2]
    lev0 = STARTS[chunk]
    beside = 16 * (1 - core)
    beyond = 2 + 14 * core
    for source, first in ((st, ROWS), (stp, beside)):
        for f in range(3):
            for r in range(ROWS):
                for h in range(2):
                    at = ((2 * f + h) * ROWS + r) * LEV + lev0
                    ext[f, first + r, :, h * 128 : (h + 1) * 128] = source[at : at + levels, :]
    for f in range(3):
        for j in range(HALO):
            for h in range(2):
                at = ((2 * f + h) * HALO + j) * levels
                ext[f, beyond + j, :, h * 128 : (h + 1) * 128] = main[at : at + levels, :]
    for tiles, rows, first, a, b in (
        (EDGE_TILES, ROWS, ROWS, edge_a, edge_b),
        (EDGE_TILES, ROWS, beside, edgep_a, edgep_b),
        (CORNER_TILES, HALO, beyond, corner_a, corner_b),
    ):
        for g in range(tiles):
            here = slice(g * LEV + lev0, g * LEV + lev0 + levels)
            high, low = ordered(a[here, :], b[here, :], north_odd)
            for slot in range(min(SLOTS, 3 * rows - SLOTS * g)):
                f, r = divmod(SLOTS * g + slot, rows)
                ext[f, first + r, :, COLS:] = unpack(high, low, slot)

    def beyond_plane(tiles, a, b, slot):
        high, low = ordered(a[tiles * LEV :, :], b[tiles * LEV :, :], north_odd)
        return unpack(high, low, slot)

    for f in range(3):
        flat[f, :, :COLS] = plane[f]
        flat[f, :, COLS:] = beyond_plane(EDGE_TILES, edge_a, edge_b, f)
    remote[0, :, COLS:] = beyond_plane(EDGE_TILES, edgep_a, edgep_b, 1)
    remote[1, :, COLS:] = beyond_plane(CORNER_TILES, corner_a, corner_b, 1)
    for h in range(2):
        at = 6 * ROWS * LEV + 8 * h
        remote[0, :, h * 128 : (h + 1) * 128] = stp[at : at + 8, :]
        at = 6 * HALO * SIZES[0] + 8 * h
        remote[1, :, h * 128 : (h + 1) * 128] = main0[at : at + 8, :]
    for r in range(ROWS):
        counts[ROWS + r] = jnp.broadcast_to(flat[1, r : r + 1, :], (8, WIDE))
        counts[beside + r] = jnp.broadcast_to(remote[0, r : r + 1, :], (8, WIDE))
    for j in range(HALO):
        counts[beyond + j] = jnp.broadcast_to(remote[1, pl.ds(2 * (1 - core) + j, 1), :], (8, WIDE))

    sub = lax.broadcasted_iota(jnp.int32, (8, WIDE), 0)

    def stage(source, lead, rows, inset, write, slot):
        def row(o, _):
            count = counts[o + inset]
            if chunk:
                sum_x = jnp.broadcast_to(carry_in[pl.ds(slot + 2 * o, 1), :], (8, WIDE))
                sum_y = jnp.broadcast_to(carry_in[pl.ds(slot + 2 * o + 1, 1), :], (8, WIDE))
            else:
                sum_x = jnp.zeros((8, WIDE), F32)
                sum_y = jnp.zeros((8, WIDE), F32)
            for t in range(levels // 8):
                here = slice(8 * t, 8 * t + 8)
                mid = []
                dxs = []
                dys = []
                laps = []
                for f in range(3):
                    q = source[f, o + lead + 2, here, :]
                    back2, back = source[f, o + lead, here, :], source[f, o + lead + 1, here, :]
                    fore, fore2 = source[f, o + lead + 3, here, :], source[f, o + lead + 4, here, :]
                    right, left, right2, left2 = shifts(q)
                    mid.append(q)
                    dxs.append(slope(fore, back, fore2, back2))
                    dys.append(slope(right, left, right2, left2))
                    laps.append((fore + back) + (right + left) - 4.0 * q)
                press_x = running(dxs[2], sub) + sum_x
                press_y = running(dys[2], sub) + sum_y
                sum_x = jnp.broadcast_to(press_x[7:8, :], (8, WIDE))
                sum_y = jnp.broadcast_to(press_y[7:8, :], (8, WIDE))
                u, v, _s = mid
                rates = [VISCOSITY * laps[f] - (u * dxs[f] + v * dys[f]) for f in range(3)]
                rates[0] = rates[0] + (CORIOLIS * v - PRESS_COEF * press_x)
                rates[1] = rates[1] - (CORIOLIS * u + PRESS_COEF * press_y)
                keep = count > (sub + (lev0 + 8 * t)).astype(F32)
                write(o, here, t, mid, [jnp.where(keep, r, 0.0) for r in rates])
            carry[pl.ds(slot + 2 * o, 1), :] = sum_x[:1, :]
            carry[pl.ds(slot + 2 * o + 1, 1), :] = sum_y[:1, :]
            return 0

        lax.fori_loop(0, rows, row, 0, unroll=max(1, min(4, 32 // levels)))

    def write1(o, here, t, mid, rates):
        for f in range(3):
            one[f, o, here, :] = mid[f] + TIME_STEP * rates[f]

    def write2(o, here, t, mid, rates):
        for f in range(3):
            first = ext[f, o + 6, here, :]
            two[f, o, here, :] = 0.75 * first + (0.25 * mid[f] + (0.25 * TIME_STEP) * rates[f])

    def write3(o, here, t, mid, rates):
        for f in range(3):
            first = ext[f, o + 8, here, :]
            value = (1.0 / 3.0) * first + ((2.0 / 3.0) * mid[f] + (2.0 / 3.0 * TIME_STEP) * rates[f])
            at = pl.multiple_of(o * levels + 8 * t, 8)
            for h in range(2):
                out[f, h, pl.ds(at, 8), :] = value[:, h * 128 : (h + 1) * 128]
            if f < 2:
                if t == 0:
                    sums[f, o] = value + sums_in[f, o] if chunk else value
                else:
                    sums[f, o] = sums[f, o] + value

    stage(ext, 2, 16, 4, write1, 0)
    stage(one, 0, 12, 6, write2, 32)
    stage(two, 0, 8, 8, write3, 56)
    if chunk == CHUNKS - 1:
        for f in range(2):
            for o in range(ROWS):
                flows[f, o : o + 1, :] = jnp.sum(sums[f, o], axis=0, keepdims=True)
            flows[f] = flat[2] * (flows[f] * (1.0 / LEV))
            flows[2 + f] = flat[f]


def solve_kernel(sc, mine, pair, remote, remote_pair, far, *rest):
    states = rest[:CHUNKS]
    east, north, salt, level = rest[CHUNKS : CHUNKS + 4]
    wide = rest[CHUNKS + 4]
    core = sc[1]
    wide[:, 24:32, :] = mine[...]
    for slot, block in (
        (4 - 2 * core, pair[...]),
        (2 + 2 * core, remote[0]),
        (1 + 4 * core, remote[1]),
        (5 - 4 * core, remote_pair[0]),
        (6 - 6 * core, remote_pair[1]),
        (6 * core, far[...]),
    ):
        wide[:, pl.ds(pl.multiple_of(8 * slot, 8), 8), :] = block
    high = 56

    def up(x):
        return pltpu.roll(x, high - 1, 0)

    def down(x):
        return pltpu.roll(x, 1, 0)

    def right(x):
        return pltpu.roll(x, WIDE - 1, 1)

    def left(x):
        return pltpu.roll(x, 1, 1)

    wet = jnp.where(wide[3] > 0.0, 1.0, 0.0)
    dry = 1.0 - wet

    def apply(e):
        w = wet * e
        rows = up(w) + down(w)
        mix = 4.0 * w + rows
        sides = right(mix) + left(mix)
        stencil = (20.0 / 6.0) * w - (4.0 / 6.0) * rows - (1.0 / 6.0) * sides
        return wet * (SIGMA_SHIFT * e + stencil) + dry * e

    flow_east = wide[0]
    flow_north = wide[1]
    x = wide[2]
    div = 0.5 * (up(flow_east) - down(flow_east)) + 0.5 * (right(flow_north) - left(flow_north))
    res = wet * (SIGMA_SHIFT * x - DIVERGENCE_COEF * div) - apply(x)
    step = res * (1.0 / CHEB_CENTER)
    keeps, gains = cheb_table(ITERS)
    for index in range(ITERS):
        x = x + step
        if index < ITERS - 1:
            res = res - apply(step)
            step = keeps[index] * step + gains[index] * res
    slope_east = (0.5 * (up(x) - down(x)))[24:32, :COLS]
    slope_north = (0.5 * (right(x) - left(x)))[24:32, :COLS]
    level[...] = x[24:32, :COLS]
    count = mine[3][:, :COLS]
    for lev in range(LEV):
        c = max(i for i in range(CHUNKS) if STARTS[i] <= lev)
        levels = SIZES[c]
        at = lev - STARTS[c]
        keep = count > lev
        for h in range(2):
            cols = slice(h * 128, (h + 1) * 128)
            parts = [states[c][f, h, pl.ds(at, ROWS, stride=levels), :] for f in range(3)]
            east[lev, :, cols] = jnp.where(keep[:, cols], parts[0] - slope_east[:, cols], 0.0)
            north[lev, :, cols] = jnp.where(keep[:, cols], parts[1] - slope_north[:, cols], 0.0)
            salt[lev, :, cols] = parts[2]


def swap(pairs):
    return [p for a, b in pairs for p in ((a, b), (b, a))]


def call(body, outs, scratch=(), ins=0, space=pltpu.VMEM, cost=None):
    vmem = pl.BlockSpec(memory_space=pltpu.VMEM)
    smem = pl.BlockSpec(memory_space=pltpu.SMEM)
    return pl.pallas_call(
        body,
        out_shape=[jax.ShapeDtypeStruct(s, F32) for s in outs],
        in_specs=[smem] + [pl.BlockSpec(memory_space=space)] * ins,
        out_specs=[vmem] * len(outs),
        scratch_shapes=[pltpu.VMEM(s, F32) if isinstance(s, tuple) else s for s in scratch],
        cost_estimate=cost and pl.CostEstimate(flops=cost, transcendentals=0, bytes_accessed=0),
        compiler_params=pltpu.CompilerParams(vmem_limit_bytes=16 * 1024 * 1024),
    )


def local(u, v, s, surface, depth, wet, active):
    gx = lax.axis_size("gx")
    gy = lax.axis_size("gy")
    me = lax.axis_index("gx")
    scalars = jnp.stack([me, me % 2, lax.axis_index("gy") % 2]).astype(jnp.int32)
    on_chip = swap([(i, i + 1) for i in range(0, gx, 2)])
    next_chip = swap([(i, i + 1) for i in range(1, gx - 1, 2)])
    far_chip = swap([(i, i + 3) for i in range(1, gx - 3, 2)])
    even = swap([(i, i + 1) for i in range(0, gy, 2)])
    odd = swap([(i, i + 1) for i in range(1, gy - 1, 2)])

    def both(first, second):
        return [(i * gy + j, k * gy + l) for i, k in first for j, l in second]

    edge_a, edge_b, corner_a, corner_b, *packed = call(
        pack_kernel,
        [(EDGE_TILES * LEV + 8, 128)] * 2
        + [(CORNER_TILES * LEV + 8, 128)] * 2
        + [(6 * HALO * levels + (0 if c else 16), 128) for c, levels in enumerate(SIZES)]
        + [(6 * ROWS * LEV + 16, 128), (3, ROWS, COLS)],
        [pltpu.VMEM((ROWS, COLS), jnp.int32)] * 2
        + [(ROWS, COLS)] * 2
        + [(LEV, ROWS, COLS)] * 3
        + [pltpu.SemaphoreType.DMA((7,))],
        ins=7,
        space=pltpu.HBM,
    )(scalars, *(pltpu.with_memory_space_constraint(x, pltpu.HBM) for x in (u, v, s, wet, active, surface, depth)))
    mains = packed[:CHUNKS]
    st, plane = packed[CHUNKS:]
    stp = lax.ppermute(st, "gx", on_chip)
    edge_a = lax.ppermute(edge_a, "gy", even)
    edge_b = lax.ppermute(edge_b, "gy", odd)
    corner_a = lax.ppermute(corner_a, ("gx", "gy"), both(next_chip, even))
    corner_b = lax.ppermute(corner_b, ("gx", "gy"), both(next_chip, odd))
    edge_a, edge_b, corner_a, corner_b, stp, *mains = lax.optimization_barrier((edge_a, edge_b, corner_a, corner_b, stp, *mains))
    main = [lax.ppermute(m, "gx", next_chip) for m in mains]
    edgep_a = lax.ppermute(edge_a, "gx", on_chip)
    edgep_b = lax.ppermute(edge_b, "gx", on_chip)

    states = []
    tail = []
    for c, levels in enumerate(SIZES):
        *flows, out, carry, sums = call(
            functools.partial(rk_kernel, c),
            [(4, ROWS, WIDE)] * (c == CHUNKS - 1)
            + [(3, 2, ROWS * levels, 128), (72, WIDE), (2, ROWS, 8, WIDE)],
            [(3, 24, levels, WIDE), (3, 16, levels, WIDE), (3, 12, levels, WIDE)]
            + [(24, 8, WIDE), (3, ROWS, WIDE), (2, ROWS, WIDE)],
            ins=11 + len(tail),
        )(scalars, st, stp, edge_a, edge_b, edgep_a, edgep_b, main[c], main[0], corner_a, corner_b, plane, *tail)
        tail = [carry, sums]
        states.append(out)
    flows = flows[0]
    far = lax.ppermute(flows, "gx", far_chip)
    pair = lax.ppermute(flows, "gx", on_chip)
    remote = lax.ppermute(jnp.stack([flows, pair]), "gx", next_chip)
    remote, far = lax.optimization_barrier((remote, far))
    remote_pair = lax.ppermute(remote, "gx", on_chip)
    east, north, salt, level = call(
        solve_kernel,
        [(LEV, ROWS, COLS)] * 3 + [(ROWS, COLS)],
        [(4, 56, WIDE)],
        ins=5 + CHUNKS,
    )(scalars, flows, pair, remote, remote_pair, far, *states)
    return east, north, salt, level


def solution(mesh):
    cube = P(None, "gx", "gy")
    flat = P("gx", "gy")
    return jax.shard_map(
        local,
        mesh=mesh,
        in_specs=(cube, cube, cube, flat, flat, flat, flat),
        out_specs=(cube, cube, cube, flat),
        check_vma=False,
    )
```

```python
import jax
import jax.numpy as jnp
from jax import lax
from jax.experimental import pallas as pl
from jax.experimental.pallas import tpu as pltpu
from jax.sharding import PartitionSpec as P

ITERS = 16
TIME_STEP = 0.2
CORIOLIS = 0.3
PRESS_COEF = 0.05
VISCOSITY = 0.1
DIFFUSIVITY = 0.1
SIGMA_SHIFT = 0.25
CHEB_CENTER = 3.625
CHEB_HALF = 3.375
DIVERGENCE_COEF = 8.0

LEV = 48
ROWS = 8
COLS = 256
EXT = 128
WIDE = COLS + EXT
HALO = 6
SIZES = (48,)
CHUNKS = len(SIZES)
STARTS = tuple(sum(SIZES[:c]) for c in range(CHUNKS))
TILES = LEV // 8
SLOT = 25
SLOTS = 5
EDGE_TILES = -(-3 * ROWS // SLOTS)
CORNER_TILES = -(-3 * HALO // SLOTS)
F32 = jnp.float32


def cheb_table(count):
    first = CHEB_CENTER / CHEB_HALF
    ratio = 1.0 / first
    keeps = []
    gains = []
    for index in range(count):
        ratio_next = 1.0 / (2.0 * first - ratio)
        keeps.append(ratio_next * ratio)
        gains.append(2.0 * ratio_next / CHEB_HALF)
        ratio = ratio_next
    return (keeps, gains)


def lanes(shape):
    return lax.broadcasted_iota(jnp.int32, shape, len(shape) - 1)


def place(low, high, units, slot):
    left, right = units
    lane = lanes(low.shape)
    here = (lane >= SLOT * slot) & (lane < SLOT * slot + SLOT)
    low = low if slot == 0 else pltpu.roll(low, SLOT * slot, 1)
    high = pltpu.roll(high, SLOT * slot + SLOT, 1)
    return jnp.where(here, low, left), jnp.where(here, high, right)


def unpack(high, low, slot):
    lane = lanes(high.shape)
    high = high if slot == 0 else pltpu.roll(high, 128 - SLOT * slot, 1)
    low = pltpu.roll(low, 128 - SLOT - SLOT * slot, 1)
    return jnp.where(lane < SLOT, high, jnp.where(lane >= 128 - SLOT, low, 0.0))


def ordered(first, second, flag):
    odd = jnp.full(first.shape, flag, jnp.int32) == 1
    return jnp.where(odd, second, first), jnp.where(odd, first, second)


def pack_kernel(sc, u, v, s, wet, act, surf, depth, edge_a, edge_b, corner_a, corner_b, *rest):
    mains = rest[:CHUNKS]
    st, plane = rest[CHUNKS : CHUNKS + 2]
    buffers = rest[CHUNKS + 2 : CHUNKS + 9]
    sems = rest[CHUNKS + 9]
    core = sc[1]
    north_odd = sc[2]
    sources = (wet, act, surf, depth, u, v, s)
    copies = [pltpu.make_async_copy(a, b, sems.at[i]) for i, (a, b) in enumerate(zip(sources, buffers))]
    for copy in copies:
        copy.start()
    for copy in copies[:4]:
        copy.wait()
    wet, act, surf, depth, *cubes = buffers
    count = (act[...] * wet[...]).astype(F32)
    plane[0] = surf[...]
    plane[1] = count
    plane[2] = depth[...]
    for f in range(3):
        copies[4 + f].wait()
        for lev in range(LEV):
            tile = jnp.where(count > lev, cubes[f][lev], 0.0)
            spot = 8 * (lev % TILES) + lev // TILES
            for h in range(2):
                st[pl.ds((2 * f + h) * ROWS * LEV + spot, ROWS, stride=LEV), :] = tile[:, h * 128 : (h + 1) * 128]
    base = 2 * core
    for c in range(CHUNKS):
        levels = SIZES[c]
        for f in range(3):
            for j in range(HALO):
                for h in range(2):
                    start = pl.multiple_of(((2 * f + h) * ROWS + base + j) * LEV + STARTS[c], 8)
                    at = ((2 * f + h) * HALO + j) * levels
                    mains[c][at : at + levels, :] = st[pl.ds(start, levels), :]
    for h in range(2):
        at = 6 * HALO * SIZES[0] + 8 * h
        mains[0][at : at + 8, :] = count[:, 128 * h : 128 * h + 128]
        at = 6 * ROWS * LEV + 8 * h
        st[at : at + 8, :] = count[:, 128 * h : 128 * h + 128]
    blank = jnp.zeros((LEV, 128), F32)
    for tiles, rows, first, a, b in (
        (EDGE_TILES, ROWS, 0, edge_a, edge_b),
        (CORNER_TILES, HALO, base, corner_a, corner_b),
    ):
        for g in range(tiles):
            units = (blank, blank)
            for slot in range(min(SLOTS, 3 * rows - SLOTS * g)):
                f, r = divmod(SLOTS * g + slot, rows)
                low = pl.multiple_of((2 * f * ROWS + first + r) * LEV, 8)
                high = pl.multiple_of(((2 * f + 1) * ROWS + first + r) * LEV, 8)
                units = place(st[pl.ds(low, LEV), :], st[pl.ds(high, LEV), :], units, slot)
            b[g * LEV : g * LEV + LEV, :], a[g * LEV : g * LEV + LEV, :] = ordered(*units, north_odd)
    units = (blank[:ROWS], blank[:ROWS])
    for slot, field in enumerate((surf[...], count, depth[...])):
        units = place(field[:, :128], field[:, 128:], units, slot)
    left, right = ordered(*units, north_odd)
    for tiles, a, b in ((EDGE_TILES, edge_a, edge_b), (CORNER_TILES, corner_a, corner_b)):
        b[tiles * LEV :, :] = left
        a[tiles * LEV :, :] = right


def shifts(q):
    return (
        pltpu.roll(q, WIDE - 1, 1),
        pltpu.roll(q, 1, 1),
        pltpu.roll(q, WIDE - 2, 1),
        pltpu.roll(q, 2, 1),
    )


def before(x, sub):
    total = x
    for step in (1, 2, 4):
        total = total + jnp.where(sub >= step, pltpu.roll(total, step, 0), 0.0)
    return total - x


def rk_kernel(sc, st, stp, edge_a, edge_b, edgep_a, edgep_b, *rest):
    mains = rest[:CHUNKS]
    corner_a, corner_b, plane, flows, east, north, salt, ext, one, two, counts, flat, remote, runs = rest[CHUNKS:]
    core = sc[1]
    north_odd = sc[2]
    beside = 16 * (1 - core)
    beyond = 2 + 14 * core
    for source, first in ((st, ROWS), (stp, beside)):
        for f in range(3):
            for r in range(ROWS):
                for h in range(2):
                    at = ((2 * f + h) * ROWS + r) * LEV
                    ext[f, first + r, :, h * 128 : (h + 1) * 128] = source[at : at + LEV, :]
    for f in range(3):
        for j in range(HALO):
            for h in range(2):
                for main, levels, lev0 in zip(mains, SIZES, STARTS):
                    at = ((2 * f + h) * HALO + j) * levels
                    ext[f, beyond + j, lev0 : lev0 + levels, h * 128 : (h + 1) * 128] = main[at : at + levels, :]
    for tiles, rows, first, a, b in (
        (EDGE_TILES, ROWS, ROWS, edge_a, edge_b),
        (EDGE_TILES, ROWS, beside, edgep_a, edgep_b),
        (CORNER_TILES, HALO, beyond, corner_a, corner_b),
    ):
        for g in range(tiles):
            here = slice(g * LEV, g * LEV + LEV)
            high, low = ordered(a[here, :], b[here, :], north_odd)
            for slot in range(min(SLOTS, 3 * rows - SLOTS * g)):
                f, r = divmod(SLOTS * g + slot, rows)
                ext[f, first + r, :, COLS:] = unpack(high, low, slot)

    def beyond_plane(tiles, a, b, slot):
        high, low = ordered(a[tiles * LEV :, :], b[tiles * LEV :, :], north_odd)
        return unpack(high, low, slot)

    for f in range(3):
        flat[f, :, :COLS] = plane[f]
        flat[f, :, COLS:] = beyond_plane(EDGE_TILES, edge_a, edge_b, f)
    remote[0, :, COLS:] = beyond_plane(EDGE_TILES, edgep_a, edgep_b, 1)
    remote[1, :, COLS:] = beyond_plane(CORNER_TILES, corner_a, corner_b, 1)
    for h in range(2):
        at = 6 * ROWS * LEV + 8 * h
        remote[0, :, h * 128 : (h + 1) * 128] = stp[at : at + 8, :]
        at = 6 * HALO * SIZES[0] + 8 * h
        remote[1, :, h * 128 : (h + 1) * 128] = mains[0][at : at + 8, :]
    for r in range(ROWS):
        counts[ROWS + r] = jnp.broadcast_to(flat[1, r : r + 1, :], (8, WIDE))
        counts[beside + r] = jnp.broadcast_to(remote[0, r : r + 1, :], (8, WIDE))
    for j in range(HALO):
        counts[beyond + j] = jnp.broadcast_to(remote[1, pl.ds(2 * (1 - core) + j, 1), :], (8, WIDE))

    sub = lax.broadcasted_iota(jnp.int32, (8, WIDE), 0)

    def stage(source, lead, rows, inset, weight, scale, write, base=None):
        press = PRESS_COEF * scale / 12.0

        def twelve(ahead, behind, ahead2, behind2):
            return 8.0 * (ahead - behind) - (ahead2 - behind2)

        def row(o, _):
            count = counts[o + inset]
            total_x = jnp.zeros((8, WIDE), F32)
            total_y = jnp.zeros((8, WIDE), F32)
            for t in range(TILES):
                here = slice(8 * t, 8 * t + 8)
                back2, back, q, fore, fore2 = [source[2, o + lead + k, here, :] for k in range(5)]
                right, left, right2, left2 = shifts(q)
                grad_x = twelve(fore, back, fore2, back2)
                grad_y = twelve(right, left, right2, left2)
                around = (fore + back) + (right + left)
                total_x = total_x + grad_x
                total_y = total_y + grad_y
                runs[0, here, :] = total_x
                runs[1, here, :] = total_y
                advect = (scale / 12.0) * (
                    source[0, o + lead + 2, here, :] * grad_x + source[1, o + lead + 2, here, :] * grad_y
                )
                value = (weight - 4.0 * VISCOSITY * scale) * q + (VISCOSITY * scale * around - advect)
                if base:
                    value = value + base * ext[2, o + inset, here, :]
                keep = count > (TILES * sub + t).astype(F32)
                write(o, t, 2, jnp.where(keep, value, 0.0))
            above_x = before(total_x, sub)
            above_y = before(total_y, sub)
            for t in range(TILES):
                here = slice(8 * t, 8 * t + 8)
                u = source[0, o + lead + 2, here, :]
                v = source[1, o + lead + 2, here, :]
                us = (scale / 12.0) * u
                vs = (scale / 12.0) * v
                keep = count > (TILES * sub + t).astype(F32)
                for f in range(2):
                    q = source[f, o + lead + 2, here, :]
                    back2, back = source[f, o + lead, here, :], source[f, o + lead + 1, here, :]
                    fore, fore2 = source[f, o + lead + 3, here, :], source[f, o + lead + 4, here, :]
                    right, left, right2, left2 = shifts(q)
                    advect = us * twelve(fore, back, fore2, back2) + vs * twelve(right, left, right2, left2)
                    around = (fore + back) + (right + left)
                    value = (weight - 4.0 * VISCOSITY * scale) * q + (VISCOSITY * scale * around - advect)
                    if f == 0:
                        value = value + (CORIOLIS * scale * v - press * (runs[0, here, :] + above_x))
                    if f == 1:
                        value = value - (CORIOLIS * scale * u + press * (runs[1, here, :] + above_y))
                    if base:
                        value = value + base * ext[f, o + inset, here, :]
                    write(o, t, f, jnp.where(keep, value, 0.0))
            return 0

        lax.fori_loop(0, rows, row, 0, unroll=4)

    def write1(o, t, f, value):
        one[f, o, 8 * t : 8 * t + 8, :] = value

    def write2(o, t, f, value):
        two[f, o, 8 * t : 8 * t + 8, :] = value

    partial = {}

    def write3(o, t, f, value):
        out = (east, north, salt)[f]
        for h in range(2):
            out[h, pl.ds(ROWS * t + o, 8, stride=ROWS * TILES), :] = value[:, h * 128 : (h + 1) * 128]
        if f < 2:
            partial[f] = partial[f] + value if t else value
            if t == TILES - 1:
                flows[f, pl.ds(o, 1), :] = jnp.sum(partial[f], axis=0, keepdims=True)

    stage(ext, 2, 16, 4, 1.0, TIME_STEP, write1)
    stage(one, 0, 12, 6, 0.25, 0.25 * TIME_STEP, write2, 0.75)
    stage(two, 0, 8, 8, 2.0 / 3.0, 2.0 / 3.0 * TIME_STEP, write3, 1.0 / 3.0)
    for f in range(2):
        flows[f] = flat[2] * (flows[f] * (1.0 / LEV))
        flows[2 + f] = flat[f]


def solve_kernel(sc, mine, pair, remote, remote_pair, far, u, v, s, east, north, salt, level, wide, out_u, out_v, sems):
    core = sc[1]
    halves = [slice(128 * h, 128 * h + 128) for h in range(2)]
    copies = [pltpu.make_async_copy(s.at[h], salt.at[:, :, halves[h]], sems.at[h]) for h in range(2)]
    for copy in copies:
        copy.start()
    wide[:, 24:32, :] = mine[...]
    for slot, block in (
        (4 - 2 * core, pair[...]),
        (2 + 2 * core, remote[0]),
        (1 + 4 * core, remote[1]),
        (5 - 4 * core, remote_pair[0]),
        (6 - 6 * core, remote_pair[1]),
        (6 * core, far[...]),
    ):
        wide[:, pl.ds(pl.multiple_of(8 * slot, 8), 8), :] = block
    high = 48
    near = slice(4, 52)
    own = slice(20, 28)

    def up(x):
        return pltpu.roll(x, high - 1, 0)

    def down(x):
        return pltpu.roll(x, 1, 0)

    def right(x):
        return pltpu.roll(x, WIDE - 1, 1)

    def left(x):
        return pltpu.roll(x, 1, 1)

    wet = jnp.where(wide[3, near, :] > 0.0, 1.0, 0.0)
    sixth = wet * (1.0 / 6.0)
    middle = wet * (SIGMA_SHIFT + 20.0 / 6.0) + (1.0 - wet)

    def less(res, e):
        w = wet * e
        rows = up(w) + down(w)
        mix = 4.0 * w + rows
        return (res - middle * e) + sixth * (4.0 * rows + (right(mix) + left(mix)))

    flow_east = wide[0, near, :]
    flow_north = wide[1, near, :]
    x = wide[2, near, :]
    div = 0.5 * (up(flow_east) - down(flow_east)) + 0.5 * (right(flow_north) - left(flow_north))
    res = less(wet * (SIGMA_SHIFT * x - DIVERGENCE_COEF * div), x)
    step = res * (1.0 / CHEB_CENTER)
    keeps, gains = cheb_table(ITERS)
    for index in range(ITERS):
        x = x + step
        if index < ITERS - 1:
            res = less(res, step)
            step = keeps[index] * step + gains[index] * res
    slope_east = (0.5 * (up(x) - down(x)))[own, :COLS]
    slope_north = (0.5 * (right(x) - left(x)))[own, :COLS]
    level[...] = x[own, :COLS]
    count = mine[3][:, :COLS]
    part = LEV // 4
    for first in range(0, LEV, part):
        for lev in range(first, first + part):
            keep = count > lev
            for h, cols in enumerate(halves):
                out_u[h, lev] = jnp.where(keep[:, cols], u[h, lev] - slope_east[:, cols], 0.0)
                out_v[h, lev] = jnp.where(keep[:, cols], v[h, lev] - slope_north[:, cols], 0.0)
        some = slice(first, first + part)
        for source, target in ((out_u, east), (out_v, north)):
            for h, cols in enumerate(halves):
                copy = pltpu.make_async_copy(source.at[h, some], target.at[some, :, cols], sems.at[len(copies)])
                copy.start()
                copies.append(copy)
    for copy in copies:
        copy.wait()


def swap(pairs):
    return [p for a, b in pairs for p in ((a, b), (b, a))]


def call(body, outs, scratch=(), ins=0, space=pltpu.VMEM, away=0):
    vmem = pl.BlockSpec(memory_space=pltpu.VMEM)
    smem = pl.BlockSpec(memory_space=pltpu.SMEM)
    return pl.pallas_call(
        body,
        out_shape=[jax.ShapeDtypeStruct(s, F32) for s in outs],
        in_specs=[smem] + [pl.BlockSpec(memory_space=space)] * ins,
        out_specs=[pl.BlockSpec(memory_space=pltpu.HBM)] * away + [vmem] * (len(outs) - away),
        scratch_shapes=[pltpu.VMEM(s, F32) if isinstance(s, tuple) else s for s in scratch],
        compiler_params=pltpu.CompilerParams(vmem_limit_bytes=16 * 1024 * 1024),
    )


def local(u, v, s, surface, depth, wet, active):
    gx = lax.axis_size("gx")
    gy = lax.axis_size("gy")
    me = lax.axis_index("gx")
    scalars = jnp.stack([me, me % 2, lax.axis_index("gy") % 2]).astype(jnp.int32)
    on_chip = swap([(i, i + 1) for i in range(0, gx, 2)])
    next_chip = swap([(i, i + 1) for i in range(1, gx - 1, 2)])
    far_chip = swap([(i, i + 3) for i in range(1, gx - 3, 2)])
    even = swap([(i, i + 1) for i in range(0, gy, 2)])
    odd = swap([(i, i + 1) for i in range(1, gy - 1, 2)])

    def both(first, second):
        return [(i * gy + j, k * gy + l) for i, k in first for j, l in second]

    edge_a, edge_b, corner_a, corner_b, *packed = call(
        pack_kernel,
        [(EDGE_TILES * LEV + 8, 128)] * 2
        + [(CORNER_TILES * LEV + 8, 128)] * 2
        + [(6 * HALO * levels + (0 if c else 16), 128) for c, levels in enumerate(SIZES)]
        + [(6 * ROWS * LEV + 16, 128), (3, ROWS, COLS)],
        [pltpu.VMEM((ROWS, COLS), jnp.int32)] * 2
        + [(ROWS, COLS)] * 2
        + [(LEV, ROWS, COLS)] * 3
        + [pltpu.SemaphoreType.DMA((7,))],
        ins=7,
        space=pltpu.HBM,
    )(scalars, *(pltpu.with_memory_space_constraint(x, pltpu.HBM) for x in (u, v, s, wet, active, surface, depth)))
    mains = packed[:CHUNKS]
    st, plane = packed[CHUNKS:]
    stp = lax.ppermute(st, "gx", on_chip)
    main = [lax.ppermute(mains[0], "gx", next_chip)]
    stp, corner_a, corner_b = lax.optimization_barrier((stp, corner_a, corner_b))
    edge_a = lax.ppermute(edge_a, "gy", even)
    edge_b = lax.ppermute(edge_b, "gy", odd)
    corner_a = lax.ppermute(corner_a, ("gx", "gy"), both(next_chip, even))
    corner_b = lax.ppermute(corner_b, ("gx", "gy"), both(next_chip, odd))
    edge_a, edge_b, corner_a, corner_b = lax.optimization_barrier((edge_a, edge_b, corner_a, corner_b))
    edgep_a = lax.ppermute(edge_a, "gx", on_chip)
    edgep_b = lax.ppermute(edge_b, "gx", on_chip)

    flows, *state = call(
        rk_kernel,
        [(4, ROWS, WIDE)] + [(2, ROWS * LEV, 128)] * 3,
        [(3, 24, LEV, WIDE), (3, 16, LEV, WIDE), (3, 12, LEV, WIDE)]
        + [(24, 8, WIDE), (3, ROWS, WIDE), (2, ROWS, WIDE), (2, LEV, WIDE)],
        ins=9 + CHUNKS,
    )(scalars, st, stp, edge_a, edge_b, edgep_a, edgep_b, *main, corner_a, corner_b, plane)
    far = lax.ppermute(flows, "gx", far_chip)
    pair = lax.ppermute(flows, "gx", on_chip)
    remote = lax.ppermute(jnp.stack([flows, pair]), "gx", next_chip)
    remote, far = lax.optimization_barrier((remote, far))
    remote_pair = lax.ppermute(remote, "gx", on_chip)
    state = [field.reshape(2, LEV, ROWS, 128) for field in state]
    east, north, salt, level = call(
        solve_kernel,
        [(LEV, ROWS, COLS)] * 3 + [(ROWS, COLS)],
        [(4, 56, WIDE)] + [(2, LEV, ROWS, 128)] * 2 + [pltpu.SemaphoreType.DMA((18,))],
        ins=8,
        away=3,
    )(scalars, flows, pair, remote, remote_pair, far, *state)
    return east, north, salt, level


def solution(mesh):
    cube = P(None, "gx", "gy")
    flat = P("gx", "gy")
    return jax.shard_map(
        local,
        mesh=mesh,
        in_specs=(cube, cube, cube, flat, flat, flat, flat),
        out_specs=(cube, cube, cube, flat),
        check_vma=False,
    )
```

```python
import jax
import jax.numpy as jnp
from jax import lax
from jax.experimental import pallas as pl
from jax.experimental.pallas import tpu as pltpu
from jax.sharding import PartitionSpec as P

ITERS = 16
TIME_STEP = 0.2
CORIOLIS = 0.3
PRESS_COEF = 0.05
VISCOSITY = 0.1
DIFFUSIVITY = 0.1
SIGMA_SHIFT = 0.25
CHEB_CENTER = 3.625
CHEB_HALF = 3.375
DIVERGENCE_COEF = 8.0

LEV = 48
ROWS = 8
COLS = 256
EXT = 128
WIDE = COLS + EXT
HALO = 6
SIZES = (48,)
CHUNKS = len(SIZES)
STARTS = tuple(sum(SIZES[:c]) for c in range(CHUNKS))
TILES = LEV // 8
SLOT = 25
SLOTS = 5
EDGE_TILES = -(-3 * ROWS // SLOTS)
CORNER_TILES = -(-3 * HALO // SLOTS)
F32 = jnp.float32


def cheb_table(count):
    first = CHEB_CENTER / CHEB_HALF
    ratio = 1.0 / first
    keeps = []
    gains = []
    for index in range(count):
        ratio_next = 1.0 / (2.0 * first - ratio)
        keeps.append(ratio_next * ratio)
        gains.append(2.0 * ratio_next / CHEB_HALF)
        ratio = ratio_next
    return (keeps, gains)


def lanes(shape):
    return lax.broadcasted_iota(jnp.int32, shape, len(shape) - 1)


def place(low, high, units, slot):
    left, right = units
    lane = lanes(low.shape)
    here = (lane >= SLOT * slot) & (lane < SLOT * slot + SLOT)
    low = low if slot == 0 else pltpu.roll(low, SLOT * slot, 1)
    high = pltpu.roll(high, SLOT * slot + SLOT, 1)
    return jnp.where(here, low, left), jnp.where(here, high, right)


def unpack(high, low, slot):
    lane = lanes(high.shape)
    high = high if slot == 0 else pltpu.roll(high, 128 - SLOT * slot, 1)
    low = pltpu.roll(low, 128 - SLOT - SLOT * slot, 1)
    return jnp.where(lane < SLOT, high, jnp.where(lane >= 128 - SLOT, low, 0.0))


def ordered(first, second, flag):
    odd = jnp.full(first.shape, flag, jnp.int32) == 1
    return jnp.where(odd, second, first), jnp.where(odd, first, second)


def pack_kernel(sc, u, v, s, wet, act, surf, depth, edge_a, edge_b, corner_a, corner_b, *rest):
    mains = rest[:CHUNKS]
    st, plane = rest[CHUNKS : CHUNKS + 2]
    buffers = rest[CHUNKS + 2 : CHUNKS + 9]
    sems = rest[CHUNKS + 9]
    core = sc[1]
    north_odd = sc[2]
    sources = (wet, act, surf, depth, u, v, s)
    copies = [pltpu.make_async_copy(a, b, sems.at[i]) for i, (a, b) in enumerate(zip(sources, buffers))]
    for copy in copies:
        copy.start()
    for copy in copies[:4]:
        copy.wait()
    wet, act, surf, depth, *cubes = buffers
    count = (act[...] * wet[...]).astype(F32)
    plane[0] = surf[...]
    plane[1] = count
    plane[2] = depth[...]
    for f in range(3):
        copies[4 + f].wait()
        for lev in range(LEV):
            tile = jnp.where(count > lev, cubes[f][lev], 0.0)
            spot = 8 * (lev % TILES) + lev // TILES
            for h in range(2):
                st[pl.ds((2 * f + h) * ROWS * LEV + spot, ROWS, stride=LEV), :] = tile[:, h * 128 : (h + 1) * 128]
    base = 2 * core
    for c in range(CHUNKS):
        levels = SIZES[c]
        for f in range(3):
            for j in range(HALO):
                for h in range(2):
                    start = pl.multiple_of(((2 * f + h) * ROWS + base + j) * LEV + STARTS[c], 8)
                    at = ((2 * f + h) * HALO + j) * levels
                    mains[c][at : at + levels, :] = st[pl.ds(start, levels), :]
    for h in range(2):
        at = 6 * HALO * SIZES[0] + 8 * h
        mains[0][at : at + 8, :] = count[:, 128 * h : 128 * h + 128]
        at = 6 * ROWS * LEV + 8 * h
        st[at : at + 8, :] = count[:, 128 * h : 128 * h + 128]
    blank = jnp.zeros((LEV, 128), F32)
    for tiles, rows, first, a, b in (
        (EDGE_TILES, ROWS, 0, edge_a, edge_b),
        (CORNER_TILES, HALO, base, corner_a, corner_b),
    ):
        for g in range(tiles):
            units = (blank, blank)
            for slot in range(min(SLOTS, 3 * rows - SLOTS * g)):
                f, r = divmod(SLOTS * g + slot, rows)
                low = pl.multiple_of((2 * f * ROWS + first + r) * LEV, 8)
                high = pl.multiple_of(((2 * f + 1) * ROWS + first + r) * LEV, 8)
                units = place(st[pl.ds(low, LEV), :], st[pl.ds(high, LEV), :], units, slot)
            b[g * LEV : g * LEV + LEV, :], a[g * LEV : g * LEV + LEV, :] = ordered(*units, north_odd)
    units = (blank[:ROWS], blank[:ROWS])
    for slot, field in enumerate((surf[...], count, depth[...])):
        units = place(field[:, :128], field[:, 128:], units, slot)
    left, right = ordered(*units, north_odd)
    for tiles, a, b in ((EDGE_TILES, edge_a, edge_b), (CORNER_TILES, corner_a, corner_b)):
        b[tiles * LEV :, :] = left
        a[tiles * LEV :, :] = right


def shifts(q):
    return (
        pltpu.roll(q, WIDE - 1, 1),
        pltpu.roll(q, 1, 1),
        pltpu.roll(q, WIDE - 2, 1),
        pltpu.roll(q, 2, 1),
    )


def before(x, sub):
    total = x
    for step in (1, 2, 4):
        total = total + jnp.where(sub >= step, pltpu.roll(total, step, 0), 0.0)
    return total - x


def columns_beyond(ext, tiles, rows, first, a, b, north_odd):
    for g in range(tiles):
        here = slice(g * LEV, g * LEV + LEV)
        high, low = ordered(a[here, :], b[here, :], north_odd)
        for slot in range(min(SLOTS, 3 * rows - SLOTS * g)):
            f, r = divmod(SLOTS * g + slot, rows)
            ext[f, first + r, :, COLS:] = unpack(high, low, slot)


def plane_beyond(tiles, a, b, slot, north_odd):
    high, low = ordered(a[tiles * LEV :, :], b[tiles * LEV :, :], north_odd)
    return unpack(high, low, slot)


def early_kernel(sc, st, stp, edge_a, edge_b, edgep_a, edgep_b, plane, *rest):
    arrays, runs, aside = rest[:-2], rest[-2], rest[-1]
    ext, one, two, counts, flows, flat, east, north, salt = arrays
    core = sc[1]
    north_odd = sc[2]
    beside = 16 * (1 - core)
    for source, first in ((st, ROWS), (stp, beside)):
        for f in range(3):
            for r in range(ROWS):
                for h in range(2):
                    at = ((2 * f + h) * ROWS + r) * LEV
                    ext[f, first + r, :, h * 128 : (h + 1) * 128] = source[at : at + LEV, :]
    columns_beyond(ext, EDGE_TILES, ROWS, ROWS, edge_a, edge_b, north_odd)
    columns_beyond(ext, EDGE_TILES, ROWS, beside, edgep_a, edgep_b, north_odd)
    for f in range(3):
        flat[f, :, :COLS] = plane[f]
        flat[f, :, COLS:] = plane_beyond(EDGE_TILES, edge_a, edge_b, f, north_odd)
    aside[:, COLS:] = plane_beyond(EDGE_TILES, edgep_a, edgep_b, 1, north_odd)
    for h in range(2):
        at = 6 * ROWS * LEV + 8 * h
        aside[:, h * 128 : (h + 1) * 128] = stp[at : at + 8, :]
    for r in range(ROWS):
        counts[ROWS + r] = jnp.broadcast_to(flat[1, r : r + 1, :], (8, WIDE))
        counts[beside + r] = jnp.broadcast_to(aside[r : r + 1, :], (8, WIDE))
    other = 1 - core
    stages(arrays, runs, ((6 * other, 10, 5), (6 * other, 6, 3), (6 * other, 2, 2)))
    for f in range(2):
        flows[2 + f] = flat[f]


def late_kernel(sc, *rest):
    mains = rest[:CHUNKS]
    corner_a, corner_b, _e, _o, _t, _c, _f, flat, _u, _v, _s = rest[CHUNKS : CHUNKS + 11]
    ext, one, two, counts, flows, east, north, salt, runs, aside = rest[CHUNKS + 11 :]
    core = sc[1]
    north_odd = sc[2]
    beyond = 2 + 14 * core
    for f in range(3):
        for j in range(HALO):
            for h in range(2):
                for main, levels, lev0 in zip(mains, SIZES, STARTS):
                    at = ((2 * f + h) * HALO + j) * levels
                    ext[f, beyond + j, lev0 : lev0 + levels, h * 128 : (h + 1) * 128] = main[at : at + levels, :]
    columns_beyond(ext, CORNER_TILES, HALO, beyond, corner_a, corner_b, north_odd)
    aside[:, COLS:] = plane_beyond(CORNER_TILES, corner_a, corner_b, 1, north_odd)
    for h in range(2):
        at = 6 * HALO * SIZES[0] + 8 * h
        aside[:, h * 128 : (h + 1) * 128] = mains[0][at : at + 8, :]
    for j in range(HALO):
        counts[beyond + j] = jnp.broadcast_to(aside[pl.ds(2 * (1 - core) + j, 1), :], (8, WIDE))
    stages((ext, one, two, counts, flows, flat, east, north, salt), runs, ((10 * core, 6, 3), (6 * core, 6, 3), (2 * core, 6, 3)))
    for f in range(2):
        flows[f] = flat[2] * (flows[f] * (1.0 / LEV))


def stages(arrays, runs, spans):
    ext, one, two, counts, flows, _flat, east, north, salt = arrays
    sub = lax.broadcasted_iota(jnp.int32, (8, WIDE), 0)

    def stage(span, source, lead, inset, weight, scale, write, base=None):
        press = PRESS_COEF * scale / 12.0

        def twelve(ahead, behind, ahead2, behind2):
            return 8.0 * (ahead - behind) - (ahead2 - behind2)

        start, rows, together = span

        def row(index, _):
            o = start + index
            count = counts[o + inset]
            total_x = jnp.zeros((8, WIDE), F32)
            total_y = jnp.zeros((8, WIDE), F32)
            for t in range(TILES):
                here = slice(8 * t, 8 * t + 8)
                back2, back, q, fore, fore2 = [source[2, o + lead + k, here, :] for k in range(5)]
                right, left, right2, left2 = shifts(q)
                grad_x = twelve(fore, back, fore2, back2)
                grad_y = twelve(right, left, right2, left2)
                around = (fore + back) + (right + left)
                total_x = total_x + grad_x
                total_y = total_y + grad_y
                runs[0, here, :] = total_x
                runs[1, here, :] = total_y
                advect = (scale / 12.0) * (
                    source[0, o + lead + 2, here, :] * grad_x + source[1, o + lead + 2, here, :] * grad_y
                )
                value = (weight - 4.0 * VISCOSITY * scale) * q + (VISCOSITY * scale * around - advect)
                if base:
                    value = value + base * ext[2, o + inset, here, :]
                keep = count > (TILES * sub + t).astype(F32)
                write(o, t, 2, jnp.where(keep, value, 0.0))
            above_x = before(total_x, sub)
            above_y = before(total_y, sub)
            for t in range(TILES):
                here = slice(8 * t, 8 * t + 8)
                u = source[0, o + lead + 2, here, :]
                v = source[1, o + lead + 2, here, :]
                us = (scale / 12.0) * u
                vs = (scale / 12.0) * v
                keep = count > (TILES * sub + t).astype(F32)
                for f in range(2):
                    q = source[f, o + lead + 2, here, :]
                    back2, back = source[f, o + lead, here, :], source[f, o + lead + 1, here, :]
                    fore, fore2 = source[f, o + lead + 3, here, :], source[f, o + lead + 4, here, :]
                    right, left, right2, left2 = shifts(q)
                    advect = us * twelve(fore, back, fore2, back2) + vs * twelve(right, left, right2, left2)
                    around = (fore + back) + (right + left)
                    value = (weight - 4.0 * VISCOSITY * scale) * q + (VISCOSITY * scale * around - advect)
                    if f == 0:
                        value = value + (CORIOLIS * scale * v - press * (runs[0, here, :] + above_x))
                    if f == 1:
                        value = value - (CORIOLIS * scale * u + press * (runs[1, here, :] + above_y))
                    if base:
                        value = value + base * ext[f, o + inset, here, :]
                    write(o, t, f, jnp.where(keep, value, 0.0))
            return 0

        lax.fori_loop(0, rows, row, 0, unroll=together)

    def write1(o, t, f, value):
        one[f, o, 8 * t : 8 * t + 8, :] = value

    def write2(o, t, f, value):
        two[f, o, 8 * t : 8 * t + 8, :] = value

    partial = {}

    def write3(o, t, f, value):
        out = (east, north, salt)[f]
        for h in range(2):
            out[h, pl.ds(ROWS * t + o, 8, stride=ROWS * TILES), :] = value[:, h * 128 : (h + 1) * 128]
        if f < 2:
            partial[f] = partial[f] + value if t else value
            if t == TILES - 1:
                flows[f, pl.ds(o, 1), :] = jnp.sum(partial[f], axis=0, keepdims=True)

    stage(spans[0], ext, 2, 4, 1.0, TIME_STEP, write1)
    stage(spans[1], one, 0, 6, 0.25, 0.25 * TIME_STEP, write2, 0.75)
    stage(spans[2], two, 0, 8, 2.0 / 3.0, 2.0 / 3.0 * TIME_STEP, write3, 1.0 / 3.0)


def solve_kernel(sc, mine, pair, remote, remote_pair, far, u, v, s, east, north, salt, level, wide, out_u, out_v, sems):
    core = sc[1]
    halves = [slice(128 * h, 128 * h + 128) for h in range(2)]
    copies = [pltpu.make_async_copy(s.at[h], salt.at[:, :, halves[h]], sems.at[h]) for h in range(2)]
    for copy in copies:
        copy.start()
    wide[:, 24:32, :] = mine[...]
    for slot, block in (
        (4 - 2 * core, pair[...]),
        (2 + 2 * core, remote[0]),
        (1 + 4 * core, remote[1]),
        (5 - 4 * core, remote_pair[0]),
        (6 - 6 * core, remote_pair[1]),
        (6 * core, far[...]),
    ):
        wide[:, pl.ds(pl.multiple_of(8 * slot, 8), 8), :] = block
    high = 48
    near = slice(4, 52)
    own = slice(20, 28)

    def up(x):
        return pltpu.roll(x, high - 1, 0)

    def down(x):
        return pltpu.roll(x, 1, 0)

    def right(x):
        return pltpu.roll(x, WIDE - 1, 1)

    def left(x):
        return pltpu.roll(x, 1, 1)

    wet = jnp.where(wide[3, near, :] > 0.0, 1.0, 0.0)
    sixth = wet * (1.0 / 6.0)
    middle = wet * (SIGMA_SHIFT + 20.0 / 6.0) + (1.0 - wet)

    def less(res, e):
        w = wet * e
        rows = up(w) + down(w)
        mix = 4.0 * w + rows
        return (res - middle * e) + sixth * (4.0 * rows + (right(mix) + left(mix)))

    flow_east = wide[0, near, :]
    flow_north = wide[1, near, :]
    x = wide[2, near, :]
    div = 0.5 * (up(flow_east) - down(flow_east)) + 0.5 * (right(flow_north) - left(flow_north))
    res = less(wet * (SIGMA_SHIFT * x - DIVERGENCE_COEF * div), x)
    step = res * (1.0 / CHEB_CENTER)
    keeps, gains = cheb_table(ITERS)
    for index in range(ITERS):
        x = x + step
        if index < ITERS - 1:
            res = less(res, step)
            step = keeps[index] * step + gains[index] * res
    slope_east = (0.5 * (up(x) - down(x)))[own, :COLS]
    slope_north = (0.5 * (right(x) - left(x)))[own, :COLS]
    level[...] = x[own, :COLS]
    count = mine[3][:, :COLS]
    part = LEV // 4
    for first in range(0, LEV, part):
        for lev in range(first, first + part):
            keep = count > lev
            for h, cols in enumerate(halves):
                out_u[h, lev] = jnp.where(keep[:, cols], u[h, lev] - slope_east[:, cols], 0.0)
                out_v[h, lev] = jnp.where(keep[:, cols], v[h, lev] - slope_north[:, cols], 0.0)
        some = slice(first, first + part)
        for source, target in ((out_u, east), (out_v, north)):
            for h, cols in enumerate(halves):
                copy = pltpu.make_async_copy(source.at[h, some], target.at[some, :, cols], sems.at[len(copies)])
                copy.start()
                copies.append(copy)
    for copy in copies:
        copy.wait()


def swap(pairs):
    return [p for a, b in pairs for p in ((a, b), (b, a))]


def call(body, outs, scratch=(), ins=0, space=pltpu.VMEM, away=0, aliases={}):
    vmem = pl.BlockSpec(memory_space=pltpu.VMEM)
    smem = pl.BlockSpec(memory_space=pltpu.SMEM)
    return pl.pallas_call(
        body,
        out_shape=[jax.ShapeDtypeStruct(s, F32) for s in outs],
        in_specs=[smem] + [pl.BlockSpec(memory_space=space)] * ins,
        out_specs=[pl.BlockSpec(memory_space=pltpu.HBM)] * away + [vmem] * (len(outs) - away),
        scratch_shapes=[pltpu.VMEM(s, F32) if isinstance(s, tuple) else s for s in scratch],
        input_output_aliases=aliases,
        compiler_params=pltpu.CompilerParams(vmem_limit_bytes=16 * 1024 * 1024),
    )


def local(u, v, s, surface, depth, wet, active):
    gx = lax.axis_size("gx")
    gy = lax.axis_size("gy")
    me = lax.axis_index("gx")
    scalars = jnp.stack([me, me % 2, lax.axis_index("gy") % 2]).astype(jnp.int32)
    on_chip = swap([(i, i + 1) for i in range(0, gx, 2)])
    next_chip = swap([(i, i + 1) for i in range(1, gx - 1, 2)])
    far_chip = swap([(i, i + 3) for i in range(1, gx - 3, 2)])
    even = swap([(i, i + 1) for i in range(0, gy, 2)])
    odd = swap([(i, i + 1) for i in range(1, gy - 1, 2)])

    def both(first, second):
        return [(i * gy + j, k * gy + l) for i, k in first for j, l in second]

    edge_a, edge_b, corner_a, corner_b, *packed = call(
        pack_kernel,
        [(EDGE_TILES * LEV + 8, 128)] * 2
        + [(CORNER_TILES * LEV + 8, 128)] * 2
        + [(6 * HALO * levels + (0 if c else 16), 128) for c, levels in enumerate(SIZES)]
        + [(6 * ROWS * LEV + 16, 128), (3, ROWS, COLS)],
        [pltpu.VMEM((ROWS, COLS), jnp.int32)] * 2
        + [(ROWS, COLS)] * 2
        + [(LEV, ROWS, COLS)] * 3
        + [pltpu.SemaphoreType.DMA((7,))],
        ins=7,
        space=pltpu.HBM,
    )(scalars, *(pltpu.with_memory_space_constraint(x, pltpu.HBM) for x in (u, v, s, wet, active, surface, depth)))
    mains = packed[:CHUNKS]
    st, plane = packed[CHUNKS:]
    stp = lax.ppermute(st, "gx", on_chip)
    edge_a = lax.ppermute(edge_a, "gy", even)
    edge_b = lax.ppermute(edge_b, "gy", odd)
    edge_a, edge_b, stp, corner_a, corner_b, *mains = lax.optimization_barrier(
        (edge_a, edge_b, stp, corner_a, corner_b, *mains)
    )
    main = [lax.ppermute(m, "gx", next_chip) for m in mains]
    corner_a = lax.ppermute(corner_a, ("gx", "gy"), both(next_chip, even))
    corner_b = lax.ppermute(corner_b, ("gx", "gy"), both(next_chip, odd))
    edgep_a = lax.ppermute(edge_a, "gx", on_chip)
    edgep_b = lax.ppermute(edge_b, "gx", on_chip)

    field = (2, ROWS * LEV, 128)
    shapes = [(3, 24, LEV, WIDE), (3, 16, LEV, WIDE), (3, 12, LEV, WIDE), (24, 8, WIDE), (4, ROWS, WIDE)]
    *shared, flat, u, v, s = call(
        early_kernel,
        shapes + [(3, ROWS, WIDE)] + [field] * 3,
        [(2, LEV, WIDE), (ROWS, WIDE)],
        ins=7,
    )(scalars, st, stp, edge_a, edge_b, edgep_a, edgep_b, plane)
    shift = 1 + CHUNKS + 2
    *_, flows, u, v, s = call(
        late_kernel,
        shapes + [field] * 3,
        [(2, LEV, WIDE), (ROWS, WIDE)],
        ins=CHUNKS + 11,
        aliases={shift + i: i for i in range(5)} | {shift + 6 + i: 5 + i for i in range(3)},
    )(scalars, *main, corner_a, corner_b, *shared, flat, u, v, s)
    state = [u, v, s]
    far = lax.ppermute(flows, "gx", far_chip)
    pair = lax.ppermute(flows, "gx", on_chip)
    remote = lax.ppermute(jnp.stack([flows, pair]), "gx", next_chip)
    remote, far = lax.optimization_barrier((remote, far))
    remote_pair = lax.ppermute(remote, "gx", on_chip)
    state = [field.reshape(2, LEV, ROWS, 128) for field in state]
    east, north, salt, level = call(
        solve_kernel,
        [(LEV, ROWS, COLS)] * 3 + [(ROWS, COLS)],
        [(4, 56, WIDE)] + [(2, LEV, ROWS, 128)] * 2 + [pltpu.SemaphoreType.DMA((18,))],
        ins=8,
        away=3,
    )(scalars, flows, pair, remote, remote_pair, far, *state)
    return east, north, salt, level


def solution(mesh):
    cube = P(None, "gx", "gy")
    flat = P("gx", "gy")
    return jax.shard_map(
        local,
        mesh=mesh,
        in_specs=(cube, cube, cube, flat, flat, flat, flat),
        out_specs=(cube, cube, cube, flat),
        check_vma=False,
    )
```

```python
import jax
import jax.numpy as jnp
from jax import lax
from jax.experimental import pallas as pl
from jax.experimental.pallas import tpu as pltpu
from jax.sharding import PartitionSpec as P

ITERS = 16
TIME_STEP = 0.2
CORIOLIS = 0.3
PRESS_COEF = 0.05
VISCOSITY = 0.1
DIFFUSIVITY = 0.1
SIGMA_SHIFT = 0.25
CHEB_CENTER = 3.625
CHEB_HALF = 3.375
DIVERGENCE_COEF = 8.0

LEV = 48
ROWS = 8
COLS = 256
EXT = 128
EARLY_COST = 7_500_000_000
WIDE = COLS + EXT
HALO = 6
SIZES = (48,)
CHUNKS = len(SIZES)
STARTS = tuple(sum(SIZES[:c]) for c in range(CHUNKS))
TILES = LEV // 8
SLOT = 25
SLOTS = 5
EDGE_TILES = -(-3 * ROWS // SLOTS)
CORNER_TILES = -(-3 * HALO // SLOTS)
F32 = jnp.float32


def cheb_table(count):
    first = CHEB_CENTER / CHEB_HALF
    ratio = 1.0 / first
    keeps = []
    gains = []
    for index in range(count):
        ratio_next = 1.0 / (2.0 * first - ratio)
        keeps.append(ratio_next * ratio)
        gains.append(2.0 * ratio_next / CHEB_HALF)
        ratio = ratio_next
    return (keeps, gains)


def lanes(shape):
    return lax.broadcasted_iota(jnp.int32, shape, len(shape) - 1)


def place(low, high, units, slot):
    left, right = units
    lane = lanes(low.shape)
    here = (lane >= SLOT * slot) & (lane < SLOT * slot + SLOT)
    low = low if slot == 0 else pltpu.roll(low, SLOT * slot, 1)
    high = pltpu.roll(high, SLOT * slot + SLOT, 1)
    return jnp.where(here, low, left), jnp.where(here, high, right)


def unpack(high, low, slot):
    lane = lanes(high.shape)
    high = high if slot == 0 else pltpu.roll(high, 128 - SLOT * slot, 1)
    low = pltpu.roll(low, 128 - SLOT - SLOT * slot, 1)
    return jnp.where(lane < SLOT, high, jnp.where(lane >= 128 - SLOT, low, 0.0))


def ordered(first, second, flag):
    odd = jnp.full(first.shape, flag, jnp.int32) == 1
    return jnp.where(odd, second, first), jnp.where(odd, first, second)


def pack_kernel(sc, u, v, s, wet, act, surf, depth, edge_a, edge_b, corner_a, corner_b, *rest):
    mains = rest[:CHUNKS]
    st, plane = rest[CHUNKS : CHUNKS + 2]
    buffers = rest[CHUNKS + 2 : CHUNKS + 9]
    sems = rest[CHUNKS + 9]
    core = sc[1]
    north_odd = sc[2]
    sources = (wet, act, surf, depth, u, v, s)
    copies = [pltpu.make_async_copy(a, b, sems.at[i]) for i, (a, b) in enumerate(zip(sources, buffers))]
    for copy in copies:
        copy.start()
    for copy in copies[:4]:
        copy.wait()
    wet, act, surf, depth, *cubes = buffers
    count = (act[...] * wet[...]).astype(F32)
    plane[0] = surf[...]
    plane[1] = count
    plane[2] = depth[...]
    for f in range(3):
        copies[4 + f].wait()
        for lev in range(LEV):
            tile = jnp.where(count > lev, cubes[f][lev], 0.0)
            spot = 8 * (lev % TILES) + lev // TILES
            for h in range(2):
                st[pl.ds((2 * f + h) * ROWS * LEV + spot, ROWS, stride=LEV), :] = tile[:, h * 128 : (h + 1) * 128]
    base = 2 * core
    for c in range(CHUNKS):
        levels = SIZES[c]
        for f in range(3):
            for j in range(HALO):
                for h in range(2):
                    start = pl.multiple_of(((2 * f + h) * ROWS + base + j) * LEV + STARTS[c], 8)
                    at = ((2 * f + h) * HALO + j) * levels
                    mains[c][at : at + levels, :] = st[pl.ds(start, levels), :]
    for h in range(2):
        at = 6 * HALO * SIZES[0] + 8 * h
        mains[0][at : at + 8, :] = count[:, 128 * h : 128 * h + 128]
        at = 6 * ROWS * LEV + 8 * h
        st[at : at + 8, :] = count[:, 128 * h : 128 * h + 128]
    blank = jnp.zeros((LEV, 128), F32)
    for tiles, rows, first, a, b in (
        (EDGE_TILES, ROWS, 0, edge_a, edge_b),
        (CORNER_TILES, HALO, base, corner_a, corner_b),
    ):
        for g in range(tiles):
            units = (blank, blank)
            for slot in range(min(SLOTS, 3 * rows - SLOTS * g)):
                f, r = divmod(SLOTS * g + slot, rows)
                low = pl.multiple_of((2 * f * ROWS + first + r) * LEV, 8)
                high = pl.multiple_of(((2 * f + 1) * ROWS + first + r) * LEV, 8)
                units = place(st[pl.ds(low, LEV), :], st[pl.ds(high, LEV), :], units, slot)
            b[g * LEV : g * LEV + LEV, :], a[g * LEV : g * LEV + LEV, :] = ordered(*units, north_odd)
    units = (blank[:ROWS], blank[:ROWS])
    for slot, field in enumerate((surf[...], count, depth[...])):
        units = place(field[:, :128], field[:, 128:], units, slot)
    left, right = ordered(*units, north_odd)
    for tiles, a, b in ((EDGE_TILES, edge_a, edge_b), (CORNER_TILES, corner_a, corner_b)):
        b[tiles * LEV :, :] = left
        a[tiles * LEV :, :] = right


def shifts(q):
    return (
        pltpu.roll(q, WIDE - 1, 1),
        pltpu.roll(q, 1, 1),
        pltpu.roll(q, WIDE - 2, 1),
        pltpu.roll(q, 2, 1),
    )


def before(x, sub):
    total = x
    for step in (1, 2, 4):
        total = total + jnp.where(sub >= step, pltpu.roll(total, step, 0), 0.0)
    return total - x


def columns_beyond(ext, tiles, rows, first, a, b, north_odd):
    for g in range(tiles):
        here = slice(g * LEV, g * LEV + LEV)
        high, low = ordered(a[here, :], b[here, :], north_odd)
        for slot in range(min(SLOTS, 3 * rows - SLOTS * g)):
            f, r = divmod(SLOTS * g + slot, rows)
            ext[f, first + r, :, COLS:] = unpack(high, low, slot)


def plane_beyond(tiles, a, b, slot, north_odd):
    high, low = ordered(a[tiles * LEV :, :], b[tiles * LEV :, :], north_odd)
    return unpack(high, low, slot)


def early_kernel(sc, st, stp, edge_a, edge_b, edgep_a, edgep_b, plane, *rest):
    arrays, runs, aside = rest[:-2], rest[-2], rest[-1]
    ext, one, two, counts, flows, flat, east, north, salt = arrays
    core = sc[1]
    north_odd = sc[2]
    beside = 16 * (1 - core)
    for source, first in ((st, ROWS), (stp, beside)):
        for f in range(3):
            for r in range(ROWS):
                for h in range(2):
                    at = ((2 * f + h) * ROWS + r) * LEV
                    ext[f, first + r, :, h * 128 : (h + 1) * 128] = source[at : at + LEV, :]
    columns_beyond(ext, EDGE_TILES, ROWS, ROWS, edge_a, edge_b, north_odd)
    columns_beyond(ext, EDGE_TILES, ROWS, beside, edgep_a, edgep_b, north_odd)
    for f in range(3):
        flat[f, :, :COLS] = plane[f]
        flat[f, :, COLS:] = plane_beyond(EDGE_TILES, edge_a, edge_b, f, north_odd)
    aside[:, COLS:] = plane_beyond(EDGE_TILES, edgep_a, edgep_b, 1, north_odd)
    for h in range(2):
        at = 6 * ROWS * LEV + 8 * h
        aside[:, h * 128 : (h + 1) * 128] = stp[at : at + 8, :]
    for r in range(ROWS):
        counts[ROWS + r] = jnp.broadcast_to(flat[1, r : r + 1, :], (8, WIDE))
        counts[beside + r] = jnp.broadcast_to(aside[r : r + 1, :], (8, WIDE))
    other = 1 - core
    stages(arrays, runs, ((6 * other, 10, 5), (6 * other, 6, 3), (6 * other, 2, 2)))
    for f in range(2):
        flows[2 + f] = flat[f]


def late_kernel(sc, *rest):
    mains = rest[:CHUNKS]
    corner_a, corner_b, _e, _o, _t, _c, _f, flat, _u, _v, _s = rest[CHUNKS : CHUNKS + 11]
    ext, one, two, counts, flows, east, north, salt, runs, aside = rest[CHUNKS + 11 :]
    core = sc[1]
    north_odd = sc[2]
    beyond = 2 + 14 * core
    for f in range(3):
        for j in range(HALO):
            for h in range(2):
                for main, levels, lev0 in zip(mains, SIZES, STARTS):
                    at = ((2 * f + h) * HALO + j) * levels
                    ext[f, beyond + j, lev0 : lev0 + levels, h * 128 : (h + 1) * 128] = main[at : at + levels, :]
    columns_beyond(ext, CORNER_TILES, HALO, beyond, corner_a, corner_b, north_odd)
    aside[:, COLS:] = plane_beyond(CORNER_TILES, corner_a, corner_b, 1, north_odd)
    for h in range(2):
        at = 6 * HALO * SIZES[0] + 8 * h
        aside[:, h * 128 : (h + 1) * 128] = mains[0][at : at + 8, :]
    for j in range(HALO):
        counts[beyond + j] = jnp.broadcast_to(aside[pl.ds(2 * (1 - core) + j, 1), :], (8, WIDE))
    stages((ext, one, two, counts, flows, flat, east, north, salt), runs, ((10 * core, 6, 3), (6 * core, 6, 3), (2 * core, 6, 3)))
    for f in range(2):
        flows[f] = flat[2] * (flows[f] * (1.0 / LEV))


def stages(arrays, runs, spans):
    ext, one, two, counts, flows, _flat, east, north, salt = arrays
    sub = lax.broadcasted_iota(jnp.int32, (8, WIDE), 0)

    def stage(span, source, lead, inset, weight, scale, write, base=None):
        press = PRESS_COEF * scale / 12.0

        def twelve(ahead, behind, ahead2, behind2):
            return 8.0 * (ahead - behind) - (ahead2 - behind2)

        start, rows, together = span

        def row(index, _):
            o = start + index
            count = counts[o + inset]
            total_x = jnp.zeros((8, WIDE), F32)
            total_y = jnp.zeros((8, WIDE), F32)
            for t in range(TILES):
                here = slice(8 * t, 8 * t + 8)
                back2, back, q, fore, fore2 = [source[2, o + lead + k, here, :] for k in range(5)]
                right, left, right2, left2 = shifts(q)
                grad_x = twelve(fore, back, fore2, back2)
                grad_y = twelve(right, left, right2, left2)
                around = (fore + back) + (right + left)
                total_x = total_x + grad_x
                total_y = total_y + grad_y
                runs[0, here, :] = total_x
                runs[1, here, :] = total_y
                advect = (scale / 12.0) * (
                    source[0, o + lead + 2, here, :] * grad_x + source[1, o + lead + 2, here, :] * grad_y
                )
                value = (weight - 4.0 * VISCOSITY * scale) * q + (VISCOSITY * scale * around - advect)
                if base:
                    value = value + base * ext[2, o + inset, here, :]
                keep = count > (TILES * sub + t).astype(F32)
                write(o, t, 2, jnp.where(keep, value, 0.0))
            above_x = before(total_x, sub)
            above_y = before(total_y, sub)
            for t in range(TILES):
                here = slice(8 * t, 8 * t + 8)
                u = source[0, o + lead + 2, here, :]
                v = source[1, o + lead + 2, here, :]
                us = (scale / 12.0) * u
                vs = (scale / 12.0) * v
                keep = count > (TILES * sub + t).astype(F32)
                for f in range(2):
                    q = source[f, o + lead + 2, here, :]
                    back2, back = source[f, o + lead, here, :], source[f, o + lead + 1, here, :]
                    fore, fore2 = source[f, o + lead + 3, here, :], source[f, o + lead + 4, here, :]
                    right, left, right2, left2 = shifts(q)
                    advect = us * twelve(fore, back, fore2, back2) + vs * twelve(right, left, right2, left2)
                    around = (fore + back) + (right + left)
                    value = (weight - 4.0 * VISCOSITY * scale) * q + (VISCOSITY * scale * around - advect)
                    if f == 0:
                        value = value + (CORIOLIS * scale * v - press * (runs[0, here, :] + above_x))
                    if f == 1:
                        value = value - (CORIOLIS * scale * u + press * (runs[1, here, :] + above_y))
                    if base:
                        value = value + base * ext[f, o + inset, here, :]
                    write(o, t, f, jnp.where(keep, value, 0.0))
            return 0

        lax.fori_loop(0, rows, row, 0, unroll=together)

    def write1(o, t, f, value):
        one[f, o, 8 * t : 8 * t + 8, :] = value

    def write2(o, t, f, value):
        two[f, o, 8 * t : 8 * t + 8, :] = value

    partial = {}

    def write3(o, t, f, value):
        out = (east, north, salt)[f]
        for h in range(2):
            out[h, pl.ds(ROWS * t + o, 8, stride=ROWS * TILES), :] = value[:, h * 128 : (h + 1) * 128]
        if f < 2:
            partial[f] = partial[f] + value if t else value
            if t == TILES - 1:
                flows[f, pl.ds(o, 1), :] = jnp.sum(partial[f], axis=0, keepdims=True)

    stage(spans[0], ext, 2, 4, 1.0, TIME_STEP, write1)
    stage(spans[1], one, 0, 6, 0.25, 0.25 * TIME_STEP, write2, 0.75)
    stage(spans[2], two, 0, 8, 2.0 / 3.0, 2.0 / 3.0 * TIME_STEP, write3, 1.0 / 3.0)


def solve_kernel(sc, mine, pair, remote, remote_pair, far, u, v, s, east, north, salt, level, wide, out_u, out_v, sems):
    core = sc[1]
    halves = [slice(128 * h, 128 * h + 128) for h in range(2)]
    copies = [pltpu.make_async_copy(s.at[h], salt.at[:, :, halves[h]], sems.at[h]) for h in range(2)]
    for copy in copies:
        copy.start()
    wide[:, 24:32, :] = mine[...]
    for slot, block in (
        (4 - 2 * core, pair[...]),
        (2 + 2 * core, remote[0]),
        (1 + 4 * core, remote[1]),
        (5 - 4 * core, remote_pair[0]),
        (6 - 6 * core, remote_pair[1]),
        (6 * core, far[...]),
    ):
        wide[:, pl.ds(pl.multiple_of(8 * slot, 8), 8), :] = block
    high = 48
    near = slice(4, 52)
    own = slice(20, 28)

    def up(x):
        return pltpu.roll(x, high - 1, 0)

    def down(x):
        return pltpu.roll(x, 1, 0)

    def right(x):
        return pltpu.roll(x, WIDE - 1, 1)

    def left(x):
        return pltpu.roll(x, 1, 1)

    wet = jnp.where(wide[3, near, :] > 0.0, 1.0, 0.0)
    sixth = wet * (1.0 / 6.0)
    middle = wet * (SIGMA_SHIFT + 20.0 / 6.0) + (1.0 - wet)

    def less(res, e):
        w = wet * e
        rows = up(w) + down(w)
        mix = 4.0 * w + rows
        return (res - middle * e) + sixth * (4.0 * rows + (right(mix) + left(mix)))

    flow_east = wide[0, near, :]
    flow_north = wide[1, near, :]
    x = wide[2, near, :]
    div = 0.5 * (up(flow_east) - down(flow_east)) + 0.5 * (right(flow_north) - left(flow_north))
    res = less(wet * (SIGMA_SHIFT * x - DIVERGENCE_COEF * div), x)
    step = res * (1.0 / CHEB_CENTER)
    keeps, gains = cheb_table(ITERS)
    for index in range(ITERS):
        x = x + step
        if index < ITERS - 1:
            res = less(res, step)
            step = keeps[index] * step + gains[index] * res
    slope_east = (0.5 * (up(x) - down(x)))[own, :COLS]
    slope_north = (0.5 * (right(x) - left(x)))[own, :COLS]
    level[...] = x[own, :COLS]
    count = mine[3][:, :COLS]
    part = LEV // 4
    for first in range(0, LEV, part):
        for lev in range(first, first + part):
            keep = count > lev
            for h, cols in enumerate(halves):
                out_u[h, lev] = jnp.where(keep[:, cols], u[h, lev] - slope_east[:, cols], 0.0)
                out_v[h, lev] = jnp.where(keep[:, cols], v[h, lev] - slope_north[:, cols], 0.0)
        some = slice(first, first + part)
        for source, target in ((out_u, east), (out_v, north)):
            for h, cols in enumerate(halves):
                copy = pltpu.make_async_copy(source.at[h, some], target.at[some, :, cols], sems.at[len(copies)])
                copy.start()
                copies.append(copy)
    for copy in copies:
        copy.wait()


def swap(pairs):
    return [p for a, b in pairs for p in ((a, b), (b, a))]


def call(body, outs, scratch=(), ins=0, space=pltpu.VMEM, away=0, aliases={}, flops=None):
    vmem = pl.BlockSpec(memory_space=pltpu.VMEM)
    smem = pl.BlockSpec(memory_space=pltpu.SMEM)
    return pl.pallas_call(
        body,
        out_shape=[jax.ShapeDtypeStruct(s, F32) for s in outs],
        in_specs=[smem] + [pl.BlockSpec(memory_space=space)] * ins,
        out_specs=[pl.BlockSpec(memory_space=pltpu.HBM)] * away + [vmem] * (len(outs) - away),
        scratch_shapes=[pltpu.VMEM(s, F32) if isinstance(s, tuple) else s for s in scratch],
        input_output_aliases=aliases,
        cost_estimate=flops and pl.CostEstimate(flops=flops, transcendentals=0, bytes_accessed=0),
        compiler_params=pltpu.CompilerParams(vmem_limit_bytes=16 * 1024 * 1024),
    )


def local(u, v, s, surface, depth, wet, active):
    gx = lax.axis_size("gx")
    gy = lax.axis_size("gy")
    me = lax.axis_index("gx")
    scalars = jnp.stack([me, me % 2, lax.axis_index("gy") % 2]).astype(jnp.int32)
    on_chip = swap([(i, i + 1) for i in range(0, gx, 2)])
    next_chip = swap([(i, i + 1) for i in range(1, gx - 1, 2)])
    far_chip = swap([(i, i + 3) for i in range(1, gx - 3, 2)])
    even = swap([(i, i + 1) for i in range(0, gy, 2)])
    odd = swap([(i, i + 1) for i in range(1, gy - 1, 2)])

    def both(first, second):
        return [(i * gy + j, k * gy + l) for i, k in first for j, l in second]

    edge_a, edge_b, corner_a, corner_b, *packed = call(
        pack_kernel,
        [(EDGE_TILES * LEV + 8, 128)] * 2
        + [(CORNER_TILES * LEV + 8, 128)] * 2
        + [(6 * HALO * levels + (0 if c else 16), 128) for c, levels in enumerate(SIZES)]
        + [(6 * ROWS * LEV + 16, 128), (3, ROWS, COLS)],
        [pltpu.VMEM((ROWS, COLS), jnp.int32)] * 2
        + [(ROWS, COLS)] * 2
        + [(LEV, ROWS, COLS)] * 3
        + [pltpu.SemaphoreType.DMA((7,))],
        ins=7,
        space=pltpu.HBM,
    )(scalars, *(pltpu.with_memory_space_constraint(x, pltpu.HBM) for x in (u, v, s, wet, active, surface, depth)))
    mains = packed[:CHUNKS]
    st, plane = packed[CHUNKS:]
    stp = lax.ppermute(st, "gx", on_chip)
    edge_a = lax.ppermute(edge_a, "gy", even)
    edge_b = lax.ppermute(edge_b, "gy", odd)
    corner_a = lax.ppermute(corner_a, ("gx", "gy"), both(next_chip, even))
    corner_b = lax.ppermute(corner_b, ("gx", "gy"), both(next_chip, odd))
    stp, *mains = lax.optimization_barrier((stp, *mains))
    main = [lax.ppermute(m, "gx", next_chip) for m in mains]
    edgep_a = lax.ppermute(edge_a, "gx", on_chip)
    edgep_b = lax.ppermute(edge_b, "gx", on_chip)

    field = (2, ROWS * LEV, 128)
    shapes = [(3, 24, LEV, WIDE), (3, 16, LEV, WIDE), (3, 12, LEV, WIDE), (24, 8, WIDE), (4, ROWS, WIDE)]
    *shared, flat, u, v, s = call(
        early_kernel,
        shapes + [(3, ROWS, WIDE)] + [field] * 3,
        [(2, LEV, WIDE), (ROWS, WIDE)],
        ins=7,
        flops=EARLY_COST,
    )(scalars, st, stp, edge_a, edge_b, edgep_a, edgep_b, plane)
    shift = 1 + CHUNKS + 2
    *_, flows, u, v, s = call(
        late_kernel,
        shapes + [field] * 3,
        [(2, LEV, WIDE), (ROWS, WIDE)],
        ins=CHUNKS + 11,
        aliases={shift + i: i for i in range(5)} | {shift + 6 + i: 5 + i for i in range(3)},
    )(scalars, *main, corner_a, corner_b, *shared, flat, u, v, s)
    state = [u, v, s]
    far = lax.ppermute(flows, "gx", far_chip)
    pair = lax.ppermute(flows, "gx", on_chip)
    remote = lax.ppermute(jnp.stack([flows, pair]), "gx", next_chip)
    remote, far = lax.optimization_barrier((remote, far))
    remote_pair = lax.ppermute(remote, "gx", on_chip)
    state = [field.reshape(2, LEV, ROWS, 128) for field in state]
    east, north, salt, level = call(
        solve_kernel,
        [(LEV, ROWS, COLS)] * 3 + [(ROWS, COLS)],
        [(4, 56, WIDE)] + [(2, LEV, ROWS, 128)] * 2 + [pltpu.SemaphoreType.DMA((18,))],
        ins=8,
        away=3,
    )(scalars, flows, pair, remote, remote_pair, far, *state)
    return east, north, salt, level


def solution(mesh):
    cube = P(None, "gx", "gy")
    flat = P("gx", "gy")
    return jax.shard_map(
        local,
        mesh=mesh,
        in_specs=(cube, cube, cube, flat, flat, flat, flat),
        out_specs=(cube, cube, cube, flat),
        check_vma=False,
    )
```

```python
import jax
import jax.numpy as jnp
from jax import lax
from jax.experimental import pallas as pl
from jax.experimental.pallas import tpu as pltpu
from jax.sharding import PartitionSpec as P

ITERS = 16
TIME_STEP = 0.2
CORIOLIS = 0.3
PRESS_COEF = 0.05
VISCOSITY = 0.1
DIFFUSIVITY = 0.1
SIGMA_SHIFT = 0.25
CHEB_CENTER = 3.625
CHEB_HALF = 3.375
DIVERGENCE_COEF = 8.0

LEV = 48
ROWS = 8
COLS = 256
EXT = 128
EARLY_COST = 7_600_000_000
WIDE = COLS + EXT
HALO = 6
SIZES = (48,)
CHUNKS = len(SIZES)
STARTS = tuple(sum(SIZES[:c]) for c in range(CHUNKS))
TILES = LEV // 8
SLOT = 25
SLOTS = 5
EDGE_TILES = -(-3 * ROWS // SLOTS)
CORNER_TILES = -(-3 * HALO // SLOTS)
F32 = jnp.float32


def cheb_table(count):
    first = CHEB_CENTER / CHEB_HALF
    ratio = 1.0 / first
    keeps = []
    gains = []
    for index in range(count):
        ratio_next = 1.0 / (2.0 * first - ratio)
        keeps.append(ratio_next * ratio)
        gains.append(2.0 * ratio_next / CHEB_HALF)
        ratio = ratio_next
    return (keeps, gains)


def lanes(shape):
    return lax.broadcasted_iota(jnp.int32, shape, len(shape) - 1)


def place(low, high, units, slot):
    left, right = units
    lane = lanes(low.shape)
    here = (lane >= SLOT * slot) & (lane < SLOT * slot + SLOT)
    low = low if slot == 0 else pltpu.roll(low, SLOT * slot, 1)
    high = pltpu.roll(high, SLOT * slot + SLOT, 1)
    return jnp.where(here, low, left), jnp.where(here, high, right)


def unpack(high, low, slot):
    lane = lanes(high.shape)
    high = high if slot == 0 else pltpu.roll(high, 128 - SLOT * slot, 1)
    low = pltpu.roll(low, 128 - SLOT - SLOT * slot, 1)
    return jnp.where(lane < SLOT, high, jnp.where(lane >= 128 - SLOT, low, 0.0))


def ordered(first, second, flag):
    odd = jnp.full(first.shape, flag, jnp.int32) == 1
    return jnp.where(odd, second, first), jnp.where(odd, first, second)


def pack_kernel(sc, u, v, s, wet, act, surf, depth, edge_a, edge_b, corner_a, corner_b, *rest):
    mains = rest[:CHUNKS]
    st, plane = rest[CHUNKS : CHUNKS + 2]
    buffers = rest[CHUNKS + 2 : CHUNKS + 9]
    sems = rest[CHUNKS + 9]
    core = sc[1]
    north_odd = sc[2]
    sources = (wet, act, surf, depth, u, v, s)
    copies = [pltpu.make_async_copy(a, b, sems.at[i]) for i, (a, b) in enumerate(zip(sources, buffers))]
    for copy in copies:
        copy.start()
    for copy in copies[:4]:
        copy.wait()
    wet, act, surf, depth, *cubes = buffers
    count = (act[...] * wet[...]).astype(F32)
    plane[0] = surf[...]
    plane[1] = count
    plane[2] = depth[...]
    for f in range(3):
        copies[4 + f].wait()
        for lev in range(LEV):
            tile = jnp.where(count > lev, cubes[f][lev], 0.0)
            spot = 8 * (lev % TILES) + lev // TILES
            for h in range(2):
                st[pl.ds((2 * f + h) * ROWS * LEV + spot, ROWS, stride=LEV), :] = tile[:, h * 128 : (h + 1) * 128]
    base = 2 * core
    for c in range(CHUNKS):
        levels = SIZES[c]
        for f in range(3):
            for j in range(HALO):
                for h in range(2):
                    start = pl.multiple_of(((2 * f + h) * ROWS + base + j) * LEV + STARTS[c], 8)
                    at = ((2 * f + h) * HALO + j) * levels
                    mains[c][at : at + levels, :] = st[pl.ds(start, levels), :]
    for h in range(2):
        at = 6 * HALO * SIZES[0] + 8 * h
        mains[0][at : at + 8, :] = count[:, 128 * h : 128 * h + 128]
        at = 6 * ROWS * LEV + 8 * h
        st[at : at + 8, :] = count[:, 128 * h : 128 * h + 128]
    blank = jnp.zeros((LEV, 128), F32)
    for tiles, rows, first, a, b in (
        (EDGE_TILES, ROWS, 0, edge_a, edge_b),
        (CORNER_TILES, HALO, base, corner_a, corner_b),
    ):
        for g in range(tiles):
            units = (blank, blank)
            for slot in range(min(SLOTS, 3 * rows - SLOTS * g)):
                f, r = divmod(SLOTS * g + slot, rows)
                low = pl.multiple_of((2 * f * ROWS + first + r) * LEV, 8)
                high = pl.multiple_of(((2 * f + 1) * ROWS + first + r) * LEV, 8)
                units = place(st[pl.ds(low, LEV), :], st[pl.ds(high, LEV), :], units, slot)
            b[g * LEV : g * LEV + LEV, :], a[g * LEV : g * LEV + LEV, :] = ordered(*units, north_odd)
    units = (blank[:ROWS], blank[:ROWS])
    for slot, field in enumerate((surf[...], count, depth[...])):
        units = place(field[:, :128], field[:, 128:], units, slot)
    left, right = ordered(*units, north_odd)
    for tiles, a, b in ((EDGE_TILES, edge_a, edge_b), (CORNER_TILES, corner_a, corner_b)):
        b[tiles * LEV :, :] = left
        a[tiles * LEV :, :] = right


def shifts(q):
    return (
        pltpu.roll(q, WIDE - 1, 1),
        pltpu.roll(q, 1, 1),
        pltpu.roll(q, WIDE - 2, 1),
        pltpu.roll(q, 2, 1),
    )


def before(x, sub):
    total = x
    for step in (1, 2, 4):
        total = total + jnp.where(sub >= step, pltpu.roll(total, step, 0), 0.0)
    return total - x


def columns_beyond(ext, tiles, rows, first, a, b, north_odd):
    for g in range(tiles):
        here = slice(g * LEV, g * LEV + LEV)
        high, low = ordered(a[here, :], b[here, :], north_odd)
        for slot in range(min(SLOTS, 3 * rows - SLOTS * g)):
            f, r = divmod(SLOTS * g + slot, rows)
            ext[f, first + r, :, COLS:] = unpack(high, low, slot)


def plane_beyond(tiles, a, b, slot, north_odd):
    high, low = ordered(a[tiles * LEV :, :], b[tiles * LEV :, :], north_odd)
    return unpack(high, low, slot)


def early_kernel(sc, st, stp, edge_a, edge_b, edgep_a, edgep_b, plane, *rest):
    arrays, runs, aside = rest[:-2], rest[-2], rest[-1]
    ext, one, two, counts, flows, flat, east, north, salt = arrays
    core = sc[1]
    north_odd = sc[2]
    beside = 16 * (1 - core)
    for source, first in ((st, ROWS), (stp, beside)):
        for f in range(3):
            for r in range(ROWS):
                for h in range(2):
                    at = ((2 * f + h) * ROWS + r) * LEV
                    ext[f, first + r, :, h * 128 : (h + 1) * 128] = source[at : at + LEV, :]
    columns_beyond(ext, EDGE_TILES, ROWS, ROWS, edge_a, edge_b, north_odd)
    columns_beyond(ext, EDGE_TILES, ROWS, beside, edgep_a, edgep_b, north_odd)
    for f in range(3):
        flat[f, :, :COLS] = plane[f]
        flat[f, :, COLS:] = plane_beyond(EDGE_TILES, edge_a, edge_b, f, north_odd)
    aside[:, COLS:] = plane_beyond(EDGE_TILES, edgep_a, edgep_b, 1, north_odd)
    for h in range(2):
        at = 6 * ROWS * LEV + 8 * h
        aside[:, h * 128 : (h + 1) * 128] = stp[at : at + 8, :]
    for r in range(ROWS):
        counts[ROWS + r] = jnp.broadcast_to(flat[1, r : r + 1, :], (8, WIDE))
        counts[beside + r] = jnp.broadcast_to(aside[r : r + 1, :], (8, WIDE))
    other = 1 - core
    stages(arrays, runs, ((6 * other, 10, 5), (6 * other, 6, 3), (6 * other, 2, 2)))
    for f in range(2):
        flows[2 + f] = flat[f]


def late_kernel(sc, *rest):
    mains = rest[:CHUNKS]
    corner_a, corner_b, _e, _o, _t, _c, _f, flat, _u, _v, _s = rest[CHUNKS : CHUNKS + 11]
    ext, one, two, counts, flows, east, north, salt, runs, aside = rest[CHUNKS + 11 :]
    core = sc[1]
    north_odd = sc[2]
    beyond = 2 + 14 * core
    for f in range(3):
        for j in range(HALO):
            for h in range(2):
                for main, levels, lev0 in zip(mains, SIZES, STARTS):
                    at = ((2 * f + h) * HALO + j) * levels
                    ext[f, beyond + j, lev0 : lev0 + levels, h * 128 : (h + 1) * 128] = main[at : at + levels, :]
    columns_beyond(ext, CORNER_TILES, HALO, beyond, corner_a, corner_b, north_odd)
    aside[:, COLS:] = plane_beyond(CORNER_TILES, corner_a, corner_b, 1, north_odd)
    for h in range(2):
        at = 6 * HALO * SIZES[0] + 8 * h
        aside[:, h * 128 : (h + 1) * 128] = mains[0][at : at + 8, :]
    for j in range(HALO):
        counts[beyond + j] = jnp.broadcast_to(aside[pl.ds(2 * (1 - core) + j, 1), :], (8, WIDE))
    stages((ext, one, two, counts, flows, flat, east, north, salt), runs, ((10 * core, 6, 3), (6 * core, 6, 3), (2 * core, 6, 3)))
    for f in range(2):
        flows[f] = flat[2] * (flows[f] * (1.0 / LEV))


def stages(arrays, runs, spans):
    ext, one, two, counts, flows, _flat, east, north, salt = arrays
    sub = lax.broadcasted_iota(jnp.int32, (8, WIDE), 0)

    def stage(span, source, lead, inset, weight, scale, write, base=None):
        press = PRESS_COEF * scale / 12.0

        def twelve(ahead, behind, ahead2, behind2):
            return 8.0 * (ahead - behind) - (ahead2 - behind2)

        start, rows, together = span

        def row(index, _):
            o = start + index
            count = counts[o + inset]
            total_x = jnp.zeros((8, WIDE), F32)
            total_y = jnp.zeros((8, WIDE), F32)
            for t in range(TILES):
                here = slice(8 * t, 8 * t + 8)
                back2, back, q, fore, fore2 = [source[2, o + lead + k, here, :] for k in range(5)]
                right, left, right2, left2 = shifts(q)
                grad_x = twelve(fore, back, fore2, back2)
                grad_y = twelve(right, left, right2, left2)
                around = (fore + back) + (right + left)
                total_x = total_x + grad_x
                total_y = total_y + grad_y
                runs[0, here, :] = total_x
                runs[1, here, :] = total_y
                advect = (scale / 12.0) * (
                    source[0, o + lead + 2, here, :] * grad_x + source[1, o + lead + 2, here, :] * grad_y
                )
                value = (weight - 4.0 * VISCOSITY * scale) * q + (VISCOSITY * scale * around - advect)
                if base:
                    value = value + base * ext[2, o + inset, here, :]
                keep = count > (TILES * sub + t).astype(F32)
                write(o, t, 2, jnp.where(keep, value, 0.0))
            above_x = before(total_x, sub)
            above_y = before(total_y, sub)
            for t in range(TILES):
                here = slice(8 * t, 8 * t + 8)
                u = source[0, o + lead + 2, here, :]
                v = source[1, o + lead + 2, here, :]
                us = (scale / 12.0) * u
                vs = (scale / 12.0) * v
                keep = count > (TILES * sub + t).astype(F32)
                for f in range(2):
                    q = source[f, o + lead + 2, here, :]
                    back2, back = source[f, o + lead, here, :], source[f, o + lead + 1, here, :]
                    fore, fore2 = source[f, o + lead + 3, here, :], source[f, o + lead + 4, here, :]
                    right, left, right2, left2 = shifts(q)
                    advect = us * twelve(fore, back, fore2, back2) + vs * twelve(right, left, right2, left2)
                    around = (fore + back) + (right + left)
                    value = (weight - 4.0 * VISCOSITY * scale) * q + (VISCOSITY * scale * around - advect)
                    if f == 0:
                        value = value + (CORIOLIS * scale * v - press * (runs[0, here, :] + above_x))
                    if f == 1:
                        value = value - (CORIOLIS * scale * u + press * (runs[1, here, :] + above_y))
                    if base:
                        value = value + base * ext[f, o + inset, here, :]
                    write(o, t, f, jnp.where(keep, value, 0.0))
            return 0

        lax.fori_loop(0, rows, row, 0, unroll=together)

    def write1(o, t, f, value):
        one[f, o, 8 * t : 8 * t + 8, :] = value

    def write2(o, t, f, value):
        two[f, o, 8 * t : 8 * t + 8, :] = value

    partial = {}

    def write3(o, t, f, value):
        out = (east, north, salt)[f]
        for h in range(2):
            out[h, pl.ds(ROWS * t + o, 8, stride=ROWS * TILES), :] = value[:, h * 128 : (h + 1) * 128]
        if f < 2:
            partial[f] = partial[f] + value if t else value
            if t == TILES - 1:
                flows[f, pl.ds(o, 1), :] = jnp.sum(partial[f], axis=0, keepdims=True)

    stage(spans[0], ext, 2, 4, 1.0, TIME_STEP, write1)
    stage(spans[1], one, 0, 6, 0.25, 0.25 * TIME_STEP, write2, 0.75)
    stage(spans[2], two, 0, 8, 2.0 / 3.0, 2.0 / 3.0 * TIME_STEP, write3, 1.0 / 3.0)


def solve_kernel(sc, mine, pair, remote, remote_pair, far, u, v, s, east, north, salt, level, wide, out_u, out_v, sems):
    core = sc[1]
    halves = [slice(128 * h, 128 * h + 128) for h in range(2)]
    copies = [pltpu.make_async_copy(s.at[h], salt.at[:, :, halves[h]], sems.at[h]) for h in range(2)]
    for copy in copies:
        copy.start()
    wide[:, 24:32, :] = mine[...]
    for slot, block in (
        (4 - 2 * core, pair[...]),
        (2 + 2 * core, remote[0]),
        (1 + 4 * core, remote[1]),
        (5 - 4 * core, remote_pair[0]),
        (6 - 6 * core, remote_pair[1]),
        (6 * core, far[...]),
    ):
        wide[:, pl.ds(pl.multiple_of(8 * slot, 8), 8), :] = block
    high = 48
    near = slice(4, 52)
    own = slice(20, 28)

    def up(x):
        return pltpu.roll(x, high - 1, 0)

    def down(x):
        return pltpu.roll(x, 1, 0)

    def right(x):
        return pltpu.roll(x, WIDE - 1, 1)

    def left(x):
        return pltpu.roll(x, 1, 1)

    wet = jnp.where(wide[3, near, :] > 0.0, 1.0, 0.0)
    sixth = wet * (1.0 / 6.0)
    middle = wet * (SIGMA_SHIFT + 20.0 / 6.0) + (1.0 - wet)

    def less(res, e):
        w = wet * e
        rows = up(w) + down(w)
        mix = 4.0 * w + rows
        return (res - middle * e) + sixth * (4.0 * rows + (right(mix) + left(mix)))

    flow_east = wide[0, near, :]
    flow_north = wide[1, near, :]
    x = wide[2, near, :]
    div = 0.5 * (up(flow_east) - down(flow_east)) + 0.5 * (right(flow_north) - left(flow_north))
    res = less(wet * (SIGMA_SHIFT * x - DIVERGENCE_COEF * div), x)
    step = res * (1.0 / CHEB_CENTER)
    keeps, gains = cheb_table(ITERS)
    for index in range(ITERS):
        x = x + step
        if index < ITERS - 1:
            res = less(res, step)
            step = keeps[index] * step + gains[index] * res
    slope_east = (0.5 * (up(x) - down(x)))[own, :COLS]
    slope_north = (0.5 * (right(x) - left(x)))[own, :COLS]
    level[...] = x[own, :COLS]
    count = mine[3][:, :COLS]
    part = LEV // 4
    for first in range(0, LEV, part):
        for lev in range(first, first + part):
            keep = count > lev
            for h, cols in enumerate(halves):
                out_u[h, lev] = jnp.where(keep[:, cols], u[h, lev] - slope_east[:, cols], 0.0)
                out_v[h, lev] = jnp.where(keep[:, cols], v[h, lev] - slope_north[:, cols], 0.0)
        some = slice(first, first + part)
        for source, target in ((out_u, east), (out_v, north)):
            for h, cols in enumerate(halves):
                copy = pltpu.make_async_copy(source.at[h, some], target.at[some, :, cols], sems.at[len(copies)])
                copy.start()
                copies.append(copy)
    for copy in copies:
        copy.wait()


def swap(pairs):
    return [p for a, b in pairs for p in ((a, b), (b, a))]


def call(body, outs, scratch=(), ins=0, space=pltpu.VMEM, away=0, aliases={}, flops=None):
    vmem = pl.BlockSpec(memory_space=pltpu.VMEM)
    smem = pl.BlockSpec(memory_space=pltpu.SMEM)
    return pl.pallas_call(
        body,
        out_shape=[jax.ShapeDtypeStruct(s, F32) for s in outs],
        in_specs=[smem] + [pl.BlockSpec(memory_space=space)] * ins,
        out_specs=[pl.BlockSpec(memory_space=pltpu.HBM)] * away + [vmem] * (len(outs) - away),
        scratch_shapes=[pltpu.VMEM(s, F32) if isinstance(s, tuple) else s for s in scratch],
        input_output_aliases=aliases,
        cost_estimate=flops and pl.CostEstimate(flops=flops, transcendentals=0, bytes_accessed=0),
        compiler_params=pltpu.CompilerParams(vmem_limit_bytes=16 * 1024 * 1024),
    )


def local(u, v, s, surface, depth, wet, active):
    gx = lax.axis_size("gx")
    gy = lax.axis_size("gy")
    me = lax.axis_index("gx")
    scalars = jnp.stack([me, me % 2, lax.axis_index("gy") % 2]).astype(jnp.int32)
    on_chip = swap([(i, i + 1) for i in range(0, gx, 2)])
    next_chip = swap([(i, i + 1) for i in range(1, gx - 1, 2)])
    far_chip = swap([(i, i + 3) for i in range(1, gx - 3, 2)])
    even = swap([(i, i + 1) for i in range(0, gy, 2)])
    odd = swap([(i, i + 1) for i in range(1, gy - 1, 2)])

    def both(first, second):
        return [(i * gy + j, k * gy + l) for i, k in first for j, l in second]

    edge_a, edge_b, corner_a, corner_b, *packed = call(
        pack_kernel,
        [(EDGE_TILES * LEV + 8, 128)] * 2
        + [(CORNER_TILES * LEV + 8, 128)] * 2
        + [(6 * HALO * levels + (0 if c else 16), 128) for c, levels in enumerate(SIZES)]
        + [(6 * ROWS * LEV + 16, 128), (3, ROWS, COLS)],
        [pltpu.VMEM((ROWS, COLS), jnp.int32)] * 2
        + [(ROWS, COLS)] * 2
        + [(LEV, ROWS, COLS)] * 3
        + [pltpu.SemaphoreType.DMA((7,))],
        ins=7,
        space=pltpu.HBM,
    )(scalars, *(pltpu.with_memory_space_constraint(x, pltpu.HBM) for x in (u, v, s, wet, active, surface, depth)))
    mains = packed[:CHUNKS]
    st, plane = packed[CHUNKS:]
    stp = lax.ppermute(st, "gx", on_chip)
    edge_a = lax.ppermute(edge_a, "gy", even)
    edge_b = lax.ppermute(edge_b, "gy", odd)
    corner_a = lax.ppermute(corner_a, ("gx", "gy"), both(next_chip, even))
    corner_b = lax.ppermute(corner_b, ("gx", "gy"), both(next_chip, odd))
    stp, *mains = lax.optimization_barrier((stp, *mains))
    main = [lax.ppermute(m, "gx", next_chip) for m in mains]
    edge_a, edge_b, corner_a, corner_b = lax.optimization_barrier((edge_a, edge_b, corner_a, corner_b))
    edgep_a = lax.ppermute(edge_a, "gx", on_chip)
    edgep_b = lax.ppermute(edge_b, "gx", on_chip)

    field = (2, ROWS * LEV, 128)
    shapes = [(3, 24, LEV, WIDE), (3, 16, LEV, WIDE), (3, 12, LEV, WIDE), (24, 8, WIDE), (4, ROWS, WIDE)]
    *shared, flat, u, v, s = call(
        early_kernel,
        shapes + [(3, ROWS, WIDE)] + [field] * 3,
        [(2, LEV, WIDE), (ROWS, WIDE)],
        ins=7,
        flops=EARLY_COST,
    )(scalars, st, stp, edge_a, edge_b, edgep_a, edgep_b, plane)
    shift = 1 + CHUNKS + 2
    *_, flows, u, v, s = call(
        late_kernel,
        shapes + [field] * 3,
        [(2, LEV, WIDE), (ROWS, WIDE)],
        ins=CHUNKS + 11,
        aliases={shift + i: i for i in range(5)} | {shift + 6 + i: 5 + i for i in range(3)},
    )(scalars, *main, corner_a, corner_b, *shared, flat, u, v, s)
    state = [u, v, s]
    far = lax.ppermute(flows, "gx", far_chip)
    pair = lax.ppermute(flows, "gx", on_chip)
    remote = lax.ppermute(jnp.stack([flows, pair]), "gx", next_chip)
    remote, far = lax.optimization_barrier((remote, far))
    remote_pair = lax.ppermute(remote, "gx", on_chip)
    state = [field.reshape(2, LEV, ROWS, 128) for field in state]
    east, north, salt, level = call(
        solve_kernel,
        [(LEV, ROWS, COLS)] * 3 + [(ROWS, COLS)],
        [(4, 56, WIDE)] + [(2, LEV, ROWS, 128)] * 2 + [pltpu.SemaphoreType.DMA((18,))],
        ins=8,
        away=3,
    )(scalars, flows, pair, remote, remote_pair, far, *state)
    return east, north, salt, level


def solution(mesh):
    cube = P(None, "gx", "gy")
    flat = P("gx", "gy")
    return jax.shard_map(
        local,
        mesh=mesh,
        in_specs=(cube, cube, cube, flat, flat, flat, flat),
        out_specs=(cube, cube, cube, flat),
        check_vma=False,
    )
```

```python
import jax
import jax.numpy as jnp
from jax import lax
from jax.experimental import pallas as pl
from jax.experimental.pallas import tpu as pltpu
from jax.sharding import PartitionSpec as P

ITERS = 16
TIME_STEP = 0.2
CORIOLIS = 0.3
PRESS_COEF = 0.05
VISCOSITY = 0.1
DIFFUSIVITY = 0.1
SIGMA_SHIFT = 0.25
CHEB_CENTER = 3.625
CHEB_HALF = 3.375
DIVERGENCE_COEF = 8.0

LEV = 48
ROWS = 8
COLS = 256
EXT = 128
WIDE = COLS + EXT
HALO = 6
SIZES = (48,)
CHUNKS = len(SIZES)
STARTS = tuple(sum(SIZES[:c]) for c in range(CHUNKS))
TILES = LEV // 8
SLOT = 7
SLOTS = 18
REACH = 25
EDGE_TILES = -(-3 * ROWS // SLOTS)
CORNER_TILES = -(-3 * HALO // SLOTS)
F32 = jnp.float32


def cheb_table(count):
    first = CHEB_CENTER / CHEB_HALF
    ratio = 1.0 / first
    keeps = []
    gains = []
    for index in range(count):
        ratio_next = 1.0 / (2.0 * first - ratio)
        keeps.append(ratio_next * ratio)
        gains.append(2.0 * ratio_next / CHEB_HALF)
        ratio = ratio_next
    return (keeps, gains)


def lanes(shape):
    return lax.broadcasted_iota(jnp.int32, shape, len(shape) - 1)


def place(low, high, units, slot, width=SLOT):
    left, right = units
    lane = lanes(low.shape)
    here = (lane >= width * slot) & (lane < width * slot + width)
    low = low if slot == 0 else pltpu.roll(low, width * slot, 1)
    high = pltpu.roll(high, width * slot + width, 1)
    return jnp.where(here, low, left), jnp.where(here, high, right)


def unpack(high, low, slot, width=SLOT):
    lane = lanes(high.shape)
    high = high if slot == 0 else pltpu.roll(high, 128 - width * slot, 1)
    low = pltpu.roll(low, 128 - width - width * slot, 1)
    return jnp.where(lane < width, high, jnp.where(lane >= 128 - width, low, 0.0))


def ordered(first, second, flag):
    odd = jnp.full(first.shape, flag, jnp.int32) == 1
    return jnp.where(odd, second, first), jnp.where(odd, first, second)


def pack_kernel(sc, u, v, s, wet, act, surf, depth, edge_a, edge_b, corner_a, corner_b, *rest):
    mains = rest[:CHUNKS]
    st, plane = rest[CHUNKS : CHUNKS + 2]
    buffers = rest[CHUNKS + 2 : CHUNKS + 9]
    sems = rest[CHUNKS + 9]
    core = sc[1]
    north_odd = sc[2]
    sources = (wet, act, surf, depth, u, v, s)
    copies = [pltpu.make_async_copy(a, b, sems.at[i]) for i, (a, b) in enumerate(zip(sources, buffers))]
    for copy in copies:
        copy.start()
    for copy in copies[:4]:
        copy.wait()
    wet, act, surf, depth, *cubes = buffers
    count = (act[...] * wet[...]).astype(F32)
    plane[0] = surf[...]
    plane[1] = count
    plane[2] = depth[...]
    for f in range(3):
        copies[4 + f].wait()
        for lev in range(LEV):
            tile = jnp.where(count > lev, cubes[f][lev], 0.0)
            spot = 8 * (lev % TILES) + lev // TILES
            for h in range(2):
                st[pl.ds((2 * f + h) * ROWS * LEV + spot, ROWS, stride=LEV), :] = tile[:, h * 128 : (h + 1) * 128]
    base = 2 * core
    for c in range(CHUNKS):
        levels = SIZES[c]
        for f in range(3):
            for j in range(HALO):
                for h in range(2):
                    start = pl.multiple_of(((2 * f + h) * ROWS + base + j) * LEV + STARTS[c], 8)
                    at = ((2 * f + h) * HALO + j) * levels
                    mains[c][at : at + levels, :] = st[pl.ds(start, levels), :]
    for h in range(2):
        at = 6 * HALO * SIZES[0] + 8 * h
        mains[0][at : at + 8, :] = count[:, 128 * h : 128 * h + 128]
        at = 6 * ROWS * LEV + 8 * h
        st[at : at + 8, :] = count[:, 128 * h : 128 * h + 128]
    blank = jnp.zeros((LEV, 128), F32)
    for tiles, rows, first, a, b in (
        (EDGE_TILES, ROWS, 0, edge_a, edge_b),
        (CORNER_TILES, HALO, base, corner_a, corner_b),
    ):
        for g in range(tiles):
            units = (blank, blank)
            for slot in range(min(SLOTS, 3 * rows - SLOTS * g)):
                f, r = divmod(SLOTS * g + slot, rows)
                low = pl.multiple_of((2 * f * ROWS + first + r) * LEV, 8)
                high = pl.multiple_of(((2 * f + 1) * ROWS + first + r) * LEV, 8)
                units = place(st[pl.ds(low, LEV), :], st[pl.ds(high, LEV), :], units, slot)
            b[g * LEV : g * LEV + LEV, :], a[g * LEV : g * LEV + LEV, :] = ordered(*units, north_odd)
    units = (blank[:ROWS], blank[:ROWS])
    for slot, field in enumerate((surf[...], count, depth[...])):
        units = place(field[:, :128], field[:, 128:], units, slot)
    left, right = ordered(*units, north_odd)
    for tiles, a, b in ((EDGE_TILES, edge_a, edge_b), (CORNER_TILES, corner_a, corner_b)):
        b[tiles * LEV :, :] = left
        a[tiles * LEV :, :] = right


def shifts(q):
    return (
        pltpu.roll(q, WIDE - 1, 1),
        pltpu.roll(q, 1, 1),
        pltpu.roll(q, WIDE - 2, 1),
        pltpu.roll(q, 2, 1),
    )


def before(x, sub):
    total = x
    for step in (1, 2, 4):
        total = total + jnp.where(sub >= step, pltpu.roll(total, step, 0), 0.0)
    return total - x


def rk_kernel(sc, st, stp, edge_a, edge_b, edgep_a, edgep_b, *rest):
    mains = rest[:CHUNKS]
    corner_a, corner_b, plane, flows, side_a, side_b, east, north, salt, ext, one, two, counts, flat, remote, runs = rest[CHUNKS:]
    core = sc[1]
    north_odd = sc[2]
    beside = 16 * (1 - core)
    beyond = 2 + 14 * core
    for source, first in ((st, ROWS), (stp, beside)):
        for f in range(3):
            for r in range(ROWS):
                for h in range(2):
                    at = ((2 * f + h) * ROWS + r) * LEV
                    ext[f, first + r, :, h * 128 : (h + 1) * 128] = source[at : at + LEV, :]
    for f in range(3):
        for j in range(HALO):
            for h in range(2):
                for main, levels, lev0 in zip(mains, SIZES, STARTS):
                    at = ((2 * f + h) * HALO + j) * levels
                    ext[f, beyond + j, lev0 : lev0 + levels, h * 128 : (h + 1) * 128] = main[at : at + levels, :]
    for tiles, rows, first, a, b in (
        (EDGE_TILES, ROWS, ROWS, edge_a, edge_b),
        (EDGE_TILES, ROWS, beside, edgep_a, edgep_b),
        (CORNER_TILES, HALO, beyond, corner_a, corner_b),
    ):
        for g in range(tiles):
            here = slice(g * LEV, g * LEV + LEV)
            high, low = ordered(a[here, :], b[here, :], north_odd)
            for slot in range(min(SLOTS, 3 * rows - SLOTS * g)):
                f, r = divmod(SLOTS * g + slot, rows)
                ext[f, first + r, :, COLS:] = unpack(high, low, slot)

    def beyond_plane(tiles, a, b, slot):
        high, low = ordered(a[tiles * LEV :, :], b[tiles * LEV :, :], north_odd)
        return unpack(high, low, slot)

    for f in range(3):
        flat[f, :, :COLS] = plane[f]
        flat[f, :, COLS:] = beyond_plane(EDGE_TILES, edge_a, edge_b, f)
    remote[0, :, COLS:] = beyond_plane(EDGE_TILES, edgep_a, edgep_b, 1)
    remote[1, :, COLS:] = beyond_plane(CORNER_TILES, corner_a, corner_b, 1)
    for h in range(2):
        at = 6 * ROWS * LEV + 8 * h
        remote[0, :, h * 128 : (h + 1) * 128] = stp[at : at + 8, :]
        at = 6 * HALO * SIZES[0] + 8 * h
        remote[1, :, h * 128 : (h + 1) * 128] = mains[0][at : at + 8, :]
    for r in range(ROWS):
        counts[ROWS + r] = jnp.broadcast_to(flat[1, r : r + 1, :], (8, WIDE))
        counts[beside + r] = jnp.broadcast_to(remote[0, r : r + 1, :], (8, WIDE))
    for j in range(HALO):
        counts[beyond + j] = jnp.broadcast_to(remote[1, pl.ds(2 * (1 - core) + j, 1), :], (8, WIDE))

    sub = lax.broadcasted_iota(jnp.int32, (8, WIDE), 0)

    def stage(source, lead, rows, inset, weight, scale, write, base=None):
        press = PRESS_COEF * scale / 12.0

        def twelve(ahead, behind, ahead2, behind2):
            return 8.0 * (ahead - behind) - (ahead2 - behind2)

        def row(o, _):
            count = counts[o + inset]
            total_x = jnp.zeros((8, WIDE), F32)
            total_y = jnp.zeros((8, WIDE), F32)
            for t in range(TILES):
                here = slice(8 * t, 8 * t + 8)
                back2, back, q, fore, fore2 = [source[2, o + lead + k, here, :] for k in range(5)]
                right, left, right2, left2 = shifts(q)
                grad_x = twelve(fore, back, fore2, back2)
                grad_y = twelve(right, left, right2, left2)
                around = (fore + back) + (right + left)
                total_x = total_x + grad_x
                total_y = total_y + grad_y
                runs[0, here, :] = total_x
                runs[1, here, :] = total_y
                advect = (scale / 12.0) * (
                    source[0, o + lead + 2, here, :] * grad_x + source[1, o + lead + 2, here, :] * grad_y
                )
                value = (weight - 4.0 * VISCOSITY * scale) * q + (VISCOSITY * scale * around - advect)
                if base:
                    value = value + base * ext[2, o + inset, here, :]
                keep = count > (TILES * sub + t).astype(F32)
                write(o, t, 2, jnp.where(keep, value, 0.0))
            above_x = before(total_x, sub)
            above_y = before(total_y, sub)
            for t in range(TILES):
                here = slice(8 * t, 8 * t + 8)
                u = source[0, o + lead + 2, here, :]
                v = source[1, o + lead + 2, here, :]
                us = (scale / 12.0) * u
                vs = (scale / 12.0) * v
                keep = count > (TILES * sub + t).astype(F32)
                for f in range(2):
                    q = source[f, o + lead + 2, here, :]
                    back2, back = source[f, o + lead, here, :], source[f, o + lead + 1, here, :]
                    fore, fore2 = source[f, o + lead + 3, here, :], source[f, o + lead + 4, here, :]
                    right, left, right2, left2 = shifts(q)
                    advect = us * twelve(fore, back, fore2, back2) + vs * twelve(right, left, right2, left2)
                    around = (fore + back) + (right + left)
                    value = (weight - 4.0 * VISCOSITY * scale) * q + (VISCOSITY * scale * around - advect)
                    if f == 0:
                        value = value + (CORIOLIS * scale * v - press * (runs[0, here, :] + above_x))
                    if f == 1:
                        value = value - (CORIOLIS * scale * u + press * (runs[1, here, :] + above_y))
                    if base:
                        value = value + base * ext[f, o + inset, here, :]
                    write(o, t, f, jnp.where(keep, value, 0.0))
            return 0

        lax.fori_loop(0, rows, row, 0, unroll=4)

    def write1(o, t, f, value):
        one[f, o, 8 * t : 8 * t + 8, :] = value

    def write2(o, t, f, value):
        two[f, o, 8 * t : 8 * t + 8, :] = value

    partial = {}

    def write3(o, t, f, value):
        out = (east, north, salt)[f]
        for h in range(2):
            out[h, pl.ds(ROWS * t + o, 8, stride=ROWS * TILES), :] = value[:, h * 128 : (h + 1) * 128]
        if f < 2:
            partial[f] = partial[f] + value if t else value
            if t == TILES - 1:
                flows[f, pl.ds(o, 1), :] = jnp.sum(partial[f], axis=0, keepdims=True)

    stage(ext, 2, 16, 4, 1.0, TIME_STEP, write1)
    stage(one, 0, 12, 6, 0.25, 0.25 * TIME_STEP, write2, 0.75)
    stage(two, 0, 8, 8, 2.0 / 3.0, 2.0 / 3.0 * TIME_STEP, write3, 1.0 / 3.0)
    for f in range(2):
        flows[f] = flat[2] * (flows[f] * (1.0 / LEV))
        flows[2 + f] = flat[f]
    units = (jnp.zeros((ROWS, 128), F32), jnp.zeros((ROWS, 128), F32))
    for f in range(4):
        units = place(flows[f, :, :128], flows[f, :, 128:COLS], units, f, REACH)
    side_b[...], side_a[...] = ordered(*units, north_odd)


def widen_kernel(sc, flows, side_a, side_b, out):
    high, low = ordered(side_a[...], side_b[...], sc[2])
    for f in range(4):
        out[f, :, :COLS] = flows[f, :, :COLS]
        out[f, :, COLS:] = unpack(high, low, f, REACH)


def solve_kernel(sc, mine, pair, remote, remote_pair, far, u, v, s, east, north, salt, level, wide, out_u, out_v, sems):
    core = sc[1]
    halves = [slice(128 * h, 128 * h + 128) for h in range(2)]
    copies = [pltpu.make_async_copy(s.at[h], salt.at[:, :, halves[h]], sems.at[h]) for h in range(2)]
    for copy in copies:
        copy.start()
    wide[:, 24:32, :] = mine[...]
    for slot, block in (
        (4 - 2 * core, pair[...]),
        (2 + 2 * core, remote[0]),
        (1 + 4 * core, remote[1]),
        (5 - 4 * core, remote_pair[0]),
        (6 - 6 * core, remote_pair[1]),
        (6 * core, far[...]),
    ):
        wide[:, pl.ds(pl.multiple_of(8 * slot, 8), 8), :] = block
    high = 48
    near = slice(4, 52)
    own = slice(20, 28)

    def up(x):
        return pltpu.roll(x, high - 1, 0)

    def down(x):
        return pltpu.roll(x, 1, 0)

    def right(x):
        return pltpu.roll(x, WIDE - 1, 1)

    def left(x):
        return pltpu.roll(x, 1, 1)

    wet = jnp.where(wide[3, near, :] > 0.0, 1.0, 0.0)
    sixth = wet * (1.0 / 6.0)
    middle = wet * (SIGMA_SHIFT + 20.0 / 6.0) + (1.0 - wet)

    def less(res, e):
        w = wet * e
        rows = up(w) + down(w)
        mix = 4.0 * w + rows
        return (res - middle * e) + sixth * (4.0 * rows + (right(mix) + left(mix)))

    flow_east = wide[0, near, :]
    flow_north = wide[1, near, :]
    x = wide[2, near, :]
    div = 0.5 * (up(flow_east) - down(flow_east)) + 0.5 * (right(flow_north) - left(flow_north))
    res = less(wet * (SIGMA_SHIFT * x - DIVERGENCE_COEF * div), x)
    step = res * (1.0 / CHEB_CENTER)
    keeps, gains = cheb_table(ITERS)
    for index in range(ITERS):
        x = x + step
        if index < ITERS - 1:
            res = less(res, step)
            step = keeps[index] * step + gains[index] * res
    slope_east = (0.5 * (up(x) - down(x)))[own, :COLS]
    slope_north = (0.5 * (right(x) - left(x)))[own, :COLS]
    level[...] = x[own, :COLS]
    count = mine[3][:, :COLS]
    part = LEV // 4
    for first in range(0, LEV, part):
        for lev in range(first, first + part):
            keep = count > lev
            for h, cols in enumerate(halves):
                out_u[h, lev] = jnp.where(keep[:, cols], u[h, lev] - slope_east[:, cols], 0.0)
                out_v[h, lev] = jnp.where(keep[:, cols], v[h, lev] - slope_north[:, cols], 0.0)
        some = slice(first, first + part)
        for source, target in ((out_u, east), (out_v, north)):
            for h, cols in enumerate(halves):
                copy = pltpu.make_async_copy(source.at[h, some], target.at[some, :, cols], sems.at[len(copies)])
                copy.start()
                copies.append(copy)
    for copy in copies:
        copy.wait()


def swap(pairs):
    return [p for a, b in pairs for p in ((a, b), (b, a))]


def call(body, outs, scratch=(), ins=0, space=pltpu.VMEM, away=0):
    vmem = pl.BlockSpec(memory_space=pltpu.VMEM)
    smem = pl.BlockSpec(memory_space=pltpu.SMEM)
    return pl.pallas_call(
        body,
        out_shape=[jax.ShapeDtypeStruct(s, F32) for s in outs],
        in_specs=[smem] + [pl.BlockSpec(memory_space=space)] * ins,
        out_specs=[pl.BlockSpec(memory_space=pltpu.HBM)] * away + [vmem] * (len(outs) - away),
        scratch_shapes=[pltpu.VMEM(s, F32) if isinstance(s, tuple) else s for s in scratch],
        compiler_params=pltpu.CompilerParams(vmem_limit_bytes=16 * 1024 * 1024),
    )


def local(u, v, s, surface, depth, wet, active):
    gx = lax.axis_size("gx")
    gy = lax.axis_size("gy")
    me = lax.axis_index("gx")
    scalars = jnp.stack([me, me % 2, lax.axis_index("gy") % 2]).astype(jnp.int32)
    on_chip = swap([(i, i + 1) for i in range(0, gx, 2)])
    next_chip = swap([(i, i + 1) for i in range(1, gx - 1, 2)])
    far_chip = swap([(i, i + 3) for i in range(1, gx - 3, 2)])
    even = swap([(i, i + 1) for i in range(0, gy, 2)])
    odd = swap([(i, i + 1) for i in range(1, gy - 1, 2)])

    def both(first, second):
        return [(i * gy + j, k * gy + l) for i, k in first for j, l in second]

    edge_a, edge_b, corner_a, corner_b, *packed = call(
        pack_kernel,
        [(EDGE_TILES * LEV + 8, 128)] * 2
        + [(CORNER_TILES * LEV + 8, 128)] * 2
        + [(6 * HALO * levels + (0 if c else 16), 128) for c, levels in enumerate(SIZES)]
        + [(6 * ROWS * LEV + 16, 128), (3, ROWS, COLS)],
        [pltpu.VMEM((ROWS, COLS), jnp.int32)] * 2
        + [(ROWS, COLS)] * 2
        + [(LEV, ROWS, COLS)] * 3
        + [pltpu.SemaphoreType.DMA((7,))],
        ins=7,
        space=pltpu.HBM,
    )(scalars, *(pltpu.with_memory_space_constraint(x, pltpu.HBM) for x in (u, v, s, wet, active, surface, depth)))
    mains = packed[:CHUNKS]
    st, plane = packed[CHUNKS:]
    stp = lax.ppermute(st, "gx", on_chip)
    main = [lax.ppermute(mains[0], "gx", next_chip)]
    stp, corner_a, corner_b = lax.optimization_barrier((stp, corner_a, corner_b))
    edge_a = lax.ppermute(edge_a, "gy", even)
    edge_b = lax.ppermute(edge_b, "gy", odd)
    corner_a = lax.ppermute(corner_a, ("gx", "gy"), both(next_chip, even))
    corner_b = lax.ppermute(corner_b, ("gx", "gy"), both(next_chip, odd))
    edge_a, edge_b, corner_a, corner_b = lax.optimization_barrier((edge_a, edge_b, corner_a, corner_b))
    edgep_a = lax.ppermute(edge_a, "gx", on_chip)
    edgep_b = lax.ppermute(edge_b, "gx", on_chip)

    flows, side_a, side_b, *state = call(
        rk_kernel,
        [(4, ROWS, WIDE)] + [(ROWS, 128)] * 2 + [(2, ROWS * LEV, 128)] * 3,
        [(3, 24, LEV, WIDE), (3, 16, LEV, WIDE), (3, 12, LEV, WIDE)]
        + [(24, 8, WIDE), (3, ROWS, WIDE), (2, ROWS, WIDE), (2, LEV, WIDE)],
        ins=9 + CHUNKS,
    )(scalars, st, stp, edge_a, edge_b, edgep_a, edgep_b, *main, corner_a, corner_b, plane)
    side_a = lax.ppermute(side_a, "gy", even)
    side_b = lax.ppermute(side_b, "gy", odd)
    flows = call(widen_kernel, [(4, ROWS, WIDE)], ins=3)(scalars, flows, side_a, side_b)[0]
    far = lax.ppermute(flows, "gx", far_chip)
    pair = lax.ppermute(flows, "gx", on_chip)
    remote = lax.ppermute(jnp.stack([flows, pair]), "gx", next_chip)
    remote, far = lax.optimization_barrier((remote, far))
    remote_pair = lax.ppermute(remote, "gx", on_chip)
    state = [field.reshape(2, LEV, ROWS, 128) for field in state]
    east, north, salt, level = call(
        solve_kernel,
        [(LEV, ROWS, COLS)] * 3 + [(ROWS, COLS)],
        [(4, 56, WIDE)] + [(2, LEV, ROWS, 128)] * 2 + [pltpu.SemaphoreType.DMA((18,))],
        ins=8,
        away=3,
    )(scalars, flows, pair, remote, remote_pair, far, *state)
    return east, north, salt, level


def solution(mesh):
    cube = P(None, "gx", "gy")
    flat = P("gx", "gy")
    return jax.shard_map(
        local,
        mesh=mesh,
        in_specs=(cube, cube, cube, flat, flat, flat, flat),
        out_specs=(cube, cube, cube, flat),
        check_vma=False,
    )
```

```python
import jax
import jax.numpy as jnp
from jax import lax
from jax.experimental import pallas as pl
from jax.experimental.pallas import tpu as pltpu
from jax.sharding import PartitionSpec as P

ITERS = 16
TIME_STEP = 0.2
CORIOLIS = 0.3
PRESS_COEF = 0.05
VISCOSITY = 0.1
DIFFUSIVITY = 0.1
SIGMA_SHIFT = 0.25
CHEB_CENTER = 3.625
CHEB_HALF = 3.375
DIVERGENCE_COEF = 8.0

LEV = 48
ROWS = 8
COLS = 256
EXT = 128
WIDE = COLS + EXT
HALO = 6
SIZES = (48,)
CHUNKS = len(SIZES)
STARTS = tuple(sum(SIZES[:c]) for c in range(CHUNKS))
TILES = LEV // 8
SLOT = 25
SLOTS = 5
EDGE_TILES = -(-3 * ROWS // SLOTS)
CORNER_TILES = -(-3 * HALO // SLOTS)
F32 = jnp.float32


def cheb_table(count):
    first = CHEB_CENTER / CHEB_HALF
    ratio = 1.0 / first
    keeps = []
    gains = []
    for index in range(count):
        ratio_next = 1.0 / (2.0 * first - ratio)
        keeps.append(ratio_next * ratio)
        gains.append(2.0 * ratio_next / CHEB_HALF)
        ratio = ratio_next
    return (keeps, gains)


def lanes(shape):
    return lax.broadcasted_iota(jnp.int32, shape, len(shape) - 1)


def place(low, high, units, slot):
    left, right = units
    lane = lanes(low.shape)
    here = (lane >= SLOT * slot) & (lane < SLOT * slot + SLOT)
    low = low if slot == 0 else pltpu.roll(low, SLOT * slot, 1)
    high = pltpu.roll(high, SLOT * slot + SLOT, 1)
    return jnp.where(here, low, left), jnp.where(here, high, right)


def unpack(high, low, slot):
    lane = lanes(high.shape)
    high = high if slot == 0 else pltpu.roll(high, 128 - SLOT * slot, 1)
    low = pltpu.roll(low, 128 - SLOT - SLOT * slot, 1)
    return jnp.where(lane < SLOT, high, jnp.where(lane >= 128 - SLOT, low, 0.0))


def ordered(first, second, flag):
    odd = jnp.full(first.shape, flag, jnp.int32) == 1
    return jnp.where(odd, second, first), jnp.where(odd, first, second)


def pack_kernel(sc, u, v, s, wet, act, surf, depth, edge_a, edge_b, st, plane, *rest):
    buffers, sems = rest[:-1], rest[-1]
    north_odd = sc[2]
    sources = (wet, act, surf, depth, u, v, s)
    copies = [pltpu.make_async_copy(a, b, sems.at[i]) for i, (a, b) in enumerate(zip(sources, buffers))]
    for copy in copies:
        copy.start()
    for copy in copies[:4]:
        copy.wait()
    wet, act, surf, depth, *cubes = buffers
    count = (act[...] * wet[...]).astype(F32)
    plane[0] = surf[...]
    plane[1] = count
    plane[2] = depth[...]
    for f in range(3):
        copies[4 + f].wait()
        for lev in range(LEV):
            tile = jnp.where(count > lev, cubes[f][lev], 0.0)
            spot = 8 * (lev % TILES) + lev // TILES
            for h in range(2):
                st[pl.ds((2 * f + h) * ROWS * LEV + spot, ROWS, stride=LEV), :] = tile[:, h * 128 : (h + 1) * 128]
    for h in range(2):
        at = 6 * ROWS * LEV + 8 * h
        st[at : at + 8, :] = count[:, 128 * h : 128 * h + 128]
    pack_columns(st, EDGE_TILES, ROWS, 0, edge_a, edge_b, north_odd)
    blank = jnp.zeros((LEV, 128), F32)
    units = (blank[:ROWS], blank[:ROWS])
    for slot, field in enumerate((surf[...], count, depth[...])):
        units = place(field[:, :128], field[:, 128:], units, slot)
    left, right = ordered(*units, north_odd)
    edge_b[EDGE_TILES * LEV :, :] = left
    edge_a[EDGE_TILES * LEV :, :] = right


def pack_columns(st, tiles, rows, first, a, b, north_odd):
    blank = jnp.zeros((LEV, 128), F32)
    for g in range(tiles):
        units = (blank, blank)
        for slot in range(min(SLOTS, 3 * rows - SLOTS * g)):
            f, r = divmod(SLOTS * g + slot, rows)
            low = pl.multiple_of((2 * f * ROWS + first + r) * LEV, 8)
            high = pl.multiple_of(((2 * f + 1) * ROWS + first + r) * LEV, 8)
            units = place(st[pl.ds(low, LEV), :], st[pl.ds(high, LEV), :], units, slot)
        b[g * LEV : g * LEV + LEV, :], a[g * LEV : g * LEV + LEV, :] = ordered(*units, north_odd)


def remote_kernel(sc, stp, main, corner_a, corner_b):
    base = 2 * (1 - sc[1])
    north_odd = sc[2]
    for f in range(3):
        for h in range(2):
            start = pl.multiple_of(((2 * f + h) * ROWS + base) * LEV, 8)
            at = (2 * f + h) * HALO * LEV
            main[at : at + HALO * LEV, :] = stp[pl.ds(start, HALO * LEV), :]
    main[6 * HALO * LEV :, :] = stp[6 * ROWS * LEV :, :]
    pack_columns(stp, CORNER_TILES, HALO, base, corner_a, corner_b, north_odd)
    blank = jnp.zeros((ROWS, 128), F32)
    at = 6 * ROWS * LEV
    units = place(stp[at : at + 8, :], stp[at + 8 : at + 16, :], (blank, blank), 1)
    corner_b[CORNER_TILES * LEV :, :], corner_a[CORNER_TILES * LEV :, :] = ordered(*units, north_odd)


def shifts(q):
    return (
        pltpu.roll(q, WIDE - 1, 1),
        pltpu.roll(q, 1, 1),
        pltpu.roll(q, WIDE - 2, 1),
        pltpu.roll(q, 2, 1),
    )


def before(x, sub):
    total = x
    for step in (1, 2, 4):
        total = total + jnp.where(sub >= step, pltpu.roll(total, step, 0), 0.0)
    return total - x


def rk_kernel(sc, st, stp, edge_a, edge_b, edgep_a, edgep_b, *rest):
    mains = rest[:CHUNKS]
    corner_a, corner_b, plane, flows, east, north, salt, ext, one, two, counts, flat, remote, runs = rest[CHUNKS:]
    core = sc[1]
    north_odd = sc[2]
    beside = 16 * (1 - core)
    beyond = 2 + 14 * core
    for source, first in ((st, ROWS), (stp, beside)):
        for f in range(3):
            for r in range(ROWS):
                for h in range(2):
                    at = ((2 * f + h) * ROWS + r) * LEV
                    ext[f, first + r, :, h * 128 : (h + 1) * 128] = source[at : at + LEV, :]
    for f in range(3):
        for j in range(HALO):
            for h in range(2):
                for main, levels, lev0 in zip(mains, SIZES, STARTS):
                    at = ((2 * f + h) * HALO + j) * levels
                    ext[f, beyond + j, lev0 : lev0 + levels, h * 128 : (h + 1) * 128] = main[at : at + levels, :]
    for tiles, rows, first, a, b in (
        (EDGE_TILES, ROWS, ROWS, edge_a, edge_b),
        (EDGE_TILES, ROWS, beside, edgep_a, edgep_b),
        (CORNER_TILES, HALO, beyond, corner_a, corner_b),
    ):
        for g in range(tiles):
            here = slice(g * LEV, g * LEV + LEV)
            high, low = ordered(a[here, :], b[here, :], north_odd)
            for slot in range(min(SLOTS, 3 * rows - SLOTS * g)):
                f, r = divmod(SLOTS * g + slot, rows)
                ext[f, first + r, :, COLS:] = unpack(high, low, slot)

    def beyond_plane(tiles, a, b, slot):
        high, low = ordered(a[tiles * LEV :, :], b[tiles * LEV :, :], north_odd)
        return unpack(high, low, slot)

    for f in range(3):
        flat[f, :, :COLS] = plane[f]
        flat[f, :, COLS:] = beyond_plane(EDGE_TILES, edge_a, edge_b, f)
    remote[0, :, COLS:] = beyond_plane(EDGE_TILES, edgep_a, edgep_b, 1)
    remote[1, :, COLS:] = beyond_plane(CORNER_TILES, corner_a, corner_b, 1)
    for h in range(2):
        at = 6 * ROWS * LEV + 8 * h
        remote[0, :, h * 128 : (h + 1) * 128] = stp[at : at + 8, :]
        at = 6 * HALO * SIZES[0] + 8 * h
        remote[1, :, h * 128 : (h + 1) * 128] = mains[0][at : at + 8, :]
    for r in range(ROWS):
        counts[ROWS + r] = jnp.broadcast_to(flat[1, r : r + 1, :], (8, WIDE))
        counts[beside + r] = jnp.broadcast_to(remote[0, r : r + 1, :], (8, WIDE))
    for j in range(HALO):
        counts[beyond + j] = jnp.broadcast_to(remote[1, pl.ds(2 * (1 - core) + j, 1), :], (8, WIDE))

    sub = lax.broadcasted_iota(jnp.int32, (8, WIDE), 0)

    def stage(source, lead, rows, inset, weight, scale, write, base=None):
        press = PRESS_COEF * scale / 12.0

        def twelve(ahead, behind, ahead2, behind2):
            return 8.0 * (ahead - behind) - (ahead2 - behind2)

        def row(o, _):
            count = counts[o + inset]
            total_x = jnp.zeros((8, WIDE), F32)
            total_y = jnp.zeros((8, WIDE), F32)
            for t in range(TILES):
                here = slice(8 * t, 8 * t + 8)
                back2, back, q, fore, fore2 = [source[2, o + lead + k, here, :] for k in range(5)]
                right, left, right2, left2 = shifts(q)
                grad_x = twelve(fore, back, fore2, back2)
                grad_y = twelve(right, left, right2, left2)
                around = (fore + back) + (right + left)
                total_x = total_x + grad_x
                total_y = total_y + grad_y
                runs[0, here, :] = total_x
                runs[1, here, :] = total_y
                advect = (scale / 12.0) * (
                    source[0, o + lead + 2, here, :] * grad_x + source[1, o + lead + 2, here, :] * grad_y
                )
                value = (weight - 4.0 * VISCOSITY * scale) * q + (VISCOSITY * scale * around - advect)
                if base:
                    value = value + base * ext[2, o + inset, here, :]
                keep = count > (TILES * sub + t).astype(F32)
                write(o, t, 2, jnp.where(keep, value, 0.0))
            above_x = before(total_x, sub)
            above_y = before(total_y, sub)
            for t in range(TILES):
                here = slice(8 * t, 8 * t + 8)
                u = source[0, o + lead + 2, here, :]
                v = source[1, o + lead + 2, here, :]
                us = (scale / 12.0) * u
                vs = (scale / 12.0) * v
                keep = count > (TILES * sub + t).astype(F32)
                for f in range(2):
                    q = source[f, o + lead + 2, here, :]
                    back2, back = source[f, o + lead, here, :], source[f, o + lead + 1, here, :]
                    fore, fore2 = source[f, o + lead + 3, here, :], source[f, o + lead + 4, here, :]
                    right, left, right2, left2 = shifts(q)
                    advect = us * twelve(fore, back, fore2, back2) + vs * twelve(right, left, right2, left2)
                    around = (fore + back) + (right + left)
                    value = (weight - 4.0 * VISCOSITY * scale) * q + (VISCOSITY * scale * around - advect)
                    if f == 0:
                        value = value + (CORIOLIS * scale * v - press * (runs[0, here, :] + above_x))
                    if f == 1:
                        value = value - (CORIOLIS * scale * u + press * (runs[1, here, :] + above_y))
                    if base:
                        value = value + base * ext[f, o + inset, here, :]
                    write(o, t, f, jnp.where(keep, value, 0.0))
            return 0

        lax.fori_loop(0, rows, row, 0, unroll=4)

    def write1(o, t, f, value):
        one[f, o, 8 * t : 8 * t + 8, :] = value

    def write2(o, t, f, value):
        two[f, o, 8 * t : 8 * t + 8, :] = value

    partial = {}

    def write3(o, t, f, value):
        out = (east, north, salt)[f]
        for h in range(2):
            out[h, pl.ds(ROWS * t + o, 8, stride=ROWS * TILES), :] = value[:, h * 128 : (h + 1) * 128]
        if f < 2:
            partial[f] = partial[f] + value if t else value
            if t == TILES - 1:
                flows[f, pl.ds(o, 1), :] = jnp.sum(partial[f], axis=0, keepdims=True)

    stage(ext, 2, 16, 4, 1.0, TIME_STEP, write1)
    stage(one, 0, 12, 6, 0.25, 0.25 * TIME_STEP, write2, 0.75)
    stage(two, 0, 8, 8, 2.0 / 3.0, 2.0 / 3.0 * TIME_STEP, write3, 1.0 / 3.0)
    for f in range(2):
        flows[f] = flat[2] * (flows[f] * (1.0 / LEV))
        flows[2 + f] = flat[f]


def solve_kernel(sc, mine, pair, remote, remote_pair, far, u, v, s, east, north, salt, level, wide, out_u, out_v, sems):
    core = sc[1]
    halves = [slice(128 * h, 128 * h + 128) for h in range(2)]
    copies = [pltpu.make_async_copy(s.at[h], salt.at[:, :, halves[h]], sems.at[h]) for h in range(2)]
    for copy in copies:
        copy.start()
    wide[:, 24:32, :] = mine[...]
    for slot, block in (
        (4 - 2 * core, pair[...]),
        (2 + 2 * core, remote[1]),
        (1 + 4 * core, remote[0]),
        (5 - 4 * core, remote_pair[1]),
        (6 - 6 * core, remote_pair[0]),
        (6 * core, far[...]),
    ):
        wide[:, pl.ds(pl.multiple_of(8 * slot, 8), 8), :] = block
    high = 48
    near = slice(4, 52)
    own = slice(20, 28)

    def up(x):
        return pltpu.roll(x, high - 1, 0)

    def down(x):
        return pltpu.roll(x, 1, 0)

    def right(x):
        return pltpu.roll(x, WIDE - 1, 1)

    def left(x):
        return pltpu.roll(x, 1, 1)

    wet = jnp.where(wide[3, near, :] > 0.0, 1.0, 0.0)
    sixth = wet * (1.0 / 6.0)
    middle = wet * (SIGMA_SHIFT + 20.0 / 6.0) + (1.0 - wet)

    def less(res, e):
        w = wet * e
        rows = up(w) + down(w)
        mix = 4.0 * w + rows
        return (res - middle * e) + sixth * (4.0 * rows + (right(mix) + left(mix)))

    flow_east = wide[0, near, :]
    flow_north = wide[1, near, :]
    x = wide[2, near, :]
    div = 0.5 * (up(flow_east) - down(flow_east)) + 0.5 * (right(flow_north) - left(flow_north))
    res = less(wet * (SIGMA_SHIFT * x - DIVERGENCE_COEF * div), x)
    step = res * (1.0 / CHEB_CENTER)
    keeps, gains = cheb_table(ITERS)
    for index in range(ITERS):
        x = x + step
        if index < ITERS - 1:
            res = less(res, step)
            step = keeps[index] * step + gains[index] * res
    slope_east = (0.5 * (up(x) - down(x)))[own, :COLS]
    slope_north = (0.5 * (right(x) - left(x)))[own, :COLS]
    level[...] = x[own, :COLS]
    count = mine[3][:, :COLS]
    part = LEV // 4
    for first in range(0, LEV, part):
        for lev in range(first, first + part):
            keep = count > lev
            for h, cols in enumerate(halves):
                out_u[h, lev] = jnp.where(keep[:, cols], u[h, lev] - slope_east[:, cols], 0.0)
                out_v[h, lev] = jnp.where(keep[:, cols], v[h, lev] - slope_north[:, cols], 0.0)
        some = slice(first, first + part)
        for source, target in ((out_u, east), (out_v, north)):
            for h, cols in enumerate(halves):
                copy = pltpu.make_async_copy(source.at[h, some], target.at[some, :, cols], sems.at[len(copies)])
                copy.start()
                copies.append(copy)
    for copy in copies:
        copy.wait()


def swap(pairs):
    return [p for a, b in pairs for p in ((a, b), (b, a))]


def call(body, outs, scratch=(), ins=0, space=pltpu.VMEM, away=0):
    vmem = pl.BlockSpec(memory_space=pltpu.VMEM)
    smem = pl.BlockSpec(memory_space=pltpu.SMEM)
    return pl.pallas_call(
        body,
        out_shape=[jax.ShapeDtypeStruct(s, F32) for s in outs],
        in_specs=[smem] + [pl.BlockSpec(memory_space=space)] * ins,
        out_specs=[pl.BlockSpec(memory_space=pltpu.HBM)] * away + [vmem] * (len(outs) - away),
        scratch_shapes=[pltpu.VMEM(s, F32) if isinstance(s, tuple) else s for s in scratch],
        compiler_params=pltpu.CompilerParams(vmem_limit_bytes=16 * 1024 * 1024),
    )


def local(u, v, s, surface, depth, wet, active):
    gx = lax.axis_size("gx")
    gy = lax.axis_size("gy")
    me = lax.axis_index("gx")
    scalars = jnp.stack([me, me % 2, lax.axis_index("gy") % 2]).astype(jnp.int32)
    on_chip = swap([(i, i + 1) for i in range(0, gx, 2)])
    next_chip = [(i, i + 2) for i in range(0, gx - 2, 2)] + [(i, i - 2) for i in range(3, gx, 2)]
    far_chip = swap([(i, i + 3) for i in range(1, gx - 3, 2)])
    even = swap([(i, i + 1) for i in range(0, gy, 2)])
    odd = swap([(i, i + 1) for i in range(1, gy - 1, 2)])

    def both(first, second):
        return [(i * gy + j, k * gy + l) for i, k in first for j, l in second]

    edge_a, edge_b, st, plane = call(
        pack_kernel,
        [(EDGE_TILES * LEV + 8, 128)] * 2 + [(6 * ROWS * LEV + 16, 128), (3, ROWS, COLS)],
        [pltpu.VMEM((ROWS, COLS), jnp.int32)] * 2
        + [(ROWS, COLS)] * 2
        + [(LEV, ROWS, COLS)] * 3
        + [pltpu.SemaphoreType.DMA((7,))],
        ins=7,
        space=pltpu.HBM,
    )(scalars, *(pltpu.with_memory_space_constraint(x, pltpu.HBM) for x in (u, v, s, wet, active, surface, depth)))
    stp = lax.ppermute(st, "gx", on_chip)
    main, corner_a, corner_b = call(
        remote_kernel,
        [(6 * HALO * LEV + 16, 128)] + [(CORNER_TILES * LEV + 8, 128)] * 2,
        ins=1,
    )(scalars, stp)
    main = [lax.ppermute(main, "gx", next_chip)]
    edge_a = lax.ppermute(edge_a, "gy", even)
    edge_b = lax.ppermute(edge_b, "gy", odd)
    corner_a = lax.ppermute(corner_a, ("gx", "gy"), both(next_chip, even))
    corner_b = lax.ppermute(corner_b, ("gx", "gy"), both(next_chip, odd))
    edge_a, edge_b, corner_a, corner_b = lax.optimization_barrier((edge_a, edge_b, corner_a, corner_b))
    edgep_a = lax.ppermute(edge_a, "gx", on_chip)
    edgep_b = lax.ppermute(edge_b, "gx", on_chip)

    flows, *state = call(
        rk_kernel,
        [(4, ROWS, WIDE)] + [(2, ROWS * LEV, 128)] * 3,
        [(3, 24, LEV, WIDE), (3, 16, LEV, WIDE), (3, 12, LEV, WIDE)]
        + [(24, 8, WIDE), (3, ROWS, WIDE), (2, ROWS, WIDE), (2, LEV, WIDE)],
        ins=9 + CHUNKS,
    )(scalars, st, stp, edge_a, edge_b, edgep_a, edgep_b, *main, corner_a, corner_b, plane)
    far = lax.ppermute(flows, "gx", far_chip)
    pair = lax.ppermute(flows, "gx", on_chip)
    remote = lax.ppermute(jnp.stack([flows, pair]), "gx", next_chip)
    remote, far = lax.optimization_barrier((remote, far))
    remote_pair = lax.ppermute(remote, "gx", on_chip)
    state = [field.reshape(2, LEV, ROWS, 128) for field in state]
    east, north, salt, level = call(
        solve_kernel,
        [(LEV, ROWS, COLS)] * 3 + [(ROWS, COLS)],
        [(4, 56, WIDE)] + [(2, LEV, ROWS, 128)] * 2 + [pltpu.SemaphoreType.DMA((18,))],
        ins=8,
        away=3,
    )(scalars, flows, pair, remote, remote_pair, far, *state)
    return east, north, salt, level


def solution(mesh):
    cube = P(None, "gx", "gy")
    flat = P("gx", "gy")
    return jax.shard_map(
        local,
        mesh=mesh,
        in_specs=(cube, cube, cube, flat, flat, flat, flat),
        out_specs=(cube, cube, cube, flat),
        check_vma=False,
    )
```

```python
import functools

import jax
import jax.numpy as jnp
from jax import lax
from jax.experimental import pallas as pl
from jax.experimental.pallas import tpu as pltpu
from jax.sharding import PartitionSpec as P

ITERS = 16
TIME_STEP = 0.2
CORIOLIS = 0.3
PRESS_COEF = 0.05
VISCOSITY = 0.1
DIFFUSIVITY = 0.1
SIGMA_SHIFT = 0.25
CHEB_CENTER = 3.625
CHEB_HALF = 3.375
DIVERGENCE_COEF = 8.0

LEV = 48
ROWS = 8
COLS = 256
EXT = 128
WIDE = COLS + EXT
HALO = 6
SIZES = (32, 16)
CHUNKS = len(SIZES)
STARTS = tuple(sum(SIZES[:c]) for c in range(CHUNKS))
SLOT = 25
SLOTS = 5
EDGE_TILES = -(-3 * ROWS // SLOTS)
CORNER_TILES = -(-3 * HALO // SLOTS)
F32 = jnp.float32


def cheb_table(count):
    first = CHEB_CENTER / CHEB_HALF
    ratio = 1.0 / first
    keeps = []
    gains = []
    for index in range(count):
        ratio_next = 1.0 / (2.0 * first - ratio)
        keeps.append(ratio_next * ratio)
        gains.append(2.0 * ratio_next / CHEB_HALF)
        ratio = ratio_next
    return (keeps, gains)


def lanes(shape):
    return lax.broadcasted_iota(jnp.int32, shape, len(shape) - 1)


def place(low, high, units, slot):
    left, right = units
    lane = lanes(low.shape)
    here = (lane >= SLOT * slot) & (lane < SLOT * slot + SLOT)
    low = low if slot == 0 else pltpu.roll(low, SLOT * slot, 1)
    high = pltpu.roll(high, SLOT * slot + SLOT, 1)
    return jnp.where(here, low, left), jnp.where(here, high, right)


def unpack(high, low, slot):
    lane = lanes(high.shape)
    high = high if slot == 0 else pltpu.roll(high, 128 - SLOT * slot, 1)
    low = pltpu.roll(low, 128 - SLOT - SLOT * slot, 1)
    return jnp.where(lane < SLOT, high, jnp.where(lane >= 128 - SLOT, low, 0.0))


def ordered(first, second, flag):
    odd = jnp.full(first.shape, flag, jnp.int32) == 1
    return jnp.where(odd, second, first), jnp.where(odd, first, second)


def pack_kernel(sc, u, v, s, wet, act, surf, depth, edge_a, edge_b, corner_a, corner_b, *rest):
    mains = rest[:CHUNKS]
    st, plane = rest[CHUNKS : CHUNKS + 2]
    buffers = rest[CHUNKS + 2 : CHUNKS + 9]
    sems = rest[CHUNKS + 9]
    core = sc[1]
    north_odd = sc[2]
    sources = (wet, act, surf, depth, u, v, s)
    copies = [pltpu.make_async_copy(a, b, sems.at[i]) for i, (a, b) in enumerate(zip(sources, buffers))]
    for copy in copies:
        copy.start()
    for copy in copies[:4]:
        copy.wait()
    wet, act, surf, depth, *cubes = buffers
    count = (act[...] * wet[...]).astype(F32)
    plane[0] = surf[...]
    plane[1] = count
    plane[2] = depth[...]
    for f in range(3):
        copies[4 + f].wait()
        for lev in range(LEV):
            tile = jnp.where(count > lev, cubes[f][lev], 0.0)
            for h in range(2):
                st[pl.ds((2 * f + h) * ROWS * LEV + lev, ROWS, stride=LEV), :] = tile[:, h * 128 : (h + 1) * 128]
    base = 2 * core
    for c in range(CHUNKS):
        levels = SIZES[c]
        for f in range(3):
            for j in range(HALO):
                for h in range(2):
                    start = pl.multiple_of(((2 * f + h) * ROWS + base + j) * LEV + STARTS[c], 8)
                    at = ((2 * f + h) * HALO + j) * levels
                    mains[c][at : at + levels, :] = st[pl.ds(start, levels), :]
    for h in range(2):
        at = 6 * HALO * SIZES[0] + 8 * h
        mains[0][at : at + 8, :] = count[:, 128 * h : 128 * h + 128]
        at = 6 * ROWS * LEV + 8 * h
        st[at : at + 8, :] = count[:, 128 * h : 128 * h + 128]
    blank = jnp.zeros((LEV, 128), F32)
    for tiles, rows, first, a, b in (
        (EDGE_TILES, ROWS, 0, edge_a, edge_b),
        (CORNER_TILES, HALO, base, corner_a, corner_b),
    ):
        for g in range(tiles):
            units = (blank, blank)
            for slot in range(min(SLOTS, 3 * rows - SLOTS * g)):
                f, r = divmod(SLOTS * g + slot, rows)
                low = pl.multiple_of((2 * f * ROWS + first + r) * LEV, 8)
                high = pl.multiple_of(((2 * f + 1) * ROWS + first + r) * LEV, 8)
                units = place(st[pl.ds(low, LEV), :], st[pl.ds(high, LEV), :], units, slot)
            b[g * LEV : g * LEV + LEV, :], a[g * LEV : g * LEV + LEV, :] = ordered(*units, north_odd)
    units = (blank[:ROWS], blank[:ROWS])
    for slot, field in enumerate((surf[...], count, depth[...])):
        units = place(field[:, :128], field[:, 128:], units, slot)
    left, right = ordered(*units, north_odd)
    for tiles, a, b in ((EDGE_TILES, edge_a, edge_b), (CORNER_TILES, corner_a, corner_b)):
        b[tiles * LEV :, :] = left
        a[tiles * LEV :, :] = right


def shifts(q):
    return (
        pltpu.roll(q, WIDE - 1, 1),
        pltpu.roll(q, 1, 1),
        pltpu.roll(q, WIDE - 2, 1),
        pltpu.roll(q, 2, 1),
    )


def slope(ahead, behind, ahead2, behind2):
    return (8.0 / 12.0) * (ahead - behind) - (1.0 / 12.0) * (ahead2 - behind2)


def running(x, sub):
    for step in (1, 2, 4):
        x = x + jnp.where(sub >= step, pltpu.roll(x, step, 0), 0.0)
    return x


def rk_kernel(chunk, sc, st, stp, edge_a, edge_b, edgep_a, edgep_b, main, main0, corner_a, corner_b, plane, *rest):
    levels = SIZES[chunk]
    if chunk:
        carry_in, sums_in = rest[:2]
        rest = rest[2:]
    if chunk == CHUNKS - 1:
        flows, rest = rest[0], rest[1:]
    out, carry, sums, ext, one, two, counts, flat, remote = rest
    core = sc[1]
    north_odd = sc[2]
    lev0 = STARTS[chunk]
    beside = 16 * (1 - core)
    beyond = 2 + 14 * core
    for source, first in ((st, ROWS), (stp, beside)):
        for f in range(3):
            for r in range(ROWS):
                for h in range(2):
                    at = ((2 * f + h) * ROWS + r) * LEV + lev0
                    ext[f, first + r, :, h * 128 : (h + 1) * 128] = source[at : at + levels, :]
    for f in range(3):
        for j in range(HALO):
            for h in range(2):
                at = ((2 * f + h) * HALO + j) * levels
                ext[f, beyond + j, :, h * 128 : (h + 1) * 128] = main[at : at + levels, :]
    for tiles, rows, first, a, b in (
        (EDGE_TILES, ROWS, ROWS, edge_a, edge_b),
        (EDGE_TILES, ROWS, beside, edgep_a, edgep_b),
        (CORNER_TILES, HALO, beyond, corner_a, corner_b),
    ):
        for g in range(tiles):
            here = slice(g * LEV + lev0, g * LEV + lev0 + levels)
            high, low = ordered(a[here, :], b[here, :], north_odd)
            for slot in range(min(SLOTS, 3 * rows - SLOTS * g)):
                f, r = divmod(SLOTS * g + slot, rows)
                ext[f, first + r, :, COLS:] = unpack(high, low, slot)

    def beyond_plane(tiles, a, b, slot):
        high, low = ordered(a[tiles * LEV :, :], b[tiles * LEV :, :], north_odd)
        return unpack(high, low, slot)

    for f in range(3):
        flat[f, :, :COLS] = plane[f]
        flat[f, :, COLS:] = beyond_plane(EDGE_TILES, edge_a, edge_b, f)
    remote[0, :, COLS:] = beyond_plane(EDGE_TILES, edgep_a, edgep_b, 1)
    remote[1, :, COLS:] = beyond_plane(CORNER_TILES, corner_a, corner_b, 1)
    for h in range(2):
        at = 6 * ROWS * LEV + 8 * h
        remote[0, :, h * 128 : (h + 1) * 128] = stp[at : at + 8, :]
        at = 6 * HALO * SIZES[0] + 8 * h
        remote[1, :, h * 128 : (h + 1) * 128] = main0[at : at + 8, :]
    for r in range(ROWS):
        counts[ROWS + r] = jnp.broadcast_to(flat[1, r : r + 1, :], (8, WIDE))
        counts[beside + r] = jnp.broadcast_to(remote[0, r : r + 1, :], (8, WIDE))
    for j in range(HALO):
        counts[beyond + j] = jnp.broadcast_to(remote[1, pl.ds(2 * (1 - core) + j, 1), :], (8, WIDE))

    sub = lax.broadcasted_iota(jnp.int32, (8, WIDE), 0)

    def stage(source, lead, rows, inset, write, slot):
        def row(o, _):
            count = counts[o + inset]
            if chunk:
                sum_x = jnp.broadcast_to(carry_in[pl.ds(slot + 2 * o, 1), :], (8, WIDE))
                sum_y = jnp.broadcast_to(carry_in[pl.ds(slot + 2 * o + 1, 1), :], (8, WIDE))
            else:
                sum_x = jnp.zeros((8, WIDE), F32)
                sum_y = jnp.zeros((8, WIDE), F32)
            for t in range(levels // 8):
                here = slice(8 * t, 8 * t + 8)
                mid = []
                dxs = []
                dys = []
                laps = []
                for f in range(3):
                    q = source[f, o + lead + 2, here, :]
                    back2, back = source[f, o + lead, here, :], source[f, o + lead + 1, here, :]
                    fore, fore2 = source[f, o + lead + 3, here, :], source[f, o + lead + 4, here, :]
                    right, left, right2, left2 = shifts(q)
                    mid.append(q)
                    dxs.append(slope(fore, back, fore2, back2))
                    dys.append(slope(right, left, right2, left2))
                    laps.append((fore + back) + (right + left) - 4.0 * q)
                press_x = running(dxs[2], sub) + sum_x
                press_y = running(dys[2], sub) + sum_y
                sum_x = jnp.broadcast_to(press_x[7:8, :], (8, WIDE))
                sum_y = jnp.broadcast_to(press_y[7:8, :], (8, WIDE))
                u, v, _s = mid
                rates = [VISCOSITY * laps[f] - (u * dxs[f] + v * dys[f]) for f in range(3)]
                rates[0] = rates[0] + (CORIOLIS * v - PRESS_COEF * press_x)
                rates[1] = rates[1] - (CORIOLIS * u + PRESS_COEF * press_y)
                keep = count > (sub + (lev0 + 8 * t)).astype(F32)
                write(o, here, t, mid, [jnp.where(keep, r, 0.0) for r in rates])
            carry[pl.ds(slot + 2 * o, 1), :] = sum_x[:1, :]
            carry[pl.ds(slot + 2 * o + 1, 1), :] = sum_y[:1, :]
            return 0

        lax.fori_loop(0, rows, row, 0, unroll=max(1, min(4, 64 // levels)))

    def write1(o, here, t, mid, rates):
        for f in range(3):
            one[f, o, here, :] = mid[f] + TIME_STEP * rates[f]

    def write2(o, here, t, mid, rates):
        for f in range(3):
            first = ext[f, o + 6, here, :]
            two[f, o, here, :] = 0.75 * first + (0.25 * mid[f] + (0.25 * TIME_STEP) * rates[f])

    def write3(o, here, t, mid, rates):
        for f in range(3):
            first = ext[f, o + 8, here, :]
            value = (1.0 / 3.0) * first + ((2.0 / 3.0) * mid[f] + (2.0 / 3.0 * TIME_STEP) * rates[f])
            at = pl.multiple_of(o * levels + 8 * t, 8)
            for h in range(2):
                out[f, h, pl.ds(at, 8), :] = value[:, h * 128 : (h + 1) * 128]
            if f < 2:
                if t == 0:
                    sums[f, o] = value + sums_in[f, o] if chunk else value
                else:
                    sums[f, o] = sums[f, o] + value

    stage(ext, 2, 16, 4, write1, 0)
    stage(one, 0, 12, 6, write2, 32)
    stage(two, 0, 8, 8, write3, 56)
    if chunk == CHUNKS - 1:
        for f in range(2):
            for o in range(ROWS):
                flows[f, o : o + 1, :] = jnp.sum(sums[f, o], axis=0, keepdims=True)
            flows[f] = flat[2] * (flows[f] * (1.0 / LEV))
            flows[2 + f] = flat[f]


def solve_kernel(sc, mine, pair, remote, remote_pair, far, *rest):
    states = rest[:CHUNKS]
    east, north, salt, level = rest[CHUNKS : CHUNKS + 4]
    wide = rest[CHUNKS + 4]
    core = sc[1]
    wide[:, 24:32, :] = mine[...]
    for slot, block in (
        (4 - 2 * core, pair[...]),
        (2 + 2 * core, remote[0]),
        (1 + 4 * core, remote[1]),
        (5 - 4 * core, remote_pair[0]),
        (6 - 6 * core, remote_pair[1]),
        (6 * core, far[...]),
    ):
        wide[:, pl.ds(pl.multiple_of(8 * slot, 8), 8), :] = block
    high = 56

    def up(x):
        return pltpu.roll(x, high - 1, 0)

    def down(x):
        return pltpu.roll(x, 1, 0)

    def right(x):
        return pltpu.roll(x, WIDE - 1, 1)

    def left(x):
        return pltpu.roll(x, 1, 1)

    wet = jnp.where(wide[3] > 0.0, 1.0, 0.0)
    dry = 1.0 - wet

    def apply(e):
        w = wet * e
        rows = up(w) + down(w)
        mix = 4.0 * w + rows
        sides = right(mix) + left(mix)
        stencil = (20.0 / 6.0) * w - (4.0 / 6.0) * rows - (1.0 / 6.0) * sides
        return wet * (SIGMA_SHIFT * e + stencil) + dry * e

    flow_east = wide[0]
    flow_north = wide[1]
    x = wide[2]
    div = 0.5 * (up(flow_east) - down(flow_east)) + 0.5 * (right(flow_north) - left(flow_north))
    res = wet * (SIGMA_SHIFT * x - DIVERGENCE_COEF * div) - apply(x)
    step = res * (1.0 / CHEB_CENTER)
    keeps, gains = cheb_table(ITERS)
    for index in range(ITERS):
        x = x + step
        if index < ITERS - 1:
            res = res - apply(step)
            step = keeps[index] * step + gains[index] * res
    slope_east = (0.5 * (up(x) - down(x)))[24:32, :COLS]
    slope_north = (0.5 * (right(x) - left(x)))[24:32, :COLS]
    level[...] = x[24:32, :COLS]
    count = mine[3][:, :COLS]
    for lev in range(LEV):
        c = max(i for i in range(CHUNKS) if STARTS[i] <= lev)
        levels = SIZES[c]
        at = lev - STARTS[c]
        keep = count > lev
        for h in range(2):
            cols = slice(h * 128, (h + 1) * 128)
            parts = [states[c][f, h, pl.ds(at, ROWS, stride=levels), :] for f in range(3)]
            east[lev, :, cols] = jnp.where(keep[:, cols], parts[0] - slope_east[:, cols], 0.0)
            north[lev, :, cols] = jnp.where(keep[:, cols], parts[1] - slope_north[:, cols], 0.0)
            salt[lev, :, cols] = parts[2]


def swap(pairs):
    return [p for a, b in pairs for p in ((a, b), (b, a))]


def call(body, outs, scratch=(), ins=0, space=pltpu.VMEM, cost=None):
    vmem = pl.BlockSpec(memory_space=pltpu.VMEM)
    smem = pl.BlockSpec(memory_space=pltpu.SMEM)
    return pl.pallas_call(
        body,
        out_shape=[jax.ShapeDtypeStruct(s, F32) for s in outs],
        in_specs=[smem] + [pl.BlockSpec(memory_space=space)] * ins,
        out_specs=[vmem] * len(outs),
        scratch_shapes=[pltpu.VMEM(s, F32) if isinstance(s, tuple) else s for s in scratch],
        cost_estimate=cost and pl.CostEstimate(flops=cost, transcendentals=0, bytes_accessed=0),
        compiler_params=pltpu.CompilerParams(vmem_limit_bytes=16 * 1024 * 1024),
    )


def local(u, v, s, surface, depth, wet, active):
    gx = lax.axis_size("gx")
    gy = lax.axis_size("gy")
    me = lax.axis_index("gx")
    scalars = jnp.stack([me, me % 2, lax.axis_index("gy") % 2]).astype(jnp.int32)
    on_chip = swap([(i, i + 1) for i in range(0, gx, 2)])
    next_chip = swap([(i, i + 1) for i in range(1, gx - 1, 2)])
    far_chip = swap([(i, i + 3) for i in range(1, gx - 3, 2)])
    even = swap([(i, i + 1) for i in range(0, gy, 2)])
    odd = swap([(i, i + 1) for i in range(1, gy - 1, 2)])

    def both(first, second):
        return [(i * gy + j, k * gy + l) for i, k in first for j, l in second]

    edge_a, edge_b, corner_a, corner_b, *packed = call(
        pack_kernel,
        [(EDGE_TILES * LEV + 8, 128)] * 2
        + [(CORNER_TILES * LEV + 8, 128)] * 2
        + [(6 * HALO * levels + (0 if c else 16), 128) for c, levels in enumerate(SIZES)]
        + [(6 * ROWS * LEV + 16, 128), (3, ROWS, COLS)],
        [pltpu.VMEM((ROWS, COLS), jnp.int32)] * 2
        + [(ROWS, COLS)] * 2
        + [(LEV, ROWS, COLS)] * 3
        + [pltpu.SemaphoreType.DMA((7,))],
        ins=7,
        space=pltpu.HBM,
    )(scalars, *(pltpu.with_memory_space_constraint(x, pltpu.HBM) for x in (u, v, s, wet, active, surface, depth)))
    mains = packed[:CHUNKS]
    st, plane = packed[CHUNKS:]
    stp = lax.ppermute(st, "gx", on_chip)
    main = [lax.ppermute(mains[0], "gx", next_chip)]
    stp, corner_a, corner_b = lax.optimization_barrier((stp, corner_a, corner_b))
    edge_a = lax.ppermute(edge_a, "gy", even)
    edge_b = lax.ppermute(edge_b, "gy", odd)
    corner_a = lax.ppermute(corner_a, ("gx", "gy"), both(next_chip, even))
    corner_b = lax.ppermute(corner_b, ("gx", "gy"), both(next_chip, odd))
    corner_a, corner_b, edge_a, edge_b, *later = lax.optimization_barrier((corner_a, corner_b, edge_a, edge_b, *mains[1:]))
    main += [lax.ppermute(m, "gx", next_chip) for m in later]
    edgep_a = lax.ppermute(edge_a, "gx", on_chip)
    edgep_b = lax.ppermute(edge_b, "gx", on_chip)

    states = []
    tail = []
    for c, levels in enumerate(SIZES):
        *flows, out, carry, sums = call(
            functools.partial(rk_kernel, c),
            [(4, ROWS, WIDE)] * (c == CHUNKS - 1)
            + [(3, 2, ROWS * levels, 128), (72, WIDE), (2, ROWS, 8, WIDE)],
            [(3, 24, levels, WIDE), (3, 16, levels, WIDE), (3, 12, levels, WIDE)]
            + [(24, 8, WIDE), (3, ROWS, WIDE), (2, ROWS, WIDE)],
            ins=11 + len(tail),
        )(scalars, st, stp, edge_a, edge_b, edgep_a, edgep_b, main[c], main[0], corner_a, corner_b, plane, *tail)
        tail = [carry, sums]
        states.append(out)
    flows = flows[0]
    far = lax.ppermute(flows, "gx", far_chip)
    pair = lax.ppermute(flows, "gx", on_chip)
    remote = lax.ppermute(jnp.stack([flows, pair]), "gx", next_chip)
    remote, far = lax.optimization_barrier((remote, far))
    remote_pair = lax.ppermute(remote, "gx", on_chip)
    east, north, salt, level = call(
        solve_kernel,
        [(LEV, ROWS, COLS)] * 3 + [(ROWS, COLS)],
        [(4, 56, WIDE)],
        ins=5 + CHUNKS,
    )(scalars, flows, pair, remote, remote_pair, far, *states)
    return east, north, salt, level


def solution(mesh):
    cube = P(None, "gx", "gy")
    flat = P("gx", "gy")
    return jax.shard_map(
        local,
        mesh=mesh,
        in_specs=(cube, cube, cube, flat, flat, flat, flat),
        out_specs=(cube, cube, cube, flat),
        check_vma=False,
    )
```

```python
import functools

import jax
import jax.numpy as jnp
from jax import lax
from jax.experimental import pallas as pl
from jax.experimental.pallas import tpu as pltpu
from jax.sharding import PartitionSpec as P

ITERS = 16
TIME_STEP = 0.2
CORIOLIS = 0.3
PRESS_COEF = 0.05
VISCOSITY = 0.1
DIFFUSIVITY = 0.1
SIGMA_SHIFT = 0.25
CHEB_CENTER = 3.625
CHEB_HALF = 3.375
DIVERGENCE_COEF = 8.0

LEV = 48
ROWS = 8
COLS = 256
EXT = 128
WIDE = COLS + EXT
HALO = 6
SIZES = (32, 16)
CHUNKS = len(SIZES)
STARTS = tuple(sum(SIZES[:c]) for c in range(CHUNKS))
SLOT = 25
SLOTS = 5
EDGE_TILES = -(-3 * ROWS // SLOTS)
CORNER_TILES = -(-3 * HALO // SLOTS)
F32 = jnp.float32


def cheb_table(count):
    first = CHEB_CENTER / CHEB_HALF
    ratio = 1.0 / first
    keeps = []
    gains = []
    for index in range(count):
        ratio_next = 1.0 / (2.0 * first - ratio)
        keeps.append(ratio_next * ratio)
        gains.append(2.0 * ratio_next / CHEB_HALF)
        ratio = ratio_next
    return (keeps, gains)


def lanes(shape):
    return lax.broadcasted_iota(jnp.int32, shape, len(shape) - 1)


def place(low, high, units, slot):
    left, right = units
    lane = lanes(low.shape)
    here = (lane >= SLOT * slot) & (lane < SLOT * slot + SLOT)
    low = low if slot == 0 else pltpu.roll(low, SLOT * slot, 1)
    high = pltpu.roll(high, SLOT * slot + SLOT, 1)
    return jnp.where(here, low, left), jnp.where(here, high, right)


def unpack(high, low, slot):
    lane = lanes(high.shape)
    high = high if slot == 0 else pltpu.roll(high, 128 - SLOT * slot, 1)
    low = pltpu.roll(low, 128 - SLOT - SLOT * slot, 1)
    return jnp.where(lane < SLOT, high, jnp.where(lane >= 128 - SLOT, low, 0.0))


def ordered(first, second, flag):
    odd = jnp.full(first.shape, flag, jnp.int32) == 1
    return jnp.where(odd, second, first), jnp.where(odd, first, second)


def pack_kernel(sc, u, v, s, wet, act, surf, depth, edge_a, edge_b, corner_a, corner_b, *rest):
    mains = rest[:CHUNKS]
    st, plane = rest[CHUNKS : CHUNKS + 2]
    buffers = rest[CHUNKS + 2 : CHUNKS + 9]
    sems = rest[CHUNKS + 9]
    core = sc[1]
    north_odd = sc[2]
    sources = (wet, act, surf, depth, u, v, s)
    copies = [pltpu.make_async_copy(a, b, sems.at[i]) for i, (a, b) in enumerate(zip(sources, buffers))]
    for copy in copies:
        copy.start()
    for copy in copies[:4]:
        copy.wait()
    wet, act, surf, depth, *cubes = buffers
    count = (act[...] * wet[...]).astype(F32)
    plane[0] = surf[...]
    plane[1] = count
    plane[2] = depth[...]
    for f in range(3):
        copies[4 + f].wait()
        for lev in range(LEV):
            tile = jnp.where(count > lev, cubes[f][lev], 0.0)
            for h in range(2):
                st[pl.ds((2 * f + h) * ROWS * LEV + lev, ROWS, stride=LEV), :] = tile[:, h * 128 : (h + 1) * 128]
    base = 2 * core
    for c in range(CHUNKS):
        levels = SIZES[c]
        for f in range(3):
            for j in range(HALO):
                for h in range(2):
                    start = pl.multiple_of(((2 * f + h) * ROWS + base + j) * LEV + STARTS[c], 8)
                    at = ((2 * f + h) * HALO + j) * levels
                    mains[c][at : at + levels, :] = st[pl.ds(start, levels), :]
    for h in range(2):
        at = 6 * HALO * SIZES[0] + 8 * h
        mains[0][at : at + 8, :] = count[:, 128 * h : 128 * h + 128]
        at = 6 * ROWS * LEV + 8 * h
        st[at : at + 8, :] = count[:, 128 * h : 128 * h + 128]
    blank = jnp.zeros((LEV, 128), F32)
    for tiles, rows, first, a, b in (
        (EDGE_TILES, ROWS, 0, edge_a, edge_b),
        (CORNER_TILES, HALO, base, corner_a, corner_b),
    ):
        for g in range(tiles):
            units = (blank, blank)
            for slot in range(min(SLOTS, 3 * rows - SLOTS * g)):
                f, r = divmod(SLOTS * g + slot, rows)
                low = pl.multiple_of((2 * f * ROWS + first + r) * LEV, 8)
                high = pl.multiple_of(((2 * f + 1) * ROWS + first + r) * LEV, 8)
                units = place(st[pl.ds(low, LEV), :], st[pl.ds(high, LEV), :], units, slot)
            b[g * LEV : g * LEV + LEV, :], a[g * LEV : g * LEV + LEV, :] = ordered(*units, north_odd)
    units = (blank[:ROWS], blank[:ROWS])
    for slot, field in enumerate((surf[...], count, depth[...])):
        units = place(field[:, :128], field[:, 128:], units, slot)
    left, right = ordered(*units, north_odd)
    for tiles, a, b in ((EDGE_TILES, edge_a, edge_b), (CORNER_TILES, corner_a, corner_b)):
        b[tiles * LEV :, :] = left
        a[tiles * LEV :, :] = right


def shifts(q):
    return (
        pltpu.roll(q, WIDE - 1, 1),
        pltpu.roll(q, 1, 1),
        pltpu.roll(q, WIDE - 2, 1),
        pltpu.roll(q, 2, 1),
    )


def slope(ahead, behind, ahead2, behind2):
    return (8.0 / 12.0) * (ahead - behind) - (1.0 / 12.0) * (ahead2 - behind2)


def running(x, sub):
    for step in (1, 2, 4):
        x = x + jnp.where(sub >= step, pltpu.roll(x, step, 0), 0.0)
    return x


def rk_kernel(chunk, sc, st, stp, edge_a, edge_b, edgep_a, edgep_b, main, main0, corner_a, corner_b, plane, *rest):
    levels = SIZES[chunk]
    if chunk:
        carry_in, sums_in = rest[:2]
        rest = rest[2:]
    if chunk == CHUNKS - 1:
        flows, rest = rest[0], rest[1:]
    out, carry, sums, ext, one, two, counts, flat, remote = rest
    core = sc[1]
    north_odd = sc[2]
    lev0 = STARTS[chunk]
    beside = 16 * (1 - core)
    beyond = 2 + 14 * core
    for source, first in ((st, ROWS), (stp, beside)):
        for f in range(3):
            for r in range(ROWS):
                for h in range(2):
                    at = ((2 * f + h) * ROWS + r) * LEV + lev0
                    ext[f, first + r, :, h * 128 : (h + 1) * 128] = source[at : at + levels, :]
    for f in range(3):
        for j in range(HALO):
            for h in range(2):
                at = ((2 * f + h) * HALO + j) * levels
                ext[f, beyond + j, :, h * 128 : (h + 1) * 128] = main[at : at + levels, :]
    for tiles, rows, first, a, b in (
        (EDGE_TILES, ROWS, ROWS, edge_a, edge_b),
        (EDGE_TILES, ROWS, beside, edgep_a, edgep_b),
        (CORNER_TILES, HALO, beyond, corner_a, corner_b),
    ):
        for g in range(tiles):
            here = slice(g * LEV + lev0, g * LEV + lev0 + levels)
            high, low = ordered(a[here, :], b[here, :], north_odd)
            for slot in range(min(SLOTS, 3 * rows - SLOTS * g)):
                f, r = divmod(SLOTS * g + slot, rows)
                ext[f, first + r, :, COLS:] = unpack(high, low, slot)

    def beyond_plane(tiles, a, b, slot):
        high, low = ordered(a[tiles * LEV :, :], b[tiles * LEV :, :], north_odd)
        return unpack(high, low, slot)

    for f in range(3):
        flat[f, :, :COLS] = plane[f]
        flat[f, :, COLS:] = beyond_plane(EDGE_TILES, edge_a, edge_b, f)
    remote[0, :, COLS:] = beyond_plane(EDGE_TILES, edgep_a, edgep_b, 1)
    remote[1, :, COLS:] = beyond_plane(CORNER_TILES, corner_a, corner_b, 1)
    for h in range(2):
        at = 6 * ROWS * LEV + 8 * h
        remote[0, :, h * 128 : (h + 1) * 128] = stp[at : at + 8, :]
        at = 6 * HALO * SIZES[0] + 8 * h
        remote[1, :, h * 128 : (h + 1) * 128] = main0[at : at + 8, :]
    for r in range(ROWS):
        counts[ROWS + r] = jnp.broadcast_to(flat[1, r : r + 1, :], (8, WIDE))
        counts[beside + r] = jnp.broadcast_to(remote[0, r : r + 1, :], (8, WIDE))
    for j in range(HALO):
        counts[beyond + j] = jnp.broadcast_to(remote[1, pl.ds(2 * (1 - core) + j, 1), :], (8, WIDE))

    sub = lax.broadcasted_iota(jnp.int32, (8, WIDE), 0)

    def stage(source, lead, rows, inset, write, slot):
        def row(o, _):
            count = counts[o + inset]
            if chunk:
                sum_x = jnp.broadcast_to(carry_in[pl.ds(slot + 2 * o, 1), :], (8, WIDE))
                sum_y = jnp.broadcast_to(carry_in[pl.ds(slot + 2 * o + 1, 1), :], (8, WIDE))
            else:
                sum_x = jnp.zeros((8, WIDE), F32)
                sum_y = jnp.zeros((8, WIDE), F32)
            for t in range(levels // 8):
                here = slice(8 * t, 8 * t + 8)
                mid = []
                dxs = []
                dys = []
                laps = []
                for f in range(3):
                    q = source[f, o + lead + 2, here, :]
                    back2, back = source[f, o + lead, here, :], source[f, o + lead + 1, here, :]
                    fore, fore2 = source[f, o + lead + 3, here, :], source[f, o + lead + 4, here, :]
                    right, left, right2, left2 = shifts(q)
                    mid.append(q)
                    dxs.append(slope(fore, back, fore2, back2))
                    dys.append(slope(right, left, right2, left2))
                    laps.append((fore + back) + (right + left) - 4.0 * q)
                press_x = running(dxs[2], sub) + sum_x
                press_y = running(dys[2], sub) + sum_y
                sum_x = jnp.broadcast_to(press_x[7:8, :], (8, WIDE))
                sum_y = jnp.broadcast_to(press_y[7:8, :], (8, WIDE))
                u, v, _s = mid
                rates = [VISCOSITY * laps[f] - (u * dxs[f] + v * dys[f]) for f in range(3)]
                rates[0] = rates[0] + (CORIOLIS * v - PRESS_COEF * press_x)
                rates[1] = rates[1] - (CORIOLIS * u + PRESS_COEF * press_y)
                keep = count > (sub + (lev0 + 8 * t)).astype(F32)
                write(o, here, t, mid, [jnp.where(keep, r, 0.0) for r in rates])
            carry[pl.ds(slot + 2 * o, 1), :] = sum_x[:1, :]
            carry[pl.ds(slot + 2 * o + 1, 1), :] = sum_y[:1, :]
            return 0

        lax.fori_loop(0, rows, row, 0, unroll=4)

    def write1(o, here, t, mid, rates):
        for f in range(3):
            one[f, o, here, :] = mid[f] + TIME_STEP * rates[f]

    def write2(o, here, t, mid, rates):
        for f in range(3):
            first = ext[f, o + 6, here, :]
            two[f, o, here, :] = 0.75 * first + (0.25 * mid[f] + (0.25 * TIME_STEP) * rates[f])

    def write3(o, here, t, mid, rates):
        for f in range(3):
            first = ext[f, o + 8, here, :]
            value = (1.0 / 3.0) * first + ((2.0 / 3.0) * mid[f] + (2.0 / 3.0 * TIME_STEP) * rates[f])
            at = pl.multiple_of(o * levels + 8 * t, 8)
            for h in range(2):
                out[f, h, pl.ds(at, 8), :] = value[:, h * 128 : (h + 1) * 128]
            if f < 2:
                if t == 0:
                    sums[f, o] = value + sums_in[f, o] if chunk else value
                else:
                    sums[f, o] = sums[f, o] + value

    stage(ext, 2, 16, 4, write1, 0)
    stage(one, 0, 12, 6, write2, 32)
    stage(two, 0, 8, 8, write3, 56)
    if chunk == CHUNKS - 1:
        for f in range(2):
            for o in range(ROWS):
                flows[f, o : o + 1, :] = jnp.sum(sums[f, o], axis=0, keepdims=True)
            flows[f] = flat[2] * (flows[f] * (1.0 / LEV))
            flows[2 + f] = flat[f]


def solve_kernel(sc, mine, pair, remote, remote_pair, far, *rest):
    states = rest[:CHUNKS]
    east, north, salt, level = rest[CHUNKS : CHUNKS + 4]
    wide = rest[CHUNKS + 4]
    core = sc[1]
    wide[:, 24:32, :] = mine[...]
    for slot, block in (
        (4 - 2 * core, pair[...]),
        (2 + 2 * core, remote[0]),
        (1 + 4 * core, remote[1]),
        (5 - 4 * core, remote_pair[0]),
        (6 - 6 * core, remote_pair[1]),
        (6 * core, far[...]),
    ):
        wide[:, pl.ds(pl.multiple_of(8 * slot, 8), 8), :] = block
    high = 56

    def up(x):
        return pltpu.roll(x, high - 1, 0)

    def down(x):
        return pltpu.roll(x, 1, 0)

    def right(x):
        return pltpu.roll(x, WIDE - 1, 1)

    def left(x):
        return pltpu.roll(x, 1, 1)

    wet = jnp.where(wide[3] > 0.0, 1.0, 0.0)
    dry = 1.0 - wet

    def apply(e):
        w = wet * e
        rows = up(w) + down(w)
        mix = 4.0 * w + rows
        sides = right(mix) + left(mix)
        stencil = (20.0 / 6.0) * w - (4.0 / 6.0) * rows - (1.0 / 6.0) * sides
        return wet * (SIGMA_SHIFT * e + stencil) + dry * e

    flow_east = wide[0]
    flow_north = wide[1]
    x = wide[2]
    div = 0.5 * (up(flow_east) - down(flow_east)) + 0.5 * (right(flow_north) - left(flow_north))
    res = wet * (SIGMA_SHIFT * x - DIVERGENCE_COEF * div) - apply(x)
    step = res * (1.0 / CHEB_CENTER)
    keeps, gains = cheb_table(ITERS)
    for index in range(ITERS):
        x = x + step
        if index < ITERS - 1:
            res = res - apply(step)
            step = keeps[index] * step + gains[index] * res
    slope_east = (0.5 * (up(x) - down(x)))[24:32, :COLS]
    slope_north = (0.5 * (right(x) - left(x)))[24:32, :COLS]
    level[...] = x[24:32, :COLS]
    count = mine[3][:, :COLS]
    for lev in range(LEV):
        c = max(i for i in range(CHUNKS) if STARTS[i] <= lev)
        levels = SIZES[c]
        at = lev - STARTS[c]
        keep = count > lev
        for h in range(2):
            cols = slice(h * 128, (h + 1) * 128)
            parts = [states[c][f, h, pl.ds(at, ROWS, stride=levels), :] for f in range(3)]
            east[lev, :, cols] = jnp.where(keep[:, cols], parts[0] - slope_east[:, cols], 0.0)
            north[lev, :, cols] = jnp.where(keep[:, cols], parts[1] - slope_north[:, cols], 0.0)
            salt[lev, :, cols] = parts[2]


def swap(pairs):
    return [p for a, b in pairs for p in ((a, b), (b, a))]


def call(body, outs, scratch=(), ins=0, space=pltpu.VMEM, cost=None):
    vmem = pl.BlockSpec(memory_space=pltpu.VMEM)
    smem = pl.BlockSpec(memory_space=pltpu.SMEM)
    return pl.pallas_call(
        body,
        out_shape=[jax.ShapeDtypeStruct(s, F32) for s in outs],
        in_specs=[smem] + [pl.BlockSpec(memory_space=space)] * ins,
        out_specs=[vmem] * len(outs),
        scratch_shapes=[pltpu.VMEM(s, F32) if isinstance(s, tuple) else s for s in scratch],
        cost_estimate=cost and pl.CostEstimate(flops=cost, transcendentals=0, bytes_accessed=0),
        compiler_params=pltpu.CompilerParams(vmem_limit_bytes=16 * 1024 * 1024),
    )


def local(u, v, s, surface, depth, wet, active):
    gx = lax.axis_size("gx")
    gy = lax.axis_size("gy")
    me = lax.axis_index("gx")
    scalars = jnp.stack([me, me % 2, lax.axis_index("gy") % 2]).astype(jnp.int32)
    on_chip = swap([(i, i + 1) for i in range(0, gx, 2)])
    next_chip = swap([(i, i + 1) for i in range(1, gx - 1, 2)])
    far_chip = swap([(i, i + 3) for i in range(1, gx - 3, 2)])
    even = swap([(i, i + 1) for i in range(0, gy, 2)])
    odd = swap([(i, i + 1) for i in range(1, gy - 1, 2)])

    def both(first, second):
        return [(i * gy + j, k * gy + l) for i, k in first for j, l in second]

    edge_a, edge_b, corner_a, corner_b, *packed = call(
        pack_kernel,
        [(EDGE_TILES * LEV + 8, 128)] * 2
        + [(CORNER_TILES * LEV + 8, 128)] * 2
        + [(6 * HALO * levels + (0 if c else 16), 128) for c, levels in enumerate(SIZES)]
        + [(6 * ROWS * LEV + 16, 128), (3, ROWS, COLS)],
        [pltpu.VMEM((ROWS, COLS), jnp.int32)] * 2
        + [(ROWS, COLS)] * 2
        + [(LEV, ROWS, COLS)] * 3
        + [pltpu.SemaphoreType.DMA((7,))],
        ins=7,
        space=pltpu.HBM,
    )(scalars, *(pltpu.with_memory_space_constraint(x, pltpu.HBM) for x in (u, v, s, wet, active, surface, depth)))
    mains = packed[:CHUNKS]
    st, plane = packed[CHUNKS:]
    stp = lax.ppermute(st, "gx", on_chip)
    main = [lax.ppermute(mains[0], "gx", next_chip)]
    stp, corner_a, corner_b = lax.optimization_barrier((stp, corner_a, corner_b))
    edge_a = lax.ppermute(edge_a, "gy", even)
    edge_b = lax.ppermute(edge_b, "gy", odd)
    corner_a = lax.ppermute(corner_a, ("gx", "gy"), both(next_chip, even))
    corner_b = lax.ppermute(corner_b, ("gx", "gy"), both(next_chip, odd))
    corner_a, corner_b, edge_a, edge_b, *later = lax.optimization_barrier((corner_a, corner_b, edge_a, edge_b, *mains[1:]))
    main += [lax.ppermute(m, "gx", next_chip) for m in later]
    edgep_a = lax.ppermute(edge_a, "gx", on_chip)
    edgep_b = lax.ppermute(edge_b, "gx", on_chip)

    states = []
    tail = []
    for c, levels in enumerate(SIZES):
        *flows, out, carry, sums = call(
            functools.partial(rk_kernel, c),
            [(4, ROWS, WIDE)] * (c == CHUNKS - 1)
            + [(3, 2, ROWS * levels, 128), (72, WIDE), (2, ROWS, 8, WIDE)],
            [(3, 24, levels, WIDE), (3, 16, levels, WIDE), (3, 12, levels, WIDE)]
            + [(24, 8, WIDE), (3, ROWS, WIDE), (2, ROWS, WIDE)],
            ins=11 + len(tail),
        )(scalars, st, stp, edge_a, edge_b, edgep_a, edgep_b, main[c], main[0], corner_a, corner_b, plane, *tail)
        tail = [carry, sums]
        states.append(out)
    flows = flows[0]
    far = lax.ppermute(flows, "gx", far_chip)
    pair = lax.ppermute(flows, "gx", on_chip)
    remote = lax.ppermute(jnp.stack([flows, pair]), "gx", next_chip)
    remote, far = lax.optimization_barrier((remote, far))
    remote_pair = lax.ppermute(remote, "gx", on_chip)
    east, north, salt, level = call(
        solve_kernel,
        [(LEV, ROWS, COLS)] * 3 + [(ROWS, COLS)],
        [(4, 56, WIDE)],
        ins=5 + CHUNKS,
    )(scalars, flows, pair, remote, remote_pair, far, *states)
    return east, north, salt, level


def solution(mesh):
    cube = P(None, "gx", "gy")
    flat = P("gx", "gy")
    return jax.shard_map(
        local,
        mesh=mesh,
        in_specs=(cube, cube, cube, flat, flat, flat, flat),
        out_specs=(cube, cube, cube, flat),
        check_vma=False,
    )
```
